256 devices in a mesh: ctx: 32 (over z, y_lo, core), head: 8 (over x, y_hi).
Axes of the slice: x: 4, y: 4 (y_hi: 2, y_lo: 2; y = y_hi * 2 + y_lo), z: 8, core: 2. Of those that a mesh axis runs over, the one named last changes fastest.
Arguments:
- patch_hidden: bfloat16 [2048, 4096], P('ctx', 'head'), may hold values from -6 to 6
- queries: bfloat16 [2048, 32, 128], P('ctx', 'head'), may hold values from -6 to 6
- new_keys: bfloat16 [2048, 32, 128], P('ctx', 'head'), may hold values from -6 to 6
- new_values: bfloat16 [2048, 32, 128], P('ctx', 'head'), may hold values from -6 to 6
- cache_keys: bfloat16 [32768, 32, 128], P('ctx', 'head'), may hold values from -6 to 6
- cache_values: bfloat16 [32768, 32, 128], P('ctx', 'head'), may hold values from -6 to 6
- cache_request: int32 [32768], P('ctx'), may hold values from 0 to 7, never falling along the last dimension, each value on 1 to 8192 neighbouring positions
- new_request: int32 [2048], replicated, may hold values from 0 to 7, as said below
- out_weight: bfloat16 [32, 128, 4096], P('head'), may hold values from -0.375 to 0.375
- norm_gain: float32 [4096], replicated, may hold values from 0.1 to 1.9
- dec_kv_weight: bfloat16 [4096, 2, 1024], P(None, None, 'head'), may hold values from -0.09375 to 0.09375
- dec_query_weight: bfloat16 [1024, 1024], P(None, 'head'), may hold values from -0.1875 to 0.1875
- query_gain: float32 [64], replicated, may hold values from 0.1 to 1.9
- key_gain: float32 [64], replicated, may hold values from 0.1 to 1.9
- dec_out_weight: bfloat16 [1024, 1024], P('head'), may hold values from -0.75 to 0.75
- byte_states: bfloat16 [8192, 1024], P('ctx'), may hold values from -6 to 6
- byte_patch: int32 [8192], P('ctx'), may hold values from 0 to 2047, never falling along the last dimension, each value on 1 to 8 neighbouring positions
Outputs:
- patch_out: bfloat16 [2048, 4096], P('ctx', 'head')
- byte_out: bfloat16 [8192, 1024], P('ctx', 'head')
The draws below stay inside these ranges and needn't reach their ends.
Inputs may be any that keep to these rules, and one draw needn't show every extreme that they name: `new_request`: never falls along the patches; every request of 0 to 7 has an even number, two or more, of new patches. `cache_request`: never falls along the cached patches; every request has one or more cached patches. `byte_patch`: never falls along the bytes; every new patch owns one or more bytes.
All inputs are finite; a program needn't handle non-finite values.
Results may differ from the reference program's by a relative error of at most 0.017.
Values may be sent and summed in bfloat16 or wider, within the bound.
A program may use at most 128 MiB of HBM per device.

```python
import math
import jax
import jax.numpy as jnp
import numpy as np
from jax import lax

D = 4096
H = 32
DH = 128
DD = 1024
DEC_H = 16
DEC_DH = 64
NEW_DEV = 64
NREQ = 8
P_SIZE = 2048
CTX = 32768
NBYTES = 8192


def request_cuts(key):
    lowest = max(1, min((P_SIZE // 2 + NEW_DEV) // 2, P_SIZE // 2 - NREQ - 1))
    chosen = jax.random.permutation(key, P_SIZE // 2 - lowest)[:NREQ - 1] + lowest
    return (jnp.sort(chosen) * 2).astype(jnp.int32)


def draw_new_request(key, part):
    cuts = request_cuts(jax.random.fold_in(key, 11))
    places = jnp.arange(P_SIZE, dtype=jnp.int32)
    return jnp.sum((places[:, None] >= cuts[None, :]).astype(jnp.int32), axis=1).astype(jnp.int32)


def draw_queries(key, part):
    base = jnp.clip(1.5 * jax.random.normal(jax.random.fold_in(key, 21), (P_SIZE, H, DH), jnp.float32), -6.0, 6.0)
    return base.astype(jnp.bfloat16)


def draw_new_keys(key, part):
    base = jnp.clip(jax.random.normal(jax.random.fold_in(key, 31), (P_SIZE, H, DH), jnp.float32), -6.0, 6.0)
    return base.astype(jnp.bfloat16)


def shard_levels(own_key, dims, pieces, smallest, top_value):
    def one(dim, parts):
        heights = jax.random.uniform(jax.random.fold_in(jax.random.fold_in(own_key, 6), dim), (parts,), jnp.float32, smallest / len(pieces), top_value / len(pieces))
        return jnp.repeat(jnp.exp(heights), dims[dim] // parts).reshape((-1,) + (1,) * (len(dims) - dim - 1))

    gain = one(*pieces[0])
    for cut in pieces[1:]:
        gain = gain * one(*cut)
    return gain


def split_up(count, total, bound, slope):
    weights = [(1 << 20) // math.isqrt(grade ** slope) + 1 for grade in range(2, count + 1)]
    spare, given = total - bound - (count - 1), [1] * (count - 1)
    while spare > 0:
        free = [i for i in range(count - 1) if given[i] < bound]
        pool, left = sum([weights[i] for i in free]), spare
        for i in free:
            more = min(bound - given[i], max(1, left * weights[i] // pool), spare)
            given[i] = given[i] + more
            spare = spare - more
    return np.array([bound] + given)


def uneven(own_key, count, total, reach, slope):
    if count == 2:
        one = jax.random.randint(own_key, (), max(1, total - reach), min(reach, total - 1) + 1)
        return jnp.stack([one, total - one])
    sizes = jnp.asarray(split_up(count, total, reach, slope), jnp.int32)
    twos = (count - 1) // 2
    donor, receiver = sizes[1:1 + 2 * twos:2], sizes[2:2 + 2 * twos:2]
    margin = jnp.minimum(donor - 1, reach - receiver)
    moved = jax.random.randint(jax.random.fold_in(own_key, 1), (twos,), 0, 1 << 20) % (margin + 1)
    sizes = sizes.at[1:1 + 2 * twos:2].set(donor - moved).at[2:2 + 2 * twos:2].set(receiver + moved)
    return sizes[jax.random.permutation(jax.random.fold_in(own_key, 2), count)]


def scatter_about(rng, shape, deviation, reach, split=(), held_as=jnp.bfloat16):
    gain = shard_levels(rng, shape, split, -0.22, 0.18) if split else 1.0
    entries = jax.random.normal(rng, shape, jnp.float32) * deviation * gain
    return jnp.minimum(jnp.maximum(entries, -reach), reach).astype(held_as)


def setup_inputs(seed: int = 0) -> dict:
    key_of = jax.random.split(jax.random.key(seed), 18)
    return {
        "patch_hidden": scatter_about(key_of[0], (P_SIZE, D), 1.0, 6.0, ((0, 32), (1, 8))),
        "queries": draw_queries(jax.random.fold_in(key_of[17], 71), 0),
        "new_keys": draw_new_keys(jax.random.fold_in(key_of[17], 71), 0),
        "new_values": scatter_about(key_of[3], (P_SIZE, H, DH), 1.0, 6.0, ((0, 32), (1, 8))),
        "cache_keys": scatter_about(key_of[4], (CTX, H, DH), 1.0, 6.0, ((0, 32), (1, 8))),
        "cache_values": scatter_about(key_of[5], (CTX, H, DH), 1.0, 6.0, ((0, 32), (1, 8))),
        "cache_request": jnp.searchsorted(jnp.cumsum(uneven(key_of[6], NREQ, CTX, CTX // 4, 2)), jnp.arange(CTX), side="right").astype(jnp.int32),
        "new_request": draw_new_request(jax.random.fold_in(key_of[17], 71), 0),
        "out_weight": scatter_about(key_of[8], (H, DH, D), (H * DH // 16) ** -0.5, 0.375, ((0, 8),)),
        "norm_gain": jnp.clip(1.0 + 0.18 * jax.random.normal(key_of[9], (D,), jnp.float32), 0.1, 1.9),
        "dec_kv_weight": scatter_about(key_of[10], (D, 2, DD), D ** -0.5, 0.09375, ((2, 8),)),
        "dec_query_weight": scatter_about(key_of[11], (DD, DD), DD ** -0.5, 0.1875, ((1, 8),)),
        "query_gain": jnp.clip(1.0 + 0.18 * jax.random.normal(key_of[12], (DEC_DH,), jnp.float32), 0.1, 1.9),
        "key_gain": jnp.clip(1.0 + 0.18 * jax.random.normal(key_of[13], (DEC_DH,), jnp.float32), 0.1, 1.9),
        "dec_out_weight": scatter_about(key_of[14], (DD, DD), (DD // 16) ** -0.5, 0.75, ((0, 8),)),
        "byte_states": scatter_about(key_of[15], (NBYTES, DD), 1.0, 6.0, ((0, 32),)),
        "byte_patch": jnp.searchsorted(jnp.cumsum(uneven(key_of[16], P_SIZE, NBYTES, 8, 2)), jnp.arange(NBYTES), side="right").astype(jnp.int32),
    }


def row_norm(values, gain_values, epsilon):
    meansq = lax.optimization_barrier(jnp.mean(values * values, axis=-1, keepdims=True))
    return values * lax.rsqrt(meansq + epsilon) * gain_values

def reference(patch_hidden, queries, new_keys, new_values, cache_keys, cache_values, cache_request, new_request, out_weight, norm_gain, dec_kv_weight, dec_query_weight, query_gain, key_gain, dec_out_weight, byte_states, byte_patch):
    query_index = jnp.arange(P_SIZE, dtype=jnp.int32)
    key_request = jnp.concatenate([cache_request.astype(jnp.int32), new_request.astype(jnp.int32)])
    key_position = jnp.concatenate([jnp.full((CTX,), -1, jnp.int32), query_index])
    visible = (key_request[None, :] == new_request[:, None]) & (key_position[None, :] <= query_index[:, None])
    all_keys = jnp.transpose(jnp.concatenate([cache_keys, new_keys], 0), (1, 0, 2))
    all_values = jnp.transpose(jnp.concatenate([cache_values, new_values], 0), (1, 0, 2))
    head_queries = jnp.transpose(queries, (1, 0, 2))

    def global_head(inputs):
        query_head, key_head, value_head = inputs
        scores = jnp.dot(query_head, key_head.T, preferred_element_type=jnp.float32) * DH ** (-0.5)
        highest = lax.optimization_barrier(jnp.max(jnp.where(visible, scores, -1e+30), axis=1, keepdims=True))
        weights = jnp.where(visible, jnp.exp(scores - highest), 0.0)
        totals = lax.optimization_barrier(jnp.sum(weights, axis=1, keepdims=True))
        mixed_rows = jnp.dot(weights.astype(jnp.bfloat16), value_head, preferred_element_type=jnp.float32)
        return (mixed_rows / totals).astype(jnp.bfloat16)
    attended = lax.map(global_head, (head_queries, all_keys, all_values))
    flattened = jnp.transpose(attended, (1, 0, 2)).reshape(P_SIZE, H * DH)
    projected = jnp.dot(flattened, out_weight.reshape(H * DH, D), preferred_element_type=jnp.float32)
    patch_out = (patch_hidden.astype(jnp.float32) + projected).astype(jnp.bfloat16)
    normed = row_norm(patch_out.astype(jnp.float32), norm_gain.astype(jnp.float32), 1e-05).astype(jnp.bfloat16)
    patch_proj = jnp.dot(normed, dec_kv_weight.reshape(D, 2 * DD), preferred_element_type=jnp.float32)
    patch_keys = row_norm(patch_proj[:, :DD].reshape(P_SIZE, DEC_H, DEC_DH), key_gain.astype(jnp.float32), 1e-06).astype(jnp.bfloat16)
    patch_values = patch_proj[:, DD:].astype(jnp.bfloat16).reshape(P_SIZE, DEC_H, DEC_DH)
    query_proj = jnp.dot(byte_states, dec_query_weight, preferred_element_type=jnp.float32).reshape(NBYTES, DEC_H, DEC_DH)
    byte_query = row_norm(query_proj, query_gain.astype(jnp.float32), 1e-06).astype(jnp.bfloat16)
    byte_request = new_request[byte_patch]
    seen = (new_request[None, :] == byte_request[:, None]) & (query_index[None, :] <= byte_patch[:, None])

    def byte_head(inputs):
        query_head, key_head, value_head = inputs
        scores = jnp.dot(query_head, key_head.T, preferred_element_type=jnp.float32) * DEC_DH ** (-0.5)
        weights = jnp.where(seen, jnp.exp(scores), 0.0)
        totals = lax.optimization_barrier(jnp.sum(weights, axis=1, keepdims=True))
        mixed_rows = jnp.dot(weights.astype(jnp.bfloat16), value_head, preferred_element_type=jnp.float32)
        return (mixed_rows / totals).astype(jnp.bfloat16)
    byte_mixed = lax.map(byte_head, (jnp.transpose(byte_query, (1, 0, 2)), jnp.transpose(patch_keys, (1, 0, 2)), jnp.transpose(patch_values, (1, 0, 2))))
    byte_flat = jnp.transpose(byte_mixed, (1, 0, 2)).reshape(NBYTES, DD)
    byte_terms = jnp.dot(byte_flat, dec_out_weight, preferred_element_type=jnp.float32)
    byte_out = (byte_states.astype(jnp.float32) + byte_terms).astype(jnp.bfloat16)
    return (patch_out, byte_out)
```

```python
import functools

import jax
import jax.numpy as jnp
from jax import lax
from jax.experimental import pallas as pl
from jax.experimental.pallas import tpu as pltpu
from jax.sharding import PartitionSpec as P

MESH = pl.DeviceIdType.MESH
VMEM = pltpu.VMEM
F32 = jnp.float32
BF16 = jnp.bfloat16
LOW = -1e20
HIDE = -1e30
LOG2E = 1.4426950408889634


def in_vmem():
    return pl.BlockSpec(memory_space=pltpu.VMEM)


def in_place():
    return pl.BlockSpec(memory_space=pl.ANY)


class Place:
    def __init__(self, zn):
        c = lax.axis_index("ctx")
        self.c = c
        self.zn = zn
        self.z = lax.div(c, 4)
        self.yl = lax.rem(lax.div(c, 2), 2)
        self.k = lax.rem(c, 2)
        low = lax.rem(c, 4)
        self.core_peer = c + 1 - 2 * self.k
        self.y_peer = c + 2 - 4 * self.yl
        self.right = self.around(1) * 4 + low
        self.left = self.around(-1) * 4 + low

    def around(self, step):
        return lax.rem(self.z + (step + 2 * self.zn), self.zn)


class Sends:
    def __init__(self, send_sem, recv_sem):
        self.send_sem, self.recv_sem, self.used = send_sem, recv_sem, 0

    def make(self, src, dst, device):
        at = self.used
        self.used += 1
        return pltpu.make_async_remote_copy(
            src_ref=src,
            dst_ref=dst,
            send_sem=self.send_sem.at[at],
            recv_sem=self.recv_sem.at[at],
            device_id=device,
            device_id_type=MESH,
        )


def greet(devices):
    barrier = pltpu.get_barrier_semaphore()
    for device in devices:
        pl.semaphore_signal(barrier, inc=1, device_id=device, device_id_type=MESH)
    pl.semaphore_wait(barrier, len(devices))


def ring_gather(sends, place, buffer, rows, from_y):
    zn = place.zn
    far, near = zn // 2, zn - 1 - zn // 2

    def slot(z, y):
        start = pl.multiple_of((z * 2 + y) * rows, rows)
        return buffer.at[pl.ds(start, rows), :]

    streams = ((place.yl, far, near), (1 - place.yl, near, far))
    made = {}
    for step in range(max(far, near)):
        for which, (y, to_right, to_left) in enumerate(streams):
            if step == 0 and which == 1:
                from_y.wait_recv()
            for way, count, device in ((1, to_right, place.right), (-1, to_left, place.left)):
                if step >= count:
                    continue
                if step > 0:
                    made[which, way, step - 1].wait_recv()
                piece = slot(place.around(-way * step), y)
                copy = sends.make(piece, piece, {"ctx": device})
                copy.start()
                made[which, way, step] = copy
    if not made:
        from_y.wait_recv()
    for (which, way, step), copy in made.items():
        if (which, way, step + 1) not in made:
            copy.wait_recv()
    for copy in made.values():
        copy.wait_send()


def spread(zn, q_ref, k_ref, v_ref, cr_ref, nr_ref, qg, kc, vc, bounds, cr_both, send_sem, recv_sem, local_sem):
    place = Place(zn)
    sends = Sends(send_sem, recv_sem)
    k, z, yl = place.k, place.z, place.yl
    new = q_ref.shape[0]
    width = qg.shape[1]
    cached = k_ref.shape[0] - new
    greet([{"ctx": d} for d in (place.core_peer, place.y_peer, place.right, place.left)])
    peer = {"ctx": place.core_peer}
    own_cols = pl.ds(pl.multiple_of(k * width, width), width)
    peer_cols = pl.ds(pl.multiple_of((1 - k) * width, width), width)
    chip = z * 2 + yl
    chip_rows = pl.ds(pl.multiple_of(chip * 2 * new, 2 * new), 2 * new)
    q_rows = pl.ds(pl.multiple_of(place.c * new, new), new)
    q_send = sends.make(q_ref.at[:, peer_cols], qg.at[q_rows, :], peer)
    q_send.start()
    q_local = pltpu.make_async_copy(q_ref.at[:, own_cols], qg.at[q_rows, :], local_sem.at[0])
    q_local.start()
    cr_send = sends.make(cr_ref, cr_both.at[k], peer)
    cr_send.start()
    swaps, locals_ = [], []
    old_from, new_from = pl.ds(0, cached), pl.ds(cached, new)
    old_to = pl.ds(pl.multiple_of(k * cached, cached), cached)
    new_to = pl.ds(pl.multiple_of(2 * cached + k * new, new), new)
    for src, dst in ((k_ref, kc), (v_ref, vc)):
        for rows_from, rows_to in ((old_from, old_to), (new_from, new_to)):
            swaps.append(sends.make(src.at[rows_from, peer_cols], dst.at[rows_to, :], peer))
            locals_.append(
                pltpu.make_async_copy(
                    src.at[rows_from, own_cols], dst.at[rows_to, :], local_sem.at[1 + len(locals_)]
                )
            )
    q_local.wait()
    q_send.wait_recv()
    mine = qg.at[chip_rows, :]
    to_y = sends.make(mine, mine, {"ctx": place.y_peer})
    to_y.start()
    for copy in swaps:
        copy.start()
    for copy in locals_:
        copy.start()
    cr_send.wait_recv()
    cr_both[pl.ds(k, 1)] = cr_ref[...][None]
    ring_gather(sends, place, qg, 2 * new, to_y)
    held = cr_both[...]
    mates = nr_ref[...]
    total = mates.shape[1]
    zero = jnp.zeros((1, total), F32)
    low, high, start = zero, zero, zero
    below = jnp.zeros((1, 1), F32)
    for r in range(8):
        ones = jnp.where(held <= r, 1.0, 0.0)
        upto = jnp.sum(jnp.sum(ones, axis=0), axis=(0, 1), keepdims=True)
        first = jnp.sum(jnp.where(mates < r, 1.0, 0.0), axis=1, keepdims=True)
        here = mates == r
        low = jnp.where(here, below, low)
        high = jnp.where(here, upto, high)
        start = jnp.where(here, first, start)
        below = upto
    shift = chip * 2 * new
    index = lax.broadcasted_iota(jnp.int32, (1, total), 1)
    bounds[0:1, :] = low.astype(jnp.int32)
    bounds[1:2, :] = high.astype(jnp.int32)
    bounds[2:3, :] = start.astype(jnp.int32) - shift
    bounds[3:4, :] = index - (shift - 1)
    bounds[4:8, :] = jnp.zeros((4, total), jnp.int32)
    for copy in locals_:
        copy.wait()
    for copy in swaps:
        copy.wait()
    q_send.wait_send()
    cr_send.wait_send()
    to_y.wait_send()


def attend(cached, block, scale, q_ref, k_ref, v_ref, bv_ref, bs_ref, o_ref, m_s, l_s, acc_s):
    rows = q_ref.shape[0]
    new = k_ref.shape[0] - cached
    q0 = pl.program_id(0) * rows
    last = q0 + rows - 1
    heads, dim = acc_s.shape[0], acc_s.shape[1]
    m_s[...] = jnp.full_like(m_s, LOW).astype(BF16).astype(F32)
    l_s[...] = jnp.zeros_like(l_s)
    acc_s[...] = jnp.zeros_like(acc_s)

    def add(first, count, base, low, high):
        for h in range(heads):
            cols = slice(h * dim, (h + 1) * dim)
            scores = lax.dot_general(
                k_ref[pl.ds(first, count), cols],
                q_ref[:, cols],
                (((1,), (1,)), ((), ())),
                preferred_element_type=F32,
            )
            if low is not None:
                at = lax.broadcasted_iota(jnp.int32, scores.shape, 0) + base
                scores = jnp.where((at >= low) & (at < high), scores, HIDE)
            top = jnp.max(scores, axis=0, keepdims=True) * scale
            m_old = m_s[h]
            m_new = jnp.maximum(m_old, top.astype(BF16).astype(F32))
            weights = jnp.exp2(scores * scale - m_new)
            fade = jnp.exp2(m_old - m_new)
            m_s[h] = m_new
            l_s[h] = l_s[h] * fade + jnp.sum(weights, axis=0, keepdims=True)
            acc_s[h] = acc_s[h] * fade + lax.dot_general(
                v_ref[pl.ds(first, count), cols],
                weights.astype(BF16),
                (((0,), (0,)), ((), ())),
                preferred_element_type=F32,
            )

    low_first, low_last = bs_ref[0, q0], bs_ref[0, last]
    high_first, high_last = bs_ref[1, q0], bs_ref[1, last]
    begin = lax.div(low_first, block)
    end = jnp.where(high_last > low_first, lax.div(high_last + block - 1, block), begin)

    def one_block(b, carry):
        first = pl.multiple_of(b * block, block)
        whole = (low_last <= first) & (high_first >= first + block)

        @pl.when(whole)
        def _():
            add(first, block, first, None, None)

        @pl.when(jnp.logical_not(whole))
        def _():
            add(first, block, first, bv_ref[0:1, :], bv_ref[1:2, :])

        return carry

    lax.fori_loop(begin, end, one_block, 0)

    @pl.when((bs_ref[3, last] > 0) & (bs_ref[2, q0] < new))
    def _():
        add(cached, new, 0, bv_ref[2:3, :], bv_ref[3:4, :])

    for h in range(heads):
        pack(o_ref.at[0, h], acc_s[h], m_s[h], l_s[h])


def pack(ref, out, top, total):
    dim = out.shape[0]
    ref[0:dim, :] = out.astype(BF16)
    coarse = total.astype(BF16).astype(F32)
    row = lax.broadcasted_iota(jnp.int32, (16, out.shape[1]), 0)
    tail = jnp.where(row == 0, top, jnp.where(row == 1, coarse, jnp.where(row == 2, total - coarse, 0.0)))
    ref[dim : dim + 16, :] = tail.astype(BF16)


def unpack(ref):
    value = ref[...]
    dim = value.shape[0] - 16
    tail = value[dim:, :].astype(F32)
    return value[:dim, :].astype(F32), tail[0:1, :], tail[1:2, :] + tail[2:3, :]


def merged(parts):
    top = parts[0][1]
    for part in parts[1:]:
        top = jnp.maximum(top, part[1])
    out, total = 0.0, 0.0
    for o, m, l in parts:
        factor = jnp.exp2(m - top)
        out = out + o * factor
        total = total + l * factor
    return out, top, total


def head_norm(values, gain, half):
    lane = lax.broadcasted_iota(jnp.int32, values.shape, 1)
    first = lane < half
    squares = values * values
    s0 = jnp.sum(jnp.where(first, squares, 0.0), axis=1, keepdims=True)
    s1 = jnp.sum(jnp.where(first, 0.0, squares), axis=1, keepdims=True)
    return values * lax.rsqrt(jnp.where(first, s0, s1) / half + 1e-6) * gain


def finish(
    zn, hn, part, hidden, w_hbm, dkv_hbm, gain_ref, kgain_ref, qgain_ref, dqw_ref, dow_ref, states_ref, bp_ref, nr_ref,
    patch_out, byte_out,
    w_ref, dkv_ref, ring_in, ring_out, y_in, y_out, att_t, att, rs_out, rs_in, ag_in, kv_tile, kvg, bq_tile, bq,
    bp_both, mix_tile, mix, bs_out, bs_in, send_sem, recv_sem, local_sem,
):
    place = Place(zn)
    sends = Sends(send_sem, recv_sem)
    k, z, yl = place.k, place.z, place.yl
    me = lax.axis_index("head")
    peer, beside = {"ctx": place.core_peer}, {"ctx": place.y_peer}
    others = [lax.rem(me + i, hn) for i in range(1, hn)]
    sources = [lax.rem(me + hn - i, hn) for i in range(1, hn)]
    greet(
        [{"ctx": d} for d in (place.core_peer, place.y_peer, place.right, place.left)]
        + [{"head": d} for d in others]
    )
    w_load = pltpu.make_async_copy(w_hbm, w_ref, local_sem.at[0])
    w_load.start()
    dkv_load = pltpu.make_async_copy(dkv_hbm, dkv_ref, local_sem.at[1])
    dkv_load.start()
    pending = []
    new, slice_width = hidden.shape
    heads = part.shape[1]
    dim = part.shape[2] - 16

    bp_send = sends.make(bp_ref, bp_both.at[k], peer)
    bp_send.start()

    far, near = zn // 2, zn - 1 - zn // 2
    counts = [(far, near) if h % 2 == 0 else (near, far) for h in range(heads)]
    made = {}
    for step in range(max(far, near)):
        for h in range(heads):
            for way, device in ((0, place.right), (1, place.left)):
                count = counts[h][way]
                if step >= count:
                    continue
                ahead = count - step
                target = place.around(ahead if way == 0 else -ahead)
                if step == 0:
                    src = part.at[target, h]
                else:
                    made[h, way, step - 1].wait_recv()
                    src = ring_out.at[h, way, step]
                    pack(src, *merged([unpack(part.at[target, h]), unpack(ring_in.at[h, way, step - 1])]))
                copy = sends.make(src, ring_in.at[h, way, step], {"ctx": device})
                copy.start()
                made[h, way, step] = copy
        if step == 0:
            proj = jnp.dot(states_ref[...], dqw_ref[...], preferred_element_type=F32)
            half = proj.shape[1] // 2
            normed = head_norm(proj, qgain_ref[...], half)
            lane = lax.broadcasted_iota(jnp.int32, normed.shape, 1)
            bq_tile[0] = jnp.where(lane < half, normed, 0.0).astype(BF16)
            bq_tile[1] = jnp.where(lane < half, pltpu.roll(normed, half, 1), 0.0).astype(BF16)
            bytes_ = bq_tile.shape[1]
            byte_rows = pl.ds(pl.multiple_of(k * bytes_, bytes_), bytes_)
            bq_send = sends.make(bq_tile.at[1 - k], bq.at[byte_rows, :], peer)
            bq_send.start()
            bq[byte_rows, :] = bq_tile[k]
            pending += [bp_send, bq_send]
    y_cols = pl.ds(pl.multiple_of((1 - yl) * 2 * new, 2 * new), 2 * new)
    own_cols = pl.ds(pl.multiple_of(yl * 2 * new, 2 * new), 2 * new)
    for h in range(heads):
        got = [unpack(part.at[z, h])]
        for way in (0, 1):
            count = counts[h][way]
            if count:
                made[h, way, count - 1].wait_recv()
                got.append(unpack(ring_in.at[h, way, count - 1]))
        pack(y_out.at[h], *merged(got))
    y_send = sends.make(y_out.at[:, :, y_cols], y_in, beside)
    y_send.start()
    pending += list(made.values()) + [y_send]
    y_send.wait_recv()
    core_rows = heads * dim
    for h in range(heads):
        out, _, total = merged([unpack(y_out.at[h, :, own_cols]), unpack(y_in.at[h])])
        rows = pl.ds(pl.multiple_of(k * core_rows + h * dim, dim), dim)
        att_t[rows, :] = (out / total).astype(BF16)
    held = att_t.at[pl.ds(pl.multiple_of(k * core_rows, core_rows), core_rows), :]
    att_send = sends.make(held, held, peer)
    att_send.start()
    w_load.wait()
    att_send.wait_recv()
    pending.append(att_send)
    att[...] = att_t[...].T

    mine = att[pl.ds(pl.multiple_of(k * new, new), new), :]

    def columns_for(d):
        cols = pl.ds(pl.multiple_of(d * slice_width, slice_width), slice_width)
        return jnp.dot(mine, w_ref[:, cols], preferred_element_type=F32)

    rs_sends = []
    for i, d in enumerate(others):
        rs_out[i] = columns_for(d).astype(BF16)
        copy = sends.make(rs_out.at[i], rs_in.at[i], {"head": d})
        copy.start()
        rs_sends.append(copy)
    own = columns_for(me) + hidden[...].astype(F32)
    for i, copy in enumerate(rs_sends):
        copy.wait_recv()
        own = own + rs_in[i].astype(F32)
    rounded = own.astype(BF16)
    patch_out[...] = rounded
    ag_in[0] = rounded
    ag_sends = []
    for i, d in enumerate(others):
        copy = sends.make(ag_in.at[0], ag_in.at[1 + i], {"head": d})
        copy.start()
        ag_sends.append(copy)
    pending += rs_sends + ag_sends
    squares = 0.0
    for i in range(hn):
        if i:
            ag_sends[i - 1].wait_recv()
        wide = ag_in[i].astype(F32)
        squares = squares + jnp.sum(wide * wide, axis=1, keepdims=True)
    inverse = lax.rsqrt(squares / (hn * slice_width) + 1e-5)
    dkv_load.wait()
    proj = 0.0
    for i in range(hn):
        source = me if i == 0 else sources[i - 1]
        normed = (ag_in[i].astype(F32) * inverse * gain_ref[pl.ds(source, 1), :]).astype(BF16)
        rows = pl.ds(pl.multiple_of(source * slice_width, slice_width), slice_width)
        proj = proj + jnp.dot(normed, dkv_ref[rows, :], preferred_element_type=F32)
    width = proj.shape[1] // 2
    half = width // 2
    keys = head_norm(proj[:, :width], kgain_ref[...], half)
    values = proj[:, width:]
    lane = lax.broadcasted_iota(jnp.int32, keys.shape, 1)
    kv_tile[0] = jnp.where(lane < half, keys, pltpu.roll(values, half, 1)).astype(BF16)
    kv_tile[1] = jnp.where(lane < half, pltpu.roll(keys, half, 1), values).astype(BF16)
    kv_rows = pl.ds(pl.multiple_of(place.c * new, new), new)
    kv_send = sends.make(kv_tile.at[1 - k], kvg.at[kv_rows, :], peer)
    kv_send.start()
    kvg[kv_rows, :] = kv_tile[k]
    kv_send.wait_recv()
    chip = z * 2 + yl
    slot = kvg.at[pl.ds(pl.multiple_of(chip * 2 * new, 2 * new), 2 * new), :]
    kv_y = sends.make(slot, slot, beside)
    kv_y.start()
    pending += [kv_send, kv_y]

    bp_send.wait_recv()
    bp_both[pl.ds(k, 1)] = bp_ref[...][None]
    owner = jnp.concatenate([bp_both[0], bp_both[1]], axis=1)
    first = jnp.zeros(owner.shape, F32)
    mates = nr_ref[...]
    for r in range(1, 8):
        begins = jnp.sum(jnp.where(mates < r, 1.0, 0.0), axis=1, keepdims=True)
        first = jnp.where(owner.astype(F32) >= begins, begins, first)
    first = first.astype(jnp.int32)
    bq_send.wait_recv()
    ring_gather(sends, place, kvg, 2 * new, kv_y)

    queries = bq[...]
    block = min(512, kvg.shape[0])
    scale = half ** (-0.5) * LOG2E
    out, total = 0.0, 0.0
    for b in range(kvg.shape[0] // block):
        kv = kvg[b * block : (b + 1) * block, :]
        scores = lax.dot_general(kv, queries, (((1,), (1,)), ((), ())), preferred_element_type=F32)
        at = lax.broadcasted_iota(jnp.int32, scores.shape, 0) + b * block
        weights = jnp.where((at >= first) & (at <= owner), jnp.exp2(scores * scale), 0.0)
        total = total + jnp.sum(weights, axis=0, keepdims=True)
        out = out + lax.dot_general(
            kv, weights.astype(BF16), (((0,), (0,)), ((), ())), preferred_element_type=F32
        )
    mix_tile[...] = (out[half:, :] / total).astype(BF16)
    mix_rows = pl.ds(pl.multiple_of(k * half, half), half)
    bytes_ = states_ref.shape[0]
    theirs = pl.ds(pl.multiple_of((1 - k) * bytes_, bytes_), bytes_)
    ours = pl.ds(pl.multiple_of(k * bytes_, bytes_), bytes_)
    mix_send = sends.make(mix_tile.at[:, theirs], mix.at[mix_rows, :], peer)
    mix_send.start()
    mix[mix_rows, :] = mix_tile[:, ours]
    mix_send.wait_recv()
    pending.append(mix_send)
    mixed = mix[...]
    out_width = byte_out.shape[1]

    def byte_columns_for(d):
        cols = pl.ds(pl.multiple_of(d * out_width, out_width), out_width)
        return lax.dot_general(mixed, dow_ref[:, cols], (((0,), (0,)), ((), ())), preferred_element_type=F32)

    bs_sends = []
    for i, d in enumerate(others):
        bs_out[i] = byte_columns_for(d).astype(BF16)
        copy = sends.make(bs_out.at[i], bs_in.at[i], {"head": d})
        copy.start()
        bs_sends.append(copy)
    own_states = states_ref[:, pl.ds(pl.multiple_of(me * out_width, out_width), out_width)]
    own = byte_columns_for(me) + own_states.astype(F32)
    for i, copy in enumerate(bs_sends):
        copy.wait_recv()
        own = own + bs_in[i].astype(F32)
    byte_out[...] = own.astype(BF16)
    for copy in pending + bs_sends:
        copy.wait_send()


def per_device(
    zn,
    hn,
    patch_hidden,
    queries,
    new_keys,
    new_values,
    cache_keys,
    cache_values,
    cache_request,
    new_request,
    out_weight,
    norm_gain,
    dec_kv_weight,
    dec_query_weight,
    query_gain,
    key_gain,
    dec_out_weight,
    byte_states,
    byte_patch,
):
    new, heads, dim = queries.shape
    cached = cache_keys.shape[0]
    total = new_request.shape[0]
    pair = heads // 2 * dim
    all_keys = 2 * (cached + new)
    slice_width = patch_hidden.shape[1]
    flat_keys = jnp.concatenate([cache_keys, new_keys], 0).reshape(cached + new, heads * dim)
    flat_values = jnp.concatenate([cache_values, new_values], 0).reshape(cached + new, heads * dim)
    held = cache_request.reshape(8, cached // 8)
    mates = new_request.reshape(1, total)
    gather_copies = 8 + 2 * (zn - 1)
    gathered, keys, values, bounds = pl.pallas_call(
        functools.partial(spread, zn),
        out_shape=(
            jax.ShapeDtypeStruct((total, pair), BF16),
            jax.ShapeDtypeStruct((all_keys, pair), BF16),
            jax.ShapeDtypeStruct((all_keys, pair), BF16),
            jax.ShapeDtypeStruct((8, total), jnp.int32),
        ),
        in_specs=[in_vmem(), in_place(), in_place(), in_vmem(), in_vmem()],
        out_specs=(in_vmem(), in_place(), in_place(), in_vmem()),
        scratch_shapes=[
            VMEM((2, *held.shape), jnp.int32),
            pltpu.SemaphoreType.DMA((gather_copies,)),
            pltpu.SemaphoreType.DMA((gather_copies,)),
            pltpu.SemaphoreType.DMA((5,)),
        ],
        compiler_params=pltpu.CompilerParams(
            collective_id=0, has_side_effects=True, vmem_limit_bytes=24 * 2**20
        ),
        name="spread",
    )(queries.reshape(new, heads * dim), flat_keys, flat_values, held, mates)

    tile = 4 * new
    block = min(512, cached)
    partial = pl.pallas_call(
        functools.partial(attend, 2 * cached, block, dim ** (-0.5) * LOG2E),
        out_shape=jax.ShapeDtypeStruct((zn, heads // 2, dim + 16, tile), BF16),
        grid=(zn,),
        in_specs=[
            pl.BlockSpec((tile, pair), lambda t: (t, 0)),
            pl.BlockSpec((all_keys, pair), lambda t: (0, 0)),
            pl.BlockSpec((all_keys, pair), lambda t: (0, 0)),
            pl.BlockSpec((8, tile), lambda t: (0, t)),
            pl.BlockSpec(memory_space=pltpu.SMEM),
        ],
        out_specs=pl.BlockSpec((1, heads // 2, dim + 16, tile), lambda t: (t, 0, 0, 0)),
        scratch_shapes=[
            VMEM((heads // 2, 1, tile), F32),
            VMEM((heads // 2, 1, tile), F32),
            VMEM((heads // 2, dim, tile), F32),
        ],
        compiler_params=pltpu.CompilerParams(vmem_limit_bytes=32 * 2**20),
        name="attend",
    )(gathered, keys, values, bounds, bounds)

    kv_rows = dec_kv_weight.shape[0]
    dec_width = dec_kv_weight.shape[2]
    bytes_ = byte_states.shape[0]
    out_width = dec_out_weight.shape[1] // hn
    half = dec_width // 2
    steps = max(zn // 2, 1)
    finish_copies = 6 + 2 * 2 * (zn - 1) + 3 * (hn - 1) + 2
    return pl.pallas_call(
        functools.partial(finish, zn, hn),
        out_shape=(
            jax.ShapeDtypeStruct(patch_hidden.shape, BF16),
            jax.ShapeDtypeStruct((bytes_, out_width), BF16),
        ),
        in_specs=[in_vmem(), in_vmem(), in_place(), in_place()] + [in_vmem()] * 8,
        out_specs=(in_vmem(), in_vmem()),
        scratch_shapes=[
            VMEM((heads * dim, out_weight.shape[2]), BF16),
            VMEM((kv_rows, 2 * dec_width), BF16),
            VMEM((heads // 2, 2, steps, dim + 16, tile), BF16),
            VMEM((heads // 2, 2, steps, dim + 16, tile), BF16),
            VMEM((heads // 2, dim + 16, 2 * new), BF16),
            VMEM((heads // 2, dim + 16, tile), BF16),
            VMEM((heads * dim, 2 * new), BF16),
            VMEM((2 * new, heads * dim), BF16),
            VMEM((max(hn - 1, 1), new, slice_width), BF16),
            VMEM((max(hn - 1, 1), new, slice_width), BF16),
            VMEM((hn, new, slice_width), BF16),
            VMEM((2, new, dec_width), BF16),
            VMEM((total, dec_width), BF16),
            VMEM((2, bytes_, dec_width), BF16),
            VMEM((2 * bytes_, dec_width), BF16),
            VMEM((2, 1, bytes_), jnp.int32),
            VMEM((half, 2 * bytes_), BF16),
            VMEM((dec_width, bytes_), BF16),
            VMEM((max(hn - 1, 1), bytes_, out_width), BF16),
            VMEM((max(hn - 1, 1), bytes_, out_width), BF16),
            pltpu.SemaphoreType.DMA((finish_copies,)),
            pltpu.SemaphoreType.DMA((finish_copies,)),
            pltpu.SemaphoreType.DMA((2,)),
        ],
        compiler_params=pltpu.CompilerParams(
            collective_id=1, has_side_effects=True, vmem_limit_bytes=48 * 2**20
        ),
        name="finish",
    )(
        partial,
        patch_hidden,
        out_weight.reshape(heads * dim, -1),
        dec_kv_weight.reshape(kv_rows, 2 * dec_width),
        norm_gain.reshape(hn, slice_width),
        jnp.concatenate([key_gain, key_gain]).reshape(1, dec_width),
        jnp.concatenate([query_gain, query_gain]).reshape(1, dec_width),
        dec_query_weight,
        dec_out_weight,
        byte_states,
        byte_patch.reshape(1, bytes_),
        mates,
    )


def solution(mesh):
    placed = (
        P("ctx", "head"),
        P("ctx", "head", None),
        P("ctx", "head", None),
        P("ctx", "head", None),
        P("ctx", "head", None),
        P("ctx", "head", None),
        P("ctx"),
        P(),
        P("head", None, None),
        P(),
        P(None, None, "head"),
        P(None, "head"),
        P(),
        P(),
        P("head", None),
        P("ctx", None),
        P("ctx"),
    )
    return jax.shard_map(
        functools.partial(per_device, mesh.shape["ctx"] // 4, mesh.shape["head"]),
        mesh=mesh,
        in_specs=placed,
        out_specs=(P("ctx", "head"), P("ctx", "head")),
        check_vma=False,
    )
```

```python
import functools

import jax
import jax.numpy as jnp
from jax import lax
from jax.experimental import pallas as pl
from jax.experimental.pallas import tpu as pltpu
from jax.sharding import PartitionSpec as P

MESH = pl.DeviceIdType.MESH
VMEM = pltpu.VMEM
F32 = jnp.float32
BF16 = jnp.bfloat16
LOW = -1e20
HIDE = -1e30
LOG2E = 1.4426950408889634


def in_vmem():
    return pl.BlockSpec(memory_space=pltpu.VMEM)


def in_place():
    return pl.BlockSpec(memory_space=pl.ANY)


class Place:
    def __init__(self, zn):
        c = lax.axis_index("ctx")
        self.c = c
        self.zn = zn
        self.z = lax.div(c, 4)
        self.yl = lax.rem(lax.div(c, 2), 2)
        self.k = lax.rem(c, 2)
        self.cores = (self.k, 1 - self.k)

    def around(self, step):
        return lax.rem(self.z + (step + 2 * self.zn), self.zn)

    def device(self, step, other_y, other_core):
        y = 1 - self.yl if other_y else self.yl
        return {"ctx": self.around(step) * 4 + y * 2 + self.cores[other_core]}

    def near(self):
        found = [self.device(0, False, True)]
        for core in (False, True):
            found.append(self.device(0, True, core))
            found += [self.device(way, False, core) for way in (1, -1)]
        return found


class Copy:
    def __init__(self, dma):
        self.dma, self.got = dma, False

    def start(self):
        self.dma.start()
        return self

    def receive(self):
        if not self.got:
            self.dma.wait_recv()
        self.got = True


class Sends:
    def __init__(self, send_sem, recv_sem):
        self.send_sem, self.recv_sem, self.made = send_sem, recv_sem, []

    def make(self, src, dst, device):
        at = len(self.made)
        copy = Copy(
            pltpu.make_async_remote_copy(
                src_ref=src,
                dst_ref=dst,
                send_sem=self.send_sem.at[at],
                recv_sem=self.recv_sem.at[at],
                device_id=device,
                device_id_type=MESH,
            )
        )
        self.made.append(copy)
        return copy.start()

    def close(self):
        for copy in self.made:
            copy.receive()
        for copy in self.made:
            copy.dma.wait_send()


class Loads:
    def __init__(self, sem):
        self.sem, self.used = sem, 0

    def start(self, src, dst):
        copy = pltpu.make_async_copy(src, dst, self.sem.at[self.used])
        self.used += 1
        copy.start()
        return copy


def greet(devices):
    barrier = pltpu.get_barrier_semaphore()
    for device in devices:
        pl.semaphore_signal(barrier, inc=1, device_id=device, device_id_type=MESH)
    pl.semaphore_wait(barrier, len(devices))


def aligned(start, size):
    return pl.ds(pl.multiple_of(start, size), size)


def ring_gather(sends, place, source, buffer, idle=()):
    zn = place.zn
    rows = source.shape[1]
    far, near = zn // 2, zn - 1 - zn // 2
    mine = buffer.at[aligned(place.c * rows, rows), :]

    def first_hop(step, other_y, cores):
        return [
            sends.make(source.at[place.cores[core]], mine, place.device(step, other_y, core)) for core in cores
        ]

    arrived = {}
    for way, count in ((1, far), (-1, near)):
        if count:
            arrived[0, way, 0] = first_hop(way, False, (0, 1))
    from_y = first_hop(0, True, (0, 1))
    first_hop(0, False, (1,))
    buffer[aligned(place.c * rows, rows), :] = source[place.k]
    for turn in range(max(far, near)):
        for stream, step in ((0, turn + 1), (1, turn)):
            y = place.yl if stream == 0 else 1 - place.yl
            counts = (far, near) if stream == 0 else (near, far)
            for way, count in zip((1, -1), counts):
                if step >= count:
                    continue
                for copy in arrived[stream, way, step - 1] if step else from_y:
                    copy.receive()
                chip = place.around(-way * step) * 2 + y
                piece = buffer.at[aligned(chip * 2 * rows, 2 * rows), :]
                arrived[stream, way, step] = [sends.make(piece, piece, place.device(way, False, 0))]
        if turn < len(idle):
            idle[turn]()
    for work in idle[max(far, near) :]:
        work()


def spread(
    zn, q_hbm, nk_hbm, nv_hbm, ck_hbm, cv_hbm, cr_hbm, nr_hbm,
    qg, kc, vc, bounds,
    q_in, new_in, old_in, nr, held, q_half, kv_half, send_sem, recv_sem, local_sem,
):
    place = Place(zn)
    sends, loads = Sends(send_sem, recv_sem), Loads(local_sem)
    k = place.k
    new, cached = nk_hbm.shape[0], ck_hbm.shape[0]
    width = q_half.shape[2]
    peer = place.device(0, False, True)
    q_load = loads.start(q_hbm, q_in)
    small = [loads.start(cr_hbm, held.at[k]), loads.start(nr_hbm, nr)]
    kv_loads = [
        (loads.start(ck_hbm, old_in.at[0]), loads.start(nk_hbm, new_in.at[0])),
        (loads.start(cv_hbm, old_in.at[1]), loads.start(nv_hbm, new_in.at[1])),
    ]
    greet(place.near())
    q_load.wait()
    flat = q_in[...].reshape(new, 2 * width)
    q_half[0] = flat[:, :width]
    q_half[1] = flat[:, width:]
    chip = place.z * 2 + place.yl
    waits = []

    def swap(which, out):
        for copy in kv_loads[which]:
            copy.wait()
        for value, count, at, to in (
            (old_in[which], cached, 0, k * cached),
            (new_in[which], new, cached, 2 * cached + k * new),
        ):
            flat = value.reshape(count, 2 * width)
            rows = pl.ds(at, count)
            kv_half[which, 0, rows, :] = flat[:, :width]
            kv_half[which, 1, rows, :] = flat[:, width:]
            target = out.at[aligned(to, count), :]
            sends.make(kv_half.at[which, 1 - k, rows, :], target, peer)
            waits.append(loads.start(kv_half.at[which, k, rows, :], target))

    def see():
        small[1].wait()
        swapped.receive()
        both = held[...]
        mates = nr[...]
        total = mates.shape[1]
        zero = jnp.zeros((1, total), F32)
        low, high, start = zero, zero, zero
        below = jnp.zeros((1, 1), F32)
        for r in range(8):
            ones = jnp.where(both <= r, 1.0, 0.0)
            upto = jnp.sum(jnp.sum(ones, axis=0), axis=(0, 1), keepdims=True)
            first = jnp.sum(jnp.where(mates < r, 1.0, 0.0), axis=1, keepdims=True)
            here = mates == r
            low = jnp.where(here, below, low)
            high = jnp.where(here, upto, high)
            start = jnp.where(here, first, start)
            below = upto
        shift = chip * 2 * new
        index = lax.broadcasted_iota(jnp.int32, (1, total), 1)
        bounds[0:1, :] = low.astype(jnp.int32)
        bounds[1:2, :] = high.astype(jnp.int32)
        bounds[2:3, :] = start.astype(jnp.int32) - shift
        bounds[3:4, :] = index - (shift - 1)
        bounds[4:8, :] = jnp.zeros((4, total), jnp.int32)

    def swap_requests():
        small[0].wait()
        return sends.make(held.at[k], held.at[k], peer)

    swapped = swap_requests()
    ring_gather(
        sends, place, q_half, qg, [functools.partial(swap, 0, kc), functools.partial(swap, 1, vc), see]
    )
    for copy in waits:
        copy.wait()
    sends.close()


def attend(cached, block, scale, q_ref, k_ref, v_ref, bv_ref, bs_ref, o_ref, m_s, l_s, acc_s):
    rows = q_ref.shape[0]
    new = k_ref.shape[0] - cached
    q0 = pl.program_id(0) * rows
    last = q0 + rows - 1
    heads, dim = acc_s.shape[0], acc_s.shape[1]

    def columns(h):
        return slice(h * dim, (h + 1) * dim)

    def scores_of(first, count, base, low, high):
        found = []
        for h in range(heads):
            scores = lax.dot_general(
                k_ref[pl.ds(first, count), columns(h)],
                q_ref[:, columns(h)],
                (((1,), (1,)), ((), ())),
                preferred_element_type=F32,
            )
            if low is not None:
                at = lax.broadcasted_iota(jnp.int32, scores.shape, 0) + base
                scores = jnp.where((at >= low) & (at < high), scores, HIDE)
            found.append(scores)
        return found

    def mixed(h, first, weights):
        return lax.dot_general(
            v_ref[pl.ds(first, weights.shape[0]), columns(h)],
            weights.astype(BF16),
            (((0,), (0,)), ((), ())),
            preferred_element_type=F32,
        )

    def top_of(scores):
        return (jnp.max(scores, axis=0, keepdims=True) * scale).astype(BF16).astype(F32)

    low_first, low_last = bs_ref[0, q0], bs_ref[0, last]
    high_first, high_last = bs_ref[1, q0], bs_ref[1, last]
    sees_new = (bs_ref[3, last] > 0) & (bs_ref[2, q0] < new)
    sees_all = (low_last <= 0) & (high_first >= cached)

    @pl.when(sees_all)
    def _():
        old = scores_of(0, cached, 0, None, None)
        late = scores_of(cached, new, 0, bv_ref[2:3, :], bv_ref[3:4, :])
        kept = []
        for h in range(heads):
            top = jnp.maximum(top_of(old[h]), top_of(late[h]))
            kept.append((jnp.exp2(old[h] * scale - top), jnp.exp2(late[h] * scale - top)))
            m_s[h] = top
        for h in range(heads):
            w_old, w_late = kept[h]
            l_s[h] = jnp.sum(w_old, axis=0, keepdims=True) + jnp.sum(w_late, axis=0, keepdims=True)
            acc_s[h] = mixed(h, 0, w_old) + mixed(h, cached, w_late)

    @pl.when(jnp.logical_not(sees_all))
    def _():
        m_s[...] = jnp.full_like(m_s, LOW).astype(BF16).astype(F32)
        l_s[...] = jnp.zeros_like(l_s)
        acc_s[...] = jnp.zeros_like(acc_s)

        def add(first, count, base, low, high):
            scores = scores_of(first, count, base, low, high)
            kept = []
            for h in range(heads):
                m_old = m_s[h]
                m_new = jnp.maximum(m_old, top_of(scores[h]))
                weights = jnp.exp2(scores[h] * scale - m_new)
                fade = jnp.exp2(m_old - m_new)
                m_s[h] = m_new
                l_s[h] = l_s[h] * fade + jnp.sum(weights, axis=0, keepdims=True)
                kept.append((fade, weights))
            for h in range(heads):
                fade, weights = kept[h]
                acc_s[h] = acc_s[h] * fade + mixed(h, first, weights)

        begin = lax.div(low_first, block)
        end = jnp.where(high_last > low_first, lax.div(high_last + block - 1, block), begin)

        def one_block(b, carry):
            first = pl.multiple_of(b * block, block)
            whole = (low_last <= first) & (high_first >= first + block)

            @pl.when(whole)
            def _():
                add(first, block, first, None, None)

            @pl.when(jnp.logical_not(whole))
            def _():
                add(first, block, first, bv_ref[0:1, :], bv_ref[1:2, :])

            return carry

        lax.fori_loop(begin, end, one_block, 0)

        @pl.when(sees_new)
        def _():
            add(cached, new, 0, bv_ref[2:3, :], bv_ref[3:4, :])

    for h in range(heads):
        pack(o_ref.at[0, h], acc_s[h], m_s[h], l_s[h])


def pack(ref, out, top, total):
    dim = out.shape[0]
    ref[0:dim, :] = out.astype(BF16)
    coarse = total.astype(BF16).astype(F32)
    row = lax.broadcasted_iota(jnp.int32, (16, out.shape[1]), 0)
    tail = jnp.where(row == 0, top, jnp.where(row == 1, coarse, jnp.where(row == 2, total - coarse, 0.0)))
    ref[dim : dim + 16, :] = tail.astype(BF16)


def unpack(ref):
    value = ref[...]
    dim = value.shape[0] - 16
    tail = value[dim:, :].astype(F32)
    return value[:dim, :].astype(F32), tail[0:1, :], tail[1:2, :] + tail[2:3, :]


def merged(parts):
    top = parts[0][1]
    for part in parts[1:]:
        top = jnp.maximum(top, part[1])
    out, total = 0.0, 0.0
    for o, m, l in parts:
        factor = jnp.exp2(m - top)
        out = out + o * factor
        total = total + l * factor
    return out, top, total


def head_norm(values, gain, half):
    lane = lax.broadcasted_iota(jnp.int32, values.shape, 1)
    first = lane < half
    squares = values * values
    s0 = jnp.sum(jnp.where(first, squares, 0.0), axis=1, keepdims=True)
    s1 = jnp.sum(jnp.where(first, 0.0, squares), axis=1, keepdims=True)
    return values * lax.rsqrt(jnp.where(first, s0, s1) / half + 1e-6) * gain


def finish(
    zn, hn, part, hidden_hbm, w_hbm, dkv_hbm, gain_hbm, kgain_hbm, qgain_hbm, dqw_hbm, dow_hbm, states_hbm, bp_hbm, nr_hbm,
    patch_out, byte_out,
    hidden, w_ref, dkv_in, dkv, gain_ref, kgain, qgain, dqw_ref, dow_ref, states_ref, nr,
    ring_in, ring_out, last, last_in, att, rs_out, rs_in, ag_in, kv_tile, kvg, bq_tile, bq,
    bp_both, mix_tile, mix, bs_out, bs_in, send_sem, recv_sem, local_sem,
):
    place = Place(zn)
    sends, loads = Sends(send_sem, recv_sem), Loads(local_sem)
    k, z, yl = place.k, place.z, place.yl
    me = lax.axis_index("head")
    peer = place.device(0, False, True)
    others = [lax.rem(me + i, hn) for i in range(1, hn)]
    sources = [me] + [lax.rem(me + hn - i, hn) for i in range(1, hn)]
    for_queries = [
        loads.start(a, b)
        for a, b in ((states_hbm, states_ref), (dqw_hbm, dqw_ref), (qgain_hbm, qgain), (bp_hbm, bp_both.at[k]))
    ]
    dkv_load = loads.start(dkv_hbm, dkv_in)
    w_loads = [loads.start(w_hbm, w_ref), loads.start(hidden_hbm, hidden)]
    late = [
        loads.start(a, b)
        for a, b in ((gain_hbm, gain_ref), (kgain_hbm, kgain), (nr_hbm, nr), (dow_hbm, dow_ref))
    ]
    greet(place.near() + [{"head": d} for d in others])
    new, slice_width = hidden.shape
    heads = part.shape[1]
    dim = part.shape[2] - 16
    bytes_, half = states_ref.shape[0], kgain.shape[1]

    swapped = []

    def byte_queries():
        for copy in for_queries:
            copy.wait()
        proj = jnp.dot(states_ref[...], dqw_ref[...], preferred_element_type=F32)
        gain = jnp.concatenate([qgain[...], qgain[...]], axis=1)
        normed = head_norm(proj, gain, half)
        lane = lax.broadcasted_iota(jnp.int32, normed.shape, 1)
        bq_tile[0] = jnp.where(lane < half, normed, 0.0).astype(BF16)
        bq_tile[1] = jnp.where(lane < half, pltpu.roll(normed, half, 1), 0.0).astype(BF16)
        rows = aligned(k * bytes_, bytes_)
        swapped.append(sends.make(bp_both.at[k], bp_both.at[k], peer))
        sends.make(bq_tile.at[1 - k], bq.at[rows, :], peer)
        bq[rows, :] = bq_tile[k]

    def flat_weights():
        dkv_load.wait()
        count = dkv.shape[0] // 4
        for i in range(4):
            rows = slice(i * count, (i + 1) * count)
            dkv[rows, :] = dkv_in[rows].reshape(count, dkv.shape[1])

    idle = [byte_queries, flat_weights]
    far, near = zn // 2, zn - 1 - zn // 2
    counts = [(far, near) if h % 2 == 0 else (near, far) for h in range(heads)]
    made = {}
    for step in range(max(far, near)):
        for h in range(heads):
            for way in (0, 1):
                count = counts[h][way]
                if step >= count:
                    continue
                sign = 1 - 2 * way
                target = place.around(sign * (count - step))
                if step == 0:
                    src = part.at[target, h]
                else:
                    made[h, way, step - 1].receive()
                    src = ring_out.at[h, way, step]
                    pack(src, *merged([unpack(part.at[target, h]), unpack(ring_in.at[h, way, step - 1])]))
                made[h, way, step] = sends.make(src, ring_in.at[h, way, step], place.device(sign, False, 0))
        if step < len(idle):
            idle[step]()
    for work in idle[max(far, near) :]:
        work()
    summed = []
    for h in range(heads):
        got = [unpack(part.at[z, h])]
        for way in (0, 1):
            count = counts[h][way]
            if count:
                made[h, way, count - 1].receive()
                got.append(unpack(ring_in.at[h, way, count - 1]))
        summed.append(merged(got))
    for y in (0, 1):
        cols = slice(y * 2 * new, (y + 1) * 2 * new)
        for core in (0, 1):
            joined = []
            for a, b in zip(*summed):
                a, b = a[:, cols], b[:, cols]
                lane = lax.broadcasted_iota(jnp.int32, a.shape, 1)
                if core == 0:
                    joined.append(jnp.where(lane < new, a, pltpu.roll(b, new, 1)))
                else:
                    joined.append(jnp.where(lane < new, pltpu.roll(a, new, 1), b))
            pack(last.at[y, core], *joined)
    across = sends.make(last.at[1 - yl, k], last_in.at[0], place.device(0, True, False))
    beside = sends.make(last.at[yl, 1 - k], last_in.at[1], peer)
    diagonal = sends.make(last.at[1 - yl, 1 - k], last_in.at[2], place.device(0, True, True))
    for pair, parts, waits in (
        (k, (last.at[yl, k], last_in.at[0]), (across,)),
        (1 - k, (last_in.at[1], last_in.at[2]), (beside, diagonal)),
    ):
        for copy in waits:
            copy.receive()
        out, _, total = merged([unpack(ref) for ref in parts])
        turned = (out / total).T.astype(BF16)
        both = jnp.concatenate([turned[:new], turned[new:]], axis=1)
        att[:, aligned(pair * 2 * dim, 2 * dim)] = both

    for copy in w_loads:
        copy.wait()
    mine = att[...]

    def columns_for(d):
        return jnp.dot(mine, w_ref[:, aligned(d * slice_width, slice_width)], preferred_element_type=F32)

    rs_sends = []
    for i, d in enumerate(others):
        rs_out[i] = columns_for(d).astype(BF16)
        rs_sends.append(sends.make(rs_out.at[i], rs_in.at[i], {"head": d}))
    own = columns_for(me) + hidden[...].astype(F32)
    for i, copy in enumerate(rs_sends):
        copy.receive()
        own = own + rs_in[i].astype(F32)
    rounded = own.astype(BF16)
    ag_in[0] = rounded
    ag_sends = [sends.make(ag_in.at[0], ag_in.at[1 + i], {"head": d}) for i, d in enumerate(others)]
    patch_out[...] = rounded
    for copy in late:
        copy.wait()
    squares, proj = 0.0, 0.0
    for i, source in enumerate(sources):
        if i:
            ag_sends[i - 1].receive()
        wide = ag_in[i].astype(F32)
        squares = squares + jnp.sum(wide * wide, axis=1, keepdims=True)
        scaled = (wide * gain_ref[:, aligned(source * slice_width, slice_width)]).astype(BF16)
        rows = aligned(source * slice_width, slice_width)
        proj = proj + jnp.dot(scaled, dkv[rows, :], preferred_element_type=F32)
    proj = proj * lax.rsqrt(squares / (hn * slice_width) + 1e-5)
    width = 2 * half
    keys = head_norm(proj[:, :width], jnp.concatenate([kgain[...], kgain[...]], axis=1), half)
    values = proj[:, width:]
    lane = lax.broadcasted_iota(jnp.int32, keys.shape, 1)
    kv_tile[0] = jnp.where(lane < half, keys, pltpu.roll(values, half, 1)).astype(BF16)
    kv_tile[1] = jnp.where(lane < half, pltpu.roll(keys, half, 1), values).astype(BF16)

    spans = []

    def byte_spans():
        swapped[0].receive()
        owner = jnp.concatenate([bp_both[0], bp_both[1]], axis=1)
        first = jnp.zeros(owner.shape, F32)
        mates = nr[...]
        for r in range(1, 8):
            begins = jnp.sum(jnp.where(mates < r, 1.0, 0.0), axis=1, keepdims=True)
            first = jnp.where(owner.astype(F32) >= begins, begins, first)
        spans.append((first.astype(jnp.int32), owner))

    ring_gather(sends, place, kv_tile, kvg, [byte_spans])
    for copy in sends.made:
        copy.receive()
    first, owner = spans[0]

    queries = bq[...]
    block = min(512, kvg.shape[0])
    scale = half ** (-0.5) * LOG2E
    out, total = 0.0, 0.0
    for b in range(kvg.shape[0] // block):
        kv = kvg[b * block : (b + 1) * block, :]
        scores = lax.dot_general(kv, queries, (((1,), (1,)), ((), ())), preferred_element_type=F32)
        at = lax.broadcasted_iota(jnp.int32, scores.shape, 0) + b * block
        weights = jnp.where((at >= first) & (at <= owner), jnp.exp2(scores * scale), 0.0)
        total = total + jnp.sum(weights, axis=0, keepdims=True)
        out = out + lax.dot_general(
            kv, weights.astype(BF16), (((0,), (0,)), ((), ())), preferred_element_type=F32
        )
    mix_tile[...] = (out[half:, :] / total).astype(BF16)
    mix_rows = aligned(k * half, half)
    theirs, ours = aligned((1 - k) * bytes_, bytes_), aligned(k * bytes_, bytes_)
    mix_send = sends.make(mix_tile.at[:, theirs], mix.at[mix_rows, :], peer)
    mix[mix_rows, :] = mix_tile[:, ours]
    mix_send.receive()
    mixed = mix[...]
    out_width = byte_out.shape[1]

    def byte_columns_for(d):
        cols = aligned(d * out_width, out_width)
        return lax.dot_general(mixed, dow_ref[:, cols], (((0,), (0,)), ((), ())), preferred_element_type=F32)

    bs_sends = []
    for i, d in enumerate(others):
        bs_out[i] = byte_columns_for(d).astype(BF16)
        bs_sends.append(sends.make(bs_out.at[i], bs_in.at[i], {"head": d}))
    own = byte_columns_for(me) + states_ref[:, aligned(me * out_width, out_width)].astype(F32)
    for i, copy in enumerate(bs_sends):
        copy.receive()
        own = own + bs_in[i].astype(F32)
    byte_out[...] = own.astype(BF16)
    sends.close()


def per_device(
    zn,
    hn,
    patch_hidden,
    queries,
    new_keys,
    new_values,
    cache_keys,
    cache_values,
    cache_request,
    new_request,
    out_weight,
    norm_gain,
    dec_kv_weight,
    dec_query_weight,
    query_gain,
    key_gain,
    dec_out_weight,
    byte_states,
    byte_patch,
):
    new, heads, dim = queries.shape
    cached = cache_keys.shape[0]
    total = new_request.shape[0]
    pair = heads // 2 * dim
    all_keys = 2 * (cached + new)
    slice_width = patch_hidden.shape[1]
    held = cache_request.reshape(8, cached // 8)
    mates = new_request.reshape(1, total)
    gather_copies = 1 + 4 + 7 + 2 * zn
    gathered, keys, values, bounds = pl.pallas_call(
        functools.partial(spread, zn),
        out_shape=(
            jax.ShapeDtypeStruct((total, pair), BF16),
            jax.ShapeDtypeStruct((all_keys, pair), BF16),
            jax.ShapeDtypeStruct((all_keys, pair), BF16),
            jax.ShapeDtypeStruct((8, total), jnp.int32),
        ),
        in_specs=[in_place()] * 7,
        out_specs=(in_vmem(),) * 4,
        scratch_shapes=[
            VMEM(queries.shape, BF16),
            VMEM((2, *new_keys.shape), BF16),
            VMEM((2, *cache_keys.shape), BF16),
            VMEM((1, total), jnp.int32),
            VMEM((2, *held.shape), jnp.int32),
            VMEM((2, new, pair), BF16),
            VMEM((2, 2, cached + new, pair), BF16),
            pltpu.SemaphoreType.DMA((gather_copies,)),
            pltpu.SemaphoreType.DMA((gather_copies,)),
            pltpu.SemaphoreType.DMA((11,)),
        ],
        compiler_params=pltpu.CompilerParams(
            collective_id=0, has_side_effects=True, vmem_limit_bytes=32 * 2**20
        ),
        name="spread",
    )(queries, new_keys, new_values, cache_keys, cache_values, held, mates)

    tile = 4 * new
    block = min(512, cached)
    partial = pl.pallas_call(
        functools.partial(attend, 2 * cached, block, dim ** (-0.5) * LOG2E),
        out_shape=jax.ShapeDtypeStruct((zn, heads // 2, dim + 16, tile), BF16),
        grid=(zn,),
        in_specs=[
            pl.BlockSpec((tile, pair), lambda t: (t, 0)),
            pl.BlockSpec((all_keys, pair), lambda t: (0, 0)),
            pl.BlockSpec((all_keys, pair), lambda t: (0, 0)),
            pl.BlockSpec((8, tile), lambda t: (0, t)),
            pl.BlockSpec(memory_space=pltpu.SMEM),
        ],
        out_specs=pl.BlockSpec((1, heads // 2, dim + 16, tile), lambda t: (t, 0, 0, 0)),
        scratch_shapes=[
            VMEM((heads // 2, 1, tile), F32),
            VMEM((heads // 2, 1, tile), F32),
            VMEM((heads // 2, dim, tile), F32),
        ],
        compiler_params=pltpu.CompilerParams(vmem_limit_bytes=40 * 2**20),
        name="attend",
    )(gathered, keys, values, bounds, bounds)

    kv_rows = dec_kv_weight.shape[0]
    dec_width = dec_kv_weight.shape[2]
    bytes_ = byte_states.shape[0]
    out_width = dec_out_weight.shape[1] // hn
    half = dec_width // 2
    steps = max(zn // 2, 1)
    peers = max(hn - 1, 1)
    finish_copies = 2 + 2 * (zn - 1) + 3 + 3 * (hn - 1) + 7 + 2 * zn + 1
    flat_weight = out_weight.reshape(heads * dim, -1)
    return pl.pallas_call(
        functools.partial(finish, zn, hn),
        out_shape=(
            jax.ShapeDtypeStruct(patch_hidden.shape, BF16),
            jax.ShapeDtypeStruct((bytes_, out_width), BF16),
        ),
        in_specs=[in_vmem()] + [in_place()] * 11,
        out_specs=(in_vmem(), in_vmem()),
        scratch_shapes=[
            VMEM(patch_hidden.shape, BF16),
            VMEM(flat_weight.shape, BF16),
            VMEM(dec_kv_weight.shape, BF16),
            VMEM((kv_rows, 2 * dec_width), BF16),
            VMEM((1, kv_rows), F32),
            VMEM((1, half), F32),
            VMEM((1, half), F32),
            VMEM(dec_query_weight.shape, BF16),
            VMEM(dec_out_weight.shape, BF16),
            VMEM(byte_states.shape, BF16),
            VMEM((1, total), jnp.int32),
            VMEM((heads // 2, 2, steps, dim + 16, tile), BF16),
            VMEM((heads // 2, 2, steps, dim + 16, tile), BF16),
            VMEM((2, 2, dim + 16, 2 * new), BF16),
            VMEM((3, dim + 16, 2 * new), BF16),
            VMEM((new, heads * dim), BF16),
            VMEM((peers, new, slice_width), BF16),
            VMEM((peers, new, slice_width), BF16),
            VMEM((hn, new, slice_width), BF16),
            VMEM((2, new, dec_width), BF16),
            VMEM((total, dec_width), BF16),
            VMEM((2, bytes_, dec_width), BF16),
            VMEM((2 * bytes_, dec_width), BF16),
            VMEM((2, 1, bytes_), jnp.int32),
            VMEM((half, 2 * bytes_), BF16),
            VMEM((dec_width, bytes_), BF16),
            VMEM((peers, bytes_, out_width), BF16),
            VMEM((peers, bytes_, out_width), BF16),
            pltpu.SemaphoreType.DMA((finish_copies,)),
            pltpu.SemaphoreType.DMA((finish_copies,)),
            pltpu.SemaphoreType.DMA((11,)),
        ],
        compiler_params=pltpu.CompilerParams(
            collective_id=1, has_side_effects=True, vmem_limit_bytes=48 * 2**20
        ),
        name="finish",
    )(
        partial,
        patch_hidden,
        flat_weight,
        dec_kv_weight,
        norm_gain.reshape(1, kv_rows),
        key_gain.reshape(1, half),
        query_gain.reshape(1, half),
        dec_query_weight,
        dec_out_weight,
        byte_states,
        byte_patch.reshape(1, bytes_),
        mates,
    )


def solution(mesh):
    placed = (
        P("ctx", "head"),
        P("ctx", "head", None),
        P("ctx", "head", None),
        P("ctx", "head", None),
        P("ctx", "head", None),
        P("ctx", "head", None),
        P("ctx"),
        P(),
        P("head", None, None),
        P(),
        P(None, None, "head"),
        P(None, "head"),
        P(),
        P(),
        P("head", None),
        P("ctx", None),
        P("ctx"),
    )
    return jax.shard_map(
        functools.partial(per_device, mesh.shape["ctx"] // 4, mesh.shape["head"]),
        mesh=mesh,
        in_specs=placed,
        out_specs=(P("ctx", "head"), P("ctx", "head")),
        check_vma=False,
    )
```

```python
import functools

import jax
import jax.numpy as jnp
from jax import lax
from jax.experimental import pallas as pl
from jax.experimental.pallas import tpu as pltpu
from jax.sharding import PartitionSpec as P

MESH = pl.DeviceIdType.MESH
VMEM = pltpu.VMEM
F32 = jnp.float32
BF16 = jnp.bfloat16
LOW = -1e20
HIDE = -1e30
LOG2E = 1.4426950408889634


def in_vmem():
    return pl.BlockSpec(memory_space=pltpu.VMEM)


def in_place():
    return pl.BlockSpec(memory_space=pltpu.HBM)


class Place:
    def __init__(self, zn):
        c = lax.axis_index("ctx")
        self.c = c
        self.zn = zn
        self.z = lax.div(c, 4)
        self.yl = lax.rem(lax.div(c, 2), 2)
        self.k = lax.rem(c, 2)
        self.cores = (self.k, 1 - self.k)

    def around(self, step):
        return lax.rem(self.z + (step + 2 * self.zn), self.zn)

    def device(self, step, other_y, other_core):
        y = 1 - self.yl if other_y else self.yl
        return {"ctx": self.around(step) * 4 + y * 2 + self.cores[other_core]}

    def near(self, steps):
        found = [self.device(0, False, True)]
        for core in (False, True):
            found.append(self.device(0, True, core))
            found += [self.device(step, False, core) for step in steps]
        return found


class Copy:
    def __init__(self, dma):
        self.dma, self.got = dma, False

    def start(self):
        self.dma.start()
        return self

    def receive(self):
        if not self.got:
            self.dma.wait_recv()
        self.got = True


class Sends:
    def __init__(self, send_sem, recv_sem):
        self.send_sem, self.recv_sem, self.made = send_sem, recv_sem, []

    def make(self, src, dst, device):
        at = len(self.made)
        copy = Copy(
            pltpu.make_async_remote_copy(
                src_ref=src,
                dst_ref=dst,
                send_sem=self.send_sem.at[at],
                recv_sem=self.recv_sem.at[at],
                device_id=device,
                device_id_type=MESH,
            )
        )
        self.made.append(copy)
        return copy.start()

    def close(self):
        for copy in self.made:
            copy.receive()
        for copy in self.made:
            copy.dma.wait_send()


class Loads:
    def __init__(self, sem):
        self.sem, self.used = sem, 0

    def start(self, src, dst):
        copy = pltpu.make_async_copy(src, dst, self.sem.at[self.used])
        self.used += 1
        copy.start()
        return copy


def greet(devices):
    barrier = pltpu.get_barrier_semaphore()
    for device in devices:
        pl.semaphore_signal(barrier, inc=1, device_id=device, device_id_type=MESH)
    pl.semaphore_wait(barrier, len(devices))


def aligned(start, size):
    return pl.ds(pl.multiple_of(start, size), size)


def first_hop(sends, place, source, buffer, step, other_y, cores):
    rows = source.shape[1]
    mine = buffer.at[aligned(place.c * rows, rows), :]
    return [sends.make(source.at[place.cores[core]], mine, place.device(step, other_y, core)) for core in cores]


def ring_gather(sends, place, source, buffer, idle=()):
    zn = place.zn
    rows = source.shape[1]
    far, near = zn // 2, zn - 1 - zn // 2
    arrived = {}
    for way, count in ((1, far), (-1, near)):
        if count:
            for core, copy in enumerate(first_hop(sends, place, source, buffer, way, False, (0, 1))):
                arrived[0, core, way, 0] = copy
    from_y = first_hop(sends, place, source, buffer, 0, True, (0, 1))
    first_hop(sends, place, source, buffer, 0, False, (1,))
    buffer[aligned(place.c * rows, rows), :] = source[place.k]
    for turn in range(max(far, near)):
        for stream, step in ((0, turn + 1), (1, turn)):
            y = place.yl if stream == 0 else 1 - place.yl
            counts = (far, near) if stream == 0 else (near, far)
            for core in (0, 1):
                for way, count in zip((1, -1), counts):
                    if step >= count:
                        continue
                    (arrived[stream, core, way, step - 1] if step else from_y[core]).receive()
                    owner = place.around(-way * step) * 4 + y * 2 + place.cores[core]
                    piece = buffer.at[aligned(owner * rows, rows), :]
                    arrived[stream, core, way, step] = sends.make(piece, piece, place.device(way, False, 0))
        if turn < len(idle):
            idle[turn]()
    for work in idle[max(far, near) :]:
        work()


def line_steps(zn):
    return sorted([way * n for n in range(1, zn // 2 + 1) for way in (1, -1) if 2 * n < zn or way > 0], key=lambda n: -abs(n))


def line_gather(sends, place, source, buffer, idle=()):
    rows = source.shape[1]
    found = {}
    for step in line_steps(place.zn):
        found[step] = first_hop(sends, place, source, buffer, step, False, (0, 1))
    found[0] = first_hop(sends, place, source, buffer, 0, False, (1,))
    first_hop(sends, place, source, buffer, 0, True, (0, 1))
    buffer[aligned(place.c * rows, rows), :] = source[place.k]
    for work in idle:
        work()
    for step in reversed(line_steps(place.zn)):
        for copy in found[step]:
            copy.receive()
        chip = place.around(-step) * 2 + place.yl
        piece = buffer.at[aligned(chip * 2 * rows, 2 * rows), :]
        sends.make(piece, piece, place.device(0, True, False))


def spread(
    zn, q_hbm, nk_hbm, nv_hbm, ck_hbm, cv_hbm, cr_hbm, nr_hbm,
    qg, kc, vc, bounds,
    q_in, new_in, old_in, nr, held, q_half, kv_half, send_sem, recv_sem, local_sem,
):
    place = Place(zn)
    sends, loads = Sends(send_sem, recv_sem), Loads(local_sem)
    k = place.k
    new, cached = nk_hbm.shape[0], ck_hbm.shape[0]
    width = q_half.shape[2]
    peer = place.device(0, False, True)
    q_load = loads.start(q_hbm, q_in)
    small = [loads.start(cr_hbm, held.at[k]), loads.start(nr_hbm, nr)]
    kv_loads = [
        (loads.start(ck_hbm, old_in.at[0]), loads.start(nk_hbm, new_in.at[0])),
        (loads.start(cv_hbm, old_in.at[1]), loads.start(nv_hbm, new_in.at[1])),
    ]
    greet(place.near((1, -1)))
    q_load.wait()
    flat = q_in[...].reshape(new, 2 * width)
    q_half[0] = flat[:, :width]
    q_half[1] = flat[:, width:]
    chip = place.z * 2 + place.yl
    waits = []

    def swap(which, out):
        for copy in kv_loads[which]:
            copy.wait()
        for value, count, at, to in (
            (old_in[which], cached, 0, k * cached),
            (new_in[which], new, cached, 2 * cached + k * new),
        ):
            flat = value.reshape(count, 2 * width)
            rows = pl.ds(at, count)
            kv_half[which, 0, rows, :] = flat[:, :width]
            kv_half[which, 1, rows, :] = flat[:, width:]
            target = out.at[aligned(to, count), :]
            sends.make(kv_half.at[which, 1 - k, rows, :], target, peer)
            waits.append(loads.start(kv_half.at[which, k, rows, :], target))

    def see():
        small[1].wait()
        swapped.receive()
        both = held[...]
        mates = nr[...]
        total = mates.shape[1]
        zero = jnp.zeros((1, total), F32)
        low, high, start = zero, zero, zero
        below = jnp.zeros((1, 1), F32)
        for r in range(8):
            ones = jnp.where(both <= r, 1.0, 0.0)
            upto = jnp.sum(jnp.sum(ones, axis=0), axis=(0, 1), keepdims=True)
            first = jnp.sum(jnp.where(mates < r, 1.0, 0.0), axis=1, keepdims=True)
            here = mates == r
            low = jnp.where(here, below, low)
            high = jnp.where(here, upto, high)
            start = jnp.where(here, first, start)
            below = upto
        shift = chip * 2 * new
        index = lax.broadcasted_iota(jnp.int32, (1, total), 1)
        bounds[0:1, :] = low.astype(jnp.int32)
        bounds[1:2, :] = high.astype(jnp.int32)
        bounds[2:3, :] = start.astype(jnp.int32) - shift
        bounds[3:4, :] = index - (shift - 1)
        bounds[4:8, :] = jnp.zeros((4, total), jnp.int32)

    def swap_requests():
        small[0].wait()
        return sends.make(held.at[k], held.at[k], peer)

    swapped = swap_requests()
    ring_gather(
        sends, place, q_half, qg, [functools.partial(swap, 0, kc), functools.partial(swap, 1, vc), see]
    )
    for copy in waits:
        copy.wait()
    sends.close()


def attend(rows, cached, block, scale, q_ref, k_ref, v_ref, bv_ref, bs_ref, o_ref, m_s, l_s, acc_s):
    new = k_ref.shape[0] - cached
    heads, dim = acc_s.shape[0], acc_s.shape[1]

    def columns(h):
        return slice(h * dim, (h + 1) * dim)

    def mixed(h, first, weights):
        return lax.dot_general(
            v_ref[pl.ds(first, weights.shape[0]), columns(h)],
            weights.astype(BF16),
            (((0,), (0,)), ((), ())),
            preferred_element_type=F32,
        )

    def top_of(scores):
        return (jnp.max(scores, axis=0, keepdims=True) * scale).astype(BF16).astype(F32)

    def one_tile(t, carry):
        q0 = pl.multiple_of(t * rows, rows)
        last = q0 + rows - 1
        lanes = pl.ds(q0, rows)
        low_first, low_last = bs_ref[0, q0], bs_ref[0, last]
        high_first, high_last = bs_ref[1, q0], bs_ref[1, last]
        sees_new = (bs_ref[3, last] > 0) & (bs_ref[2, q0] < new)
        sees_all = (low_last <= 0) & (high_first >= cached)
        begin = lax.div(low_first, block)
        end = jnp.where(high_last > low_first, lax.div(high_last + block - 1, block), begin)
        sees_much = end - begin > 2

        def scores_of(first, count, base, masks):
            found = []
            for h in range(heads):
                scores = lax.dot_general(
                    k_ref[pl.ds(first, count), columns(h)],
                    q_ref[lanes, columns(h)],
                    (((1,), (1,)), ((), ())),
                    preferred_element_type=F32,
                )
                if masks is not None:
                    at = lax.broadcasted_iota(jnp.int32, scores.shape, 0) + base
                    low, high = (bv_ref[m : m + 1, lanes] for m in masks)
                    scores = jnp.where((at >= low) & (at < high), scores, HIDE)
                found.append(scores)
            return found

        def one_pass(masks):
            old = scores_of(0, cached, 0, masks)
            late = scores_of(cached, new, 0, (2, 3))
            kept = []
            for h in range(heads):
                top = jnp.maximum(jnp.maximum(top_of(old[h]), top_of(late[h])), LOW)
                top = top.astype(BF16).astype(F32)
                kept.append((jnp.exp2(old[h] * scale - top), jnp.exp2(late[h] * scale - top)))
                m_s[h] = top
            for h in range(heads):
                w_old, w_late = kept[h]
                l_s[h] = jnp.sum(w_old, axis=0, keepdims=True) + jnp.sum(w_late, axis=0, keepdims=True)
                acc_s[h] = mixed(h, 0, w_old) + mixed(h, cached, w_late)

        @pl.when(sees_all)
        def _():
            one_pass(None)

        @pl.when(jnp.logical_not(sees_all) & sees_much)
        def _():
            one_pass((0, 1))

        @pl.when(jnp.logical_not(sees_all) & jnp.logical_not(sees_much))
        def _():
            m_s[...] = jnp.full_like(m_s, LOW).astype(BF16).astype(F32)
            l_s[...] = jnp.zeros_like(l_s)
            acc_s[...] = jnp.zeros_like(acc_s)

            def add(first, count, base, masks):
                scores = scores_of(first, count, base, masks)
                kept = []
                for h in range(heads):
                    m_old = m_s[h]
                    m_new = jnp.maximum(m_old, top_of(scores[h]))
                    weights = jnp.exp2(scores[h] * scale - m_new)
                    fade = jnp.exp2(m_old - m_new)
                    m_s[h] = m_new
                    l_s[h] = l_s[h] * fade + jnp.sum(weights, axis=0, keepdims=True)
                    kept.append((fade, weights))
                for h in range(heads):
                    fade, weights = kept[h]
                    acc_s[h] = acc_s[h] * fade + mixed(h, first, weights)

            def one_block(b, carry):
                first = pl.multiple_of(b * block, block)
                add(first, block, first, (0, 1))
                return carry

            lax.fori_loop(begin, end, one_block, 0)

            @pl.when(sees_new)
            def _():
                add(cached, new, 0, (2, 3))

        for h in range(heads):
            for y in (0, 1):
                cols = slice(y * rows // 2, (y + 1) * rows // 2)
                pack(o_ref.at[t, h, y], acc_s[h, :, cols], m_s[h, :, cols], l_s[h, :, cols])
        return carry

    lax.fori_loop(0, o_ref.shape[0], one_tile, 0)


def pack(ref, out, top, total):
    dim = out.shape[0]
    ref[0:dim, :] = out.astype(BF16)
    coarse = total.astype(BF16).astype(F32)
    row = lax.broadcasted_iota(jnp.int32, (16, out.shape[1]), 0)
    tail = jnp.where(row == 0, top, jnp.where(row == 1, coarse, jnp.where(row == 2, total - coarse, 0.0)))
    ref[dim : dim + 16, :] = tail.astype(BF16)


def unpack(ref):
    value = ref[...]
    dim = value.shape[0] - 16
    tail = value[dim:, :].astype(F32)
    return value[:dim, :].astype(F32), tail[0:1, :], tail[1:2, :] + tail[2:3, :]


def merged(parts):
    top = parts[0][1]
    for part in parts[1:]:
        top = jnp.maximum(top, part[1])
    out, total = 0.0, 0.0
    for o, m, l in parts:
        factor = jnp.exp2(m - top)
        out = out + o * factor
        total = total + l * factor
    return out, top, total


def head_norm(values, gain, half):
    lane = lax.broadcasted_iota(jnp.int32, values.shape, 1)
    first = lane < half
    squares = values * values
    s0 = jnp.sum(jnp.where(first, squares, 0.0), axis=1, keepdims=True)
    s1 = jnp.sum(jnp.where(first, 0.0, squares), axis=1, keepdims=True)
    return values * lax.rsqrt(jnp.where(first, s0, s1) / half + 1e-6) * gain


def finish(
    zn, hn, part, hidden_hbm, w_hbm, dkv_hbm, gain_hbm, kgain_hbm, qgain_hbm, dqw_hbm, dow_hbm, states_hbm, bp_hbm, nr_hbm,
    patch_out, byte_out,
    hidden, w_ref, dkv_in, dkv, gain_ref, kgain, qgain, dqw_ref, dow_ref, states_ref, nr,
    ring_in, ring_out, last, last_in, att, rs_out, rs_in, ag_in, kv_tile, kvg, bq_tile, bq,
    bp_both, span, mix_tile, mix, bs_out, bs_in, send_sem, recv_sem, local_sem,
):
    place = Place(zn)
    sends, loads = Sends(send_sem, recv_sem), Loads(local_sem)
    k, z, yl = place.k, place.z, place.yl
    me = lax.axis_index("head")
    peer = place.device(0, False, True)
    x, yh = lax.div(me, 2), lax.rem(me, 2)
    xn = hn // 2
    ways = [(dx, dy) for dy in (1, 0) for dx in sorted(range(xn), key=lambda n: -min(n, xn - n)) if dx or dy]

    def head_at(dx, dy):
        return lax.rem(x + dx + xn, xn) * 2 + (1 - yh if dy else yh)

    others = [head_at(dx, dy) for dx, dy in ways]
    sources = [me] + [head_at(-dx, dy) for dx, dy in ways]
    for_queries = [
        loads.start(a, b)
        for a, b in ((states_hbm, states_ref), (dqw_hbm, dqw_ref), (qgain_hbm, qgain), (bp_hbm, bp_both.at[k]))
    ]
    dkv_load = loads.start(dkv_hbm, dkv_in)
    w_loads = [loads.start(w_hbm, w_ref), loads.start(hidden_hbm, hidden)]
    late = [
        loads.start(a, b)
        for a, b in ((gain_hbm, gain_ref), (kgain_hbm, kgain), (nr_hbm, nr), (dow_hbm, dow_ref))
    ]
    greet(place.near(line_steps(zn)) + [{"head": d} for d in others])
    new, slice_width = hidden.shape
    heads = part.shape[1]
    dim = part.shape[3] - 16
    bytes_, half = states_ref.shape[0], kgain.shape[1]

    swapped = []

    def byte_queries():
        for copy in for_queries:
            copy.wait()
        proj = jnp.dot(states_ref[...], dqw_ref[...], preferred_element_type=F32)
        gain = jnp.concatenate([qgain[...], qgain[...]], axis=1)
        normed = head_norm(proj, gain, half)
        lane = lax.broadcasted_iota(jnp.int32, normed.shape, 1)
        bq_tile[0] = jnp.where(lane < half, normed, 0.0).astype(BF16)
        bq_tile[1] = jnp.where(lane < half, pltpu.roll(normed, half, 1), 0.0).astype(BF16)
        rows = aligned(k * bytes_, bytes_)
        swapped.append(sends.make(bp_both.at[k], bp_both.at[k], peer))
        sends.make(bq_tile.at[1 - k], bq.at[rows, :], peer)
        bq[rows, :] = bq_tile[k]

    def flat_weights():
        dkv_load.wait()
        count = dkv.shape[0] // 4
        for i in range(4):
            rows = slice(i * count, (i + 1) * count)
            dkv[rows, :] = dkv_in[rows].reshape(count, dkv.shape[1])

    idle = [byte_queries, flat_weights]
    far, near = zn // 2, zn - 1 - zn // 2
    chains = [(h, y) for h in range(heads) for y in (0, 1)]
    counts = {(h, y): (far, near) if h % 2 == 0 else (near, far) for h, y in chains}
    made = {}
    for step in range(max(far, near)):
        for chain in chains:
            for way in (0, 1):
                count = counts[chain][way]
                if step >= count:
                    continue
                sign = 1 - 2 * way
                target = place.around(sign * (count - step))
                if step == 0:
                    src = part.at[target, *chain]
                else:
                    made[chain, way, step - 1].receive()
                    src = ring_out.at[*chain, way, step]
                    pack(src, *merged([unpack(part.at[target, *chain]), unpack(ring_in.at[*chain, way, step - 1])]))
                made[chain, way, step] = sends.make(
                    src, ring_in.at[*chain, way, step], place.device(sign, False, 0)
                )
        if step < len(idle):
            idle[step]()
    for work in idle[max(far, near) :]:
        work()
    summed = {}
    for chain in chains:
        got = [unpack(part.at[z, *chain])]
        for way in (0, 1):
            count = counts[chain][way]
            if count:
                made[chain, way, count - 1].receive()
                got.append(unpack(ring_in.at[*chain, way, count - 1]))
        summed[chain] = merged(got)
    for y in (0, 1):
        for core in (0, 1):
            joined = []
            for a, b in zip(summed[0, y], summed[1, y]):
                lane = lax.broadcasted_iota(jnp.int32, a.shape, 1)
                if core == 0:
                    joined.append(jnp.where(lane < new, a, pltpu.roll(b, new, 1)))
                else:
                    joined.append(jnp.where(lane < new, pltpu.roll(a, new, 1), b))
            pack(last.at[y, core], *joined)
    across = sends.make(last.at[1 - yl, k], last_in.at[0], place.device(0, True, False))
    beside = sends.make(last.at[yl, 1 - k], last_in.at[1], peer)
    diagonal = sends.make(last.at[1 - yl, 1 - k], last_in.at[2], place.device(0, True, True))
    for pair, parts, waits in (
        (k, (last.at[yl, k], last_in.at[0]), (across,)),
        (1 - k, (last_in.at[1], last_in.at[2]), (beside, diagonal)),
    ):
        for copy in waits:
            copy.receive()
        out, _, total = merged([unpack(ref) for ref in parts])
        turned = (out / total).T.astype(BF16)
        both = jnp.concatenate([turned[:new], turned[new:]], axis=1)
        att[:, aligned(pair * 2 * dim, 2 * dim)] = both

    for copy in w_loads:
        copy.wait()
    mine = att[...]

    def columns_for(d):
        return jnp.dot(mine, w_ref[:, aligned(d * slice_width, slice_width)], preferred_element_type=F32)

    rs_sends = []
    for i, d in enumerate(others):
        rs_out[i] = columns_for(d).astype(BF16)
        rs_sends.append(sends.make(rs_out.at[i], rs_in.at[i], {"head": d}))
    own = columns_for(me) + hidden[...].astype(F32)
    for i, copy in enumerate(rs_sends):
        copy.receive()
        own = own + rs_in[i].astype(F32)
    rounded = own.astype(BF16)
    ag_in[0] = rounded
    ag_sends = [sends.make(ag_in.at[0], ag_in.at[1 + i], {"head": d}) for i, d in enumerate(others)]
    patch_out[...] = rounded
    for copy in late:
        copy.wait()
    squares, proj = 0.0, 0.0
    for i, source in enumerate(sources):
        if i:
            ag_sends[i - 1].receive()
        wide = ag_in[i].astype(F32)
        squares = squares + jnp.sum(wide * wide, axis=1, keepdims=True)
        scaled = (wide * gain_ref[:, aligned(source * slice_width, slice_width)]).astype(BF16)
        rows = aligned(source * slice_width, slice_width)
        proj = proj + jnp.dot(scaled, dkv[rows, :], preferred_element_type=F32)
    proj = proj * lax.rsqrt(squares / (hn * slice_width) + 1e-5)
    width = 2 * half
    keys = head_norm(proj[:, :width], jnp.concatenate([kgain[...], kgain[...]], axis=1), half)
    values = proj[:, width:]
    lane = lax.broadcasted_iota(jnp.int32, keys.shape, 1)
    kv_tile[0] = jnp.where(lane < half, keys, pltpu.roll(values, half, 1)).astype(BF16)
    kv_tile[1] = jnp.where(lane < half, pltpu.roll(keys, half, 1), values).astype(BF16)

    def byte_spans():
        swapped[0].receive()
        owners = bp_both[...]
        first = jnp.zeros(owners.shape, F32)
        mates = nr[...]
        for r in range(1, 8):
            begins = jnp.sum(jnp.where(mates < r, 1.0, 0.0), axis=1, keepdims=True)[None]
            first = jnp.where(owners.astype(F32) >= begins, begins, first)
        span[...] = first.astype(jnp.int32)

    line_gather(sends, place, kv_tile, kvg, [byte_spans])
    for copy in sends.made:
        copy.receive()
    spans = (span, bp_both)

    block = min(512, kvg.shape[0])
    scale = half ** (-0.5) * LOG2E

    def byte_attention(core):
        queries = bq[aligned(core * bytes_, bytes_), :]
        first, owner = spans[0][core], spans[1][core]
        out, total = 0.0, 0.0
        for b in range(kvg.shape[0] // block):
            kv = kvg[b * block : (b + 1) * block, :]
            scores = lax.dot_general(kv, queries, (((1,), (1,)), ((), ())), preferred_element_type=F32)
            at = lax.broadcasted_iota(jnp.int32, scores.shape, 0) + b * block
            weights = jnp.where((at >= first) & (at <= owner), jnp.exp2(scores * scale), 0.0)
            total = total + jnp.sum(weights, axis=0, keepdims=True)
            out = out + lax.dot_general(
                kv, weights.astype(BF16), (((0,), (0,)), ((), ())), preferred_element_type=F32
            )
        return (out[half:, :] / total).astype(BF16)

    mix_rows = aligned(k * half, half)
    mix_tile[...] = byte_attention(1 - k)
    mix_send = sends.make(mix_tile, mix.at[mix_rows, :], peer)
    mix[mix_rows, :] = byte_attention(k)
    mix_send.receive()
    mixed = mix[...]
    out_width = byte_out.shape[1]

    def byte_columns_for(d):
        cols = aligned(d * out_width, out_width)
        return lax.dot_general(mixed, dow_ref[:, cols], (((0,), (0,)), ((), ())), preferred_element_type=F32)

    bs_sends = []
    for i, d in enumerate(others):
        bs_out[i] = byte_columns_for(d).astype(BF16)
        bs_sends.append(sends.make(bs_out.at[i], bs_in.at[i], {"head": d}))
    own = byte_columns_for(me) + states_ref[:, aligned(me * out_width, out_width)].astype(F32)
    for i, copy in enumerate(bs_sends):
        copy.receive()
        own = own + bs_in[i].astype(F32)
    byte_out[...] = own.astype(BF16)
    sends.close()


def per_device(
    zn,
    hn,
    patch_hidden,
    queries,
    new_keys,
    new_values,
    cache_keys,
    cache_values,
    cache_request,
    new_request,
    out_weight,
    norm_gain,
    dec_kv_weight,
    dec_query_weight,
    query_gain,
    key_gain,
    dec_out_weight,
    byte_states,
    byte_patch,
):
    new, heads, dim = queries.shape
    cached = cache_keys.shape[0]
    total = new_request.shape[0]
    pair = heads // 2 * dim
    all_keys = 2 * (cached + new)
    slice_width = patch_hidden.shape[1]
    held = cache_request.reshape(8, cached // 8)
    mates = new_request.reshape(1, total)
    gather_copies = 1 + 4 + 7 + 4 * zn
    gathered, keys, values, bounds = pl.pallas_call(
        functools.partial(spread, zn),
        out_shape=(
            jax.ShapeDtypeStruct((total, pair), BF16),
            jax.ShapeDtypeStruct((all_keys, pair), BF16),
            jax.ShapeDtypeStruct((all_keys, pair), BF16),
            jax.ShapeDtypeStruct((8, total), jnp.int32),
        ),
        in_specs=[in_place()] * 7,
        out_specs=(in_vmem(),) * 4,
        scratch_shapes=[
            VMEM(queries.shape, BF16),
            VMEM((2, *new_keys.shape), BF16),
            VMEM((2, *cache_keys.shape), BF16),
            VMEM((1, total), jnp.int32),
            VMEM((2, *held.shape), jnp.int32),
            VMEM((2, new, pair), BF16),
            VMEM((2, 2, cached + new, pair), BF16),
            pltpu.SemaphoreType.DMA((gather_copies,)),
            pltpu.SemaphoreType.DMA((gather_copies,)),
            pltpu.SemaphoreType.DMA((11,)),
        ],
        compiler_params=pltpu.CompilerParams(
            collective_id=0, has_side_effects=True, vmem_limit_bytes=32 * 2**20
        ),
        name="spread",
    )(queries, new_keys, new_values, cache_keys, cache_values, held, mates)

    tile = 4 * new
    block = min(512, cached)
    partial = pl.pallas_call(
        functools.partial(attend, tile, 2 * cached, block, dim ** (-0.5) * LOG2E),
        out_shape=jax.ShapeDtypeStruct((zn, heads // 2, 2, dim + 16, 2 * new), BF16),
        in_specs=[in_vmem()] * 4 + [pl.BlockSpec(memory_space=pltpu.SMEM)],
        out_specs=in_vmem(),
        scratch_shapes=[
            VMEM((heads // 2, 1, tile), F32),
            VMEM((heads // 2, 1, tile), F32),
            VMEM((heads // 2, dim, tile), F32),
        ],
        compiler_params=pltpu.CompilerParams(vmem_limit_bytes=40 * 2**20),
        name="attend",
    )(gathered, keys, values, bounds, bounds)

    kv_rows = dec_kv_weight.shape[0]
    dec_width = dec_kv_weight.shape[2]
    bytes_ = byte_states.shape[0]
    out_width = dec_out_weight.shape[1] // hn
    half = dec_width // 2
    steps = max(zn // 2, 1)
    peers = max(hn - 1, 1)
    finish_copies = 2 + 4 * (zn - 1) + 3 + 3 * (hn - 1) + 3 + 3 * (zn - 1) + 1
    flat_weight = out_weight.reshape(heads * dim, -1)
    return pl.pallas_call(
        functools.partial(finish, zn, hn),
        out_shape=(
            jax.ShapeDtypeStruct(patch_hidden.shape, BF16),
            jax.ShapeDtypeStruct((bytes_, out_width), BF16),
        ),
        in_specs=[in_vmem()] + [in_place()] * 11,
        out_specs=(in_vmem(), in_vmem()),
        scratch_shapes=[
            VMEM(patch_hidden.shape, BF16),
            VMEM(flat_weight.shape, BF16),
            VMEM(dec_kv_weight.shape, BF16),
            VMEM((kv_rows, 2 * dec_width), BF16),
            VMEM((1, kv_rows), F32),
            VMEM((1, half), F32),
            VMEM((1, half), F32),
            VMEM(dec_query_weight.shape, BF16),
            VMEM(dec_out_weight.shape, BF16),
            VMEM(byte_states.shape, BF16),
            VMEM((1, total), jnp.int32),
            VMEM((heads // 2, 2, 2, steps, dim + 16, 2 * new), BF16),
            VMEM((heads // 2, 2, 2, steps, dim + 16, 2 * new), BF16),
            VMEM((2, 2, dim + 16, 2 * new), BF16),
            VMEM((3, dim + 16, 2 * new), BF16),
            VMEM((new, heads * dim), BF16),
            VMEM((peers, new, slice_width), BF16),
            VMEM((peers, new, slice_width), BF16),
            VMEM((hn, new, slice_width), BF16),
            VMEM((2, new, dec_width), BF16),
            VMEM((total, dec_width), BF16),
            VMEM((2, bytes_, dec_width), BF16),
            VMEM((2 * bytes_, dec_width), BF16),
            VMEM((2, 1, bytes_), jnp.int32),
            VMEM((2, 1, bytes_), jnp.int32),
            VMEM((half, bytes_), BF16),
            VMEM((dec_width, bytes_), BF16),
            VMEM((peers, bytes_, out_width), BF16),
            VMEM((peers, bytes_, out_width), BF16),
            pltpu.SemaphoreType.DMA((finish_copies,)),
            pltpu.SemaphoreType.DMA((finish_copies,)),
            pltpu.SemaphoreType.DMA((11,)),
        ],
        compiler_params=pltpu.CompilerParams(
            collective_id=1, has_side_effects=True, vmem_limit_bytes=48 * 2**20
        ),
        name="finish",
    )(
        partial,
        patch_hidden,
        flat_weight,
        dec_kv_weight,
        norm_gain.reshape(1, kv_rows),
        key_gain.reshape(1, half),
        query_gain.reshape(1, half),
        dec_query_weight,
        dec_out_weight,
        byte_states,
        byte_patch.reshape(1, bytes_),
        mates,
    )


def solution(mesh):
    placed = (
        P("ctx", "head"),
        P("ctx", "head", None),
        P("ctx", "head", None),
        P("ctx", "head", None),
        P("ctx", "head", None),
        P("ctx", "head", None),
        P("ctx"),
        P(),
        P("head", None, None),
        P(),
        P(None, None, "head"),
        P(None, "head"),
        P(),
        P(),
        P("head", None),
        P("ctx", None),
        P("ctx"),
    )
    return jax.shard_map(
        functools.partial(per_device, mesh.shape["ctx"] // 4, mesh.shape["head"]),
        mesh=mesh,
        in_specs=placed,
        out_specs=(P("ctx", "head"), P("ctx", "head")),
        check_vma=False,
    )
```

```python
import functools

import jax
import jax.numpy as jnp
from jax import lax
from jax.experimental import pallas as pl
from jax.experimental.pallas import tpu as pltpu
from jax.sharding import PartitionSpec as P

MESH = pl.DeviceIdType.MESH
VMEM = pltpu.VMEM
F32 = jnp.float32
BF16 = jnp.bfloat16
HIDE = -1e30
LIFT = 16384.0
LOG2E = 1.4426950408889634


def in_vmem():
    return pl.BlockSpec(memory_space=pltpu.VMEM)


def in_place():
    return pl.BlockSpec(memory_space=pltpu.HBM)


class Place:
    def __init__(self, zn):
        c = lax.axis_index("ctx")
        self.c = c
        self.zn = zn
        self.z = lax.div(c, 4)
        self.yl = lax.rem(lax.div(c, 2), 2)
        self.k = lax.rem(c, 2)
        self.cores = (self.k, 1 - self.k)

    def around(self, step):
        return lax.rem(self.z + (step + 2 * self.zn), self.zn)

    def device(self, step, other_y, other_core):
        y = 1 - self.yl if other_y else self.yl
        return {"ctx": self.around(step) * 4 + y * 2 + self.cores[other_core]}

    def near(self, steps):
        found = [self.device(0, False, True)]
        for core in (False, True):
            found.append(self.device(0, True, core))
            found += [self.device(step, False, core) for step in steps]
        return found


class Copy:
    def __init__(self, dma):
        self.dma, self.got = dma, False

    def start(self):
        self.dma.start()
        return self

    def receive(self):
        if not self.got:
            self.dma.wait_recv()
        self.got = True


class Sends:
    def __init__(self, send_sem, recv_sem):
        self.send_sem, self.recv_sem, self.made = send_sem, recv_sem, []

    def make(self, src, dst, device):
        at = len(self.made)
        copy = Copy(
            pltpu.make_async_remote_copy(
                src_ref=src,
                dst_ref=dst,
                send_sem=self.send_sem.at[at],
                recv_sem=self.recv_sem.at[at],
                device_id=device,
                device_id_type=MESH,
            )
        )
        self.made.append(copy)
        return copy.start()

    def close(self):
        for copy in self.made:
            copy.receive()
        for copy in self.made:
            copy.dma.wait_send()


class Loads:
    def __init__(self, sem):
        self.sem, self.used = sem, 0

    def start(self, src, dst):
        copy = pltpu.make_async_copy(src, dst, self.sem.at[self.used])
        self.used += 1
        copy.start()
        return copy


def greet(devices):
    barrier = pltpu.get_barrier_semaphore()
    for device in devices:
        pl.semaphore_signal(barrier, inc=1, device_id=device, device_id_type=MESH)
    pl.semaphore_wait(barrier, len(devices))


def aligned(start, size):
    return pl.ds(pl.multiple_of(start, size), size)


def first_hop(sends, place, source, buffer, step, other_y, cores):
    rows = source.shape[1]
    mine = buffer.at[aligned(place.c * rows, rows), :]
    return [sends.make(source.at[place.cores[core]], mine, place.device(step, other_y, core)) for core in cores]


def ring_gather(sends, place, source, buffer, early, work):
    zn = place.zn
    rows = source.shape[1]
    far, near = zn // 2, zn - 1 - zn // 2
    arrived = {}
    for way, count in ((1, far), (-1, near)):
        if count:
            for core, copy in enumerate(first_hop(sends, place, source, buffer, way, False, (0, 1))):
                arrived[0, core, way, 0] = copy
    from_y = first_hop(sends, place, source, buffer, 0, True, (0, 1))
    from_core = first_hop(sends, place, source, buffer, 0, False, (1,))
    buffer[aligned(place.c * rows, rows), :] = source[place.k]
    early()
    for turn in range(far + 1):
        for stream, step in ((0, turn + 1), (1, turn)):
            y = place.yl if stream == 0 else 1 - place.yl
            counts = (far, near) if stream == 0 else (near, far)
            for core in (0, 1):
                for way, count in zip((1, -1), counts):
                    if step >= count:
                        continue
                    (arrived[stream, core, way, step - 1] if step else from_y[core]).receive()
                    owner = place.around(-way * step) * 4 + y * 2 + place.cores[core]
                    piece = buffer.at[aligned(owner * rows, rows), :]
                    arrived[stream, core, way, step] = sends.make(piece, piece, place.device(way, False, 0))
        if turn == 0:
            for copy in from_y + from_core:
                copy.receive()
        for (_, _, _, step), copy in list(arrived.items()):
            if step == turn - 1:
                copy.receive()
        work(turn)


def line_steps(zn):
    return sorted([way * n for n in range(1, zn // 2 + 1) for way in (1, -1) if 2 * n < zn or way > 0], key=lambda n: -abs(n))


def line_gather(sends, place, source, buffer, idle=()):
    rows = source.shape[1]
    found = {}
    for step in line_steps(place.zn):
        found[step] = first_hop(sends, place, source, buffer, step, False, (0, 1))
    found[0] = first_hop(sends, place, source, buffer, 0, False, (1,))
    first_hop(sends, place, source, buffer, 0, True, (0, 1))
    buffer[aligned(place.c * rows, rows), :] = source[place.k]
    for work in idle:
        work()
    for step in reversed(line_steps(place.zn)):
        for copy in found[step]:
            copy.receive()
        chip = place.around(-step) * 2 + place.yl
        piece = buffer.at[aligned(chip * 2 * rows, 2 * rows), :]
        sends.make(piece, piece, place.device(0, True, False))


def pack(ref, out, top, total):
    dim = out.shape[0]
    ref[0:dim, :] = out.astype(BF16)
    coarse = total.astype(BF16).astype(F32)
    row = lax.broadcasted_iota(jnp.int32, (16, out.shape[1]), 0)
    tail = jnp.where(row == 0, top, jnp.where(row == 1, coarse, jnp.where(row == 2, total - coarse, 0.0)))
    ref[dim : dim + 16, :] = tail.astype(BF16)


def unpack(ref):
    value = ref[...]
    dim = value.shape[0] - 16
    tail = value[dim:, :].astype(F32)
    return value[:dim, :].astype(F32), tail[0:1, :], tail[1:2, :] + tail[2:3, :]


def merged(parts):
    top = parts[0][1]
    for part in parts[1:]:
        top = jnp.maximum(top, part[1])
    out, total = 0.0, 0.0
    for o, m, l in parts:
        factor = jnp.exp2(m - top)
        out = out + o * factor
        total = total + l * factor
    return out, top, total


def head_norm(values, gain, half):
    lane = lax.broadcasted_iota(jnp.int32, values.shape, 1)
    first = lane < half
    squares = values * values
    s0 = jnp.sum(jnp.where(first, squares, 0.0), axis=1, keepdims=True)
    s1 = jnp.sum(jnp.where(first, 0.0, squares), axis=1, keepdims=True)
    return values * lax.rsqrt(jnp.where(first, s0, s1) / half + 1e-6) * gain


def solve(
    zn, hn, q_hbm, nk_hbm, nv_hbm, ck_hbm, cv_hbm, cr_hbm,
    hidden_hbm, w_hbm, dkv_hbm, gain_hbm, kgain_hbm, qgain_hbm, dqw_hbm, dow_hbm, states_hbm, bp_hbm, nr_hbm,
    patch_out, byte_out,
    q_in, new_in, old_in, held, q_half, kv_half, qg, kc, vc, key_mark, query_mark, part,
    hidden, w_ref, dkv_in, dkv, gain_ref, kgain, qgain, dqw_ref, dow_ref, states_ref, nr,
    ring_in, ring_out, last, last_in, att, rs_out, rs_in, ag_in, kv_tile, kvg, bq_tile, bq,
    bp_both, span, mix_tile, mix, bs_out, bs_in, send_sem, recv_sem, local_sem,
):
    place = Place(zn)
    sends, loads = Sends(send_sem, recv_sem), Loads(local_sem)
    k, z, yl = place.k, place.z, place.yl
    me = lax.axis_index("head")
    peer = place.device(0, False, True)
    x, yh = lax.div(me, 2), lax.rem(me, 2)
    xn = hn // 2
    ways = [(dx, dy) for dy in (1, 0) for dx in sorted(range(xn), key=lambda n: -min(n, xn - n)) if dx or dy]

    def head_at(dx, dy):
        return lax.rem(x + dx + xn, xn) * 2 + (1 - yh if dy else yh)

    others = [head_at(dx, dy) for dx, dy in ways]
    sources = [me] + [head_at(-dx, dy) for dx, dy in ways]
    q_load = loads.start(q_hbm, q_in)
    kv_loads = [
        (loads.start(ck_hbm, old_in.at[0]), loads.start(nk_hbm, new_in.at[0])),
        (loads.start(cv_hbm, old_in.at[1]), loads.start(nv_hbm, new_in.at[1])),
    ]
    small = [loads.start(cr_hbm, held.at[k]), loads.start(nr_hbm, nr)]
    for_queries = [
        loads.start(a, b)
        for a, b in ((states_hbm, states_ref), (dqw_hbm, dqw_ref), (qgain_hbm, qgain), (bp_hbm, bp_both.at[k]))
    ]
    dkv_load = loads.start(dkv_hbm, dkv_in)
    w_loads = [loads.start(w_hbm, w_ref), loads.start(hidden_hbm, hidden)]
    late = [
        loads.start(a, b)
        for a, b in ((gain_hbm, gain_ref), (kgain_hbm, kgain), (dow_hbm, dow_ref))
    ]
    greet(place.near(line_steps(zn)) + [{"head": d} for d in others])
    new, slice_width = hidden.shape
    heads = part.shape[1]
    dim = part.shape[3] - 16
    bytes_, half = states_ref.shape[0], kgain.shape[1]
    cached = ck_hbm.shape[0]
    width = q_half.shape[2]
    chip = z * 2 + yl
    tile = 4 * new
    chip_first = chip * 2 * new
    scale = dim ** (-0.5) * LOG2E

    q_load.wait()
    flat = q_in[...].reshape(new, 2 * width)
    q_half[0] = flat[:, :width]
    q_half[1] = flat[:, width:]
    kept, swaps = [], []

    def swap(which, out):
        for copy in kv_loads[which]:
            copy.wait()
        for value, count, at, to in (
            (old_in[which], cached, 0, k * cached),
            (new_in[which], new, cached, 2 * cached + k * new),
        ):
            flat = value.reshape(count, 2 * width)
            rows = pl.ds(at, count)
            kv_half[which, 0, rows, :] = flat[:, :width]
            kv_half[which, 1, rows, :] = flat[:, width:]
            target = out.at[aligned(to, count), :]
            swaps.append(sends.make(kv_half.at[which, 1 - k, rows, :], target, peer))
            kept.append(loads.start(kv_half.at[which, k, rows, :], target))

    def marks(at, cuts):
        lane = lax.broadcasted_iota(jnp.int32, (1, query_mark.shape[1]), 1)
        low, high = jnp.zeros(lane.shape, F32), jnp.zeros(lane.shape, F32)
        for r in range(8):
            low = jnp.where(lane == r, cuts[r], low)
            high = jnp.where(lane == r, cuts[r + 1], high)
        return jnp.where((at >= low) & (at < high), 1.0, 0.0)

    def positions(count, first):
        return (lax.broadcasted_iota(jnp.int32, (count, query_mark.shape[1]), 0) + first).astype(F32)

    def early():
        for copy in small:
            copy.wait()
        held_swap = sends.make(held.at[k], held.at[k], peer)
        swap(0, kc)
        swap(1, vc)
        cuts = [
            jnp.sum(jnp.where(nr[...] < r, 1.0, 0.0), axis=1, keepdims=True) for r in range(9)
        ]
        query_mark[...] = marks(positions(query_mark.shape[0], 0), cuts).astype(BF16)
        key_mark[2 * cached :, :] = (LIFT * marks(positions(2 * new, chip_first), cuts)).astype(BF16)
        held_swap.receive()
        both = held[...]
        cuts = [
            jnp.sum(jnp.sum(jnp.where(both < r, 1.0, 0.0), axis=0), axis=(0, 1), keepdims=True)
            for r in range(9)
        ]
        key_mark[: 2 * cached, :] = (LIFT * marks(positions(2 * cached, 0), cuts)).astype(BF16)

    def attend(t):
        q0 = pl.multiple_of(t * tile, tile)
        rows = pl.ds(q0, tile)
        columns = [slice(h * dim, (h + 1) * dim) for h in range(heads)]
        scores = []
        for cols in columns:
            found = lax.dot_general(
                jnp.concatenate([kc[:, cols], key_mark[...]], axis=1),
                jnp.concatenate([qg[rows, cols], query_mark[rows, :]], axis=1),
                (((1,), (1,)), ((), ())),
                preferred_element_type=F32,
            )
            late = found[2 * cached :]
            at = lax.broadcasted_iota(jnp.int32, late.shape, 0) + chip_first
            asked = lax.broadcasted_iota(jnp.int32, late.shape, 1) + q0
            late = jnp.where(at <= asked, late, HIDE)
            scores.append(jnp.concatenate([found[: 2 * cached], late], axis=0))
        weights = []
        for found in scores:
            top = jnp.max(found, axis=0, keepdims=True) * scale - LIFT * scale
            top = top.astype(BF16).astype(F32)
            weights.append((top, jnp.exp2(found * scale - (top + LIFT * scale))))
        for h, (top, found) in enumerate(weights):
            total = jnp.sum(found, axis=0, keepdims=True)
            out = lax.dot_general(
                vc[:, columns[h]], found.astype(BF16), (((0,), (0,)), ((), ())), preferred_element_type=F32
            )
            for y in (0, 1):
                cols = slice(y * 2 * new, (y + 1) * 2 * new)
                pack(part.at[t, h, y], out[:, cols], top[:, cols], total[:, cols])

    far, near = zn // 2, zn - 1 - zn // 2
    chains = [(h, y) for h in range(heads) for y in (0, 1)]
    counts = {(h, y): (far, near) if h % 2 == 0 else (near, far) for h, y in chains}
    made = {}

    def reduce_step(step, chosen):
        for chain in chains:
            for way in (0, 1):
                count = counts[chain][way]
                if step >= count or count not in chosen:
                    continue
                sign = 1 - 2 * way
                target = place.around(sign * (count - step))
                if step == 0:
                    src = part.at[target, *chain]
                else:
                    made[chain, way, step - 1].receive()
                    src = ring_out.at[*chain, way, step]
                    pack(src, *merged([unpack(part.at[target, *chain]), unpack(ring_in.at[*chain, way, step - 1])]))
                made[chain, way, step] = sends.make(
                    src, ring_in.at[*chain, way, step], place.device(sign, False, 0)
                )

    def work(turn):
        if turn == 0:
            for copy in kept:
                copy.wait()
            for copy in swaps:
                copy.receive()
        if turn == far:
            reduce_step(0, (near,))

        def one(i, carry):
            attend(lax.rem(z + (1 - 2 * i) * turn + 2 * zn, zn))
            return carry

        lax.fori_loop(0, 1 if turn in (0, far) else 2, one, 0)
        if turn == far:
            reduce_step(0, (far,))

    ring_gather(sends, place, q_half, qg, early, work)

    swapped = []

    def byte_queries():
        for copy in for_queries:
            copy.wait()
        proj = jnp.dot(states_ref[...], dqw_ref[...], preferred_element_type=F32)
        gain = jnp.concatenate([qgain[...], qgain[...]], axis=1)
        normed = head_norm(proj, gain, half)
        lane = lax.broadcasted_iota(jnp.int32, normed.shape, 1)
        bq_tile[0] = jnp.where(lane < half, normed, 0.0).astype(BF16)
        bq_tile[1] = jnp.where(lane < half, pltpu.roll(normed, half, 1), 0.0).astype(BF16)
        rows = aligned(k * bytes_, bytes_)
        swapped.append(sends.make(bp_both.at[k], bp_both.at[k], peer))
        sends.make(bq_tile.at[1 - k], bq.at[rows, :], peer)
        bq[rows, :] = bq_tile[k]

    def flat_weights():
        dkv_load.wait()
        count = dkv.shape[0] // 4
        for i in range(4):
            rows = slice(i * count, (i + 1) * count)
            dkv[rows, :] = dkv_in[rows].reshape(count, dkv.shape[1])

    idle = [byte_queries, flat_weights]
    for step in range(max(far, 1)):
        if step:
            reduce_step(step, (far, near))
        if step < len(idle):
            idle[step]()
    for work_left in idle[max(far, 1) :]:
        work_left()
    summed = {}
    for chain in chains:
        got = [unpack(part.at[z, *chain])]
        for way in (0, 1):
            count = counts[chain][way]
            if count:
                made[chain, way, count - 1].receive()
                got.append(unpack(ring_in.at[*chain, way, count - 1]))
        summed[chain] = merged(got)
    for y in (0, 1):
        for core in (0, 1):
            joined = []
            for a, b in zip(summed[0, y], summed[1, y]):
                lane = lax.broadcasted_iota(jnp.int32, a.shape, 1)
                if core == 0:
                    joined.append(jnp.where(lane < new, a, pltpu.roll(b, new, 1)))
                else:
                    joined.append(jnp.where(lane < new, pltpu.roll(a, new, 1), b))
            pack(last.at[y, core], *joined)
    across = sends.make(last.at[1 - yl, k], last_in.at[0], place.device(0, True, False))
    beside = sends.make(last.at[yl, 1 - k], last_in.at[1], peer)
    diagonal = sends.make(last.at[1 - yl, 1 - k], last_in.at[2], place.device(0, True, True))
    for pair, parts, waits in (
        (k, (last.at[yl, k], last_in.at[0]), (across,)),
        (1 - k, (last_in.at[1], last_in.at[2]), (beside, diagonal)),
    ):
        for copy in waits:
            copy.receive()
        out, _, total = merged([unpack(ref) for ref in parts])
        turned = (out / total).T.astype(BF16)
        both = jnp.concatenate([turned[:new], turned[new:]], axis=1)
        att[:, aligned(pair * 2 * dim, 2 * dim)] = both

    for copy in w_loads:
        copy.wait()
    mine = att[...]

    def columns_for(d):
        return jnp.dot(mine, w_ref[:, aligned(d * slice_width, slice_width)], preferred_element_type=F32)

    rs_sends = []
    for i, d in enumerate(others):
        rs_out[i] = columns_for(d).astype(BF16)
        rs_sends.append(sends.make(rs_out.at[i], rs_in.at[i], {"head": d}))
    own = columns_for(me) + hidden[...].astype(F32)
    for i, copy in enumerate(rs_sends):
        copy.receive()
        own = own + rs_in[i].astype(F32)
    rounded = own.astype(BF16)
    ag_in[0] = rounded
    ag_sends = [sends.make(ag_in.at[0], ag_in.at[1 + i], {"head": d}) for i, d in enumerate(others)]
    patch_out[...] = rounded
    for copy in late:
        copy.wait()
    squares, proj = 0.0, 0.0
    for i, source in enumerate(sources):
        if i:
            ag_sends[i - 1].receive()
        wide = ag_in[i].astype(F32)
        squares = squares + jnp.sum(wide * wide, axis=1, keepdims=True)
        scaled = (wide * gain_ref[:, aligned(source * slice_width, slice_width)]).astype(BF16)
        rows = aligned(source * slice_width, slice_width)
        proj = proj + jnp.dot(scaled, dkv[rows, :], preferred_element_type=F32)
    proj = proj * lax.rsqrt(squares / (hn * slice_width) + 1e-5)
    keys = head_norm(proj[:, : 2 * half], jnp.concatenate([kgain[...], kgain[...]], axis=1), half)
    values = proj[:, 2 * half :]
    lane = lax.broadcasted_iota(jnp.int32, keys.shape, 1)
    kv_tile[0] = jnp.where(lane < half, keys, pltpu.roll(values, half, 1)).astype(BF16)
    kv_tile[1] = jnp.where(lane < half, pltpu.roll(keys, half, 1), values).astype(BF16)

    def byte_spans():
        swapped[0].receive()
        owners = bp_both[...]
        first = jnp.zeros(owners.shape, F32)
        mates = nr[...]
        for r in range(1, 8):
            begins = jnp.sum(jnp.where(mates < r, 1.0, 0.0), axis=1, keepdims=True)[None]
            first = jnp.where(owners.astype(F32) >= begins, begins, first)
        span[...] = first.astype(jnp.int32)

    line_gather(sends, place, kv_tile, kvg, [byte_spans])
    for copy in sends.made:
        copy.receive()
    spans = (span, bp_both)

    block = min(512, kvg.shape[0])
    byte_scale = half ** (-0.5) * LOG2E

    def byte_attention(core):
        queries = bq[aligned(core * bytes_, bytes_), :]
        first, owner = spans[0][core], spans[1][core]
        out, total = 0.0, 0.0
        for b in range(kvg.shape[0] // block):
            kv = kvg[b * block : (b + 1) * block, :]
            scores = lax.dot_general(kv, queries, (((1,), (1,)), ((), ())), preferred_element_type=F32)
            at = lax.broadcasted_iota(jnp.int32, scores.shape, 0) + b * block
            weights = jnp.where((at >= first) & (at <= owner), jnp.exp2(scores * byte_scale), 0.0)
            total = total + jnp.sum(weights, axis=0, keepdims=True)
            out = out + lax.dot_general(
                kv, weights.astype(BF16), (((0,), (0,)), ((), ())), preferred_element_type=F32
            )
        return (out[half:, :] / total).astype(BF16)

    mix_rows = aligned(k * half, half)
    mix_tile[...] = byte_attention(1 - k)
    mix_send = sends.make(mix_tile, mix.at[mix_rows, :], peer)
    mix[mix_rows, :] = byte_attention(k)
    mix_send.receive()
    mixed = mix[...]
    out_width = byte_out.shape[1]

    def byte_columns_for(d):
        cols = aligned(d * out_width, out_width)
        return lax.dot_general(mixed, dow_ref[:, cols], (((0,), (0,)), ((), ())), preferred_element_type=F32)

    bs_sends = []
    for i, d in enumerate(others):
        bs_out[i] = byte_columns_for(d).astype(BF16)
        bs_sends.append(sends.make(bs_out.at[i], bs_in.at[i], {"head": d}))
    own = byte_columns_for(me) + states_ref[:, aligned(me * out_width, out_width)].astype(F32)
    for i, copy in enumerate(bs_sends):
        copy.receive()
        own = own + bs_in[i].astype(F32)
    byte_out[...] = own.astype(BF16)
    sends.close()


def per_device(
    zn,
    hn,
    patch_hidden,
    queries,
    new_keys,
    new_values,
    cache_keys,
    cache_values,
    cache_request,
    new_request,
    out_weight,
    norm_gain,
    dec_kv_weight,
    dec_query_weight,
    query_gain,
    key_gain,
    dec_out_weight,
    byte_states,
    byte_patch,
):
    new, heads, dim = queries.shape
    cached = cache_keys.shape[0]
    total = new_request.shape[0]
    pair = heads // 2 * dim
    all_keys = 2 * (cached + new)
    slice_width = patch_hidden.shape[1]
    held = cache_request.reshape(8, cached // 8)
    mates = new_request.reshape(1, total)
    tile = 4 * new
    kv_rows = dec_kv_weight.shape[0]
    dec_width = dec_kv_weight.shape[2]
    bytes_ = byte_states.shape[0]
    out_width = dec_out_weight.shape[1] // hn
    half = dec_width // 2
    steps = max(zn // 2, 1)
    peers = max(hn - 1, 1)
    copies = 5 + 7 + 4 * zn + 2 + 4 * (zn - 1) + 3 + 3 * (hn - 1) + 3 + 3 * (zn - 1) + 1
    flat_weight = out_weight.reshape(heads * dim, -1)
    return pl.pallas_call(
        functools.partial(solve, zn, hn),
        out_shape=(
            jax.ShapeDtypeStruct(patch_hidden.shape, BF16),
            jax.ShapeDtypeStruct((bytes_, out_width), BF16),
        ),
        in_specs=[in_place()] * 17,
        out_specs=(in_vmem(), in_vmem()),
        scratch_shapes=[
            VMEM(queries.shape, BF16),
            VMEM((2, *new_keys.shape), BF16),
            VMEM((2, *cache_keys.shape), BF16),
            VMEM((2, *held.shape), jnp.int32),
            VMEM((2, new, pair), BF16),
            VMEM((2, 2, cached + new, pair), BF16),
            VMEM((total, pair), BF16),
            VMEM((all_keys, pair), BF16),
            VMEM((all_keys, pair), BF16),
            VMEM((all_keys, 128), BF16),
            VMEM((total, 128), BF16),
            VMEM((zn, heads // 2, 2, dim + 16, 2 * new), BF16),
            VMEM(patch_hidden.shape, BF16),
            VMEM(flat_weight.shape, BF16),
            VMEM(dec_kv_weight.shape, BF16),
            VMEM((kv_rows, 2 * dec_width), BF16),
            VMEM((1, kv_rows), F32),
            VMEM((1, half), F32),
            VMEM((1, half), F32),
            VMEM(dec_query_weight.shape, BF16),
            VMEM(dec_out_weight.shape, BF16),
            VMEM(byte_states.shape, BF16),
            VMEM((1, total), jnp.int32),
            VMEM((heads // 2, 2, 2, steps, dim + 16, 2 * new), BF16),
            VMEM((heads // 2, 2, 2, steps, dim + 16, 2 * new), BF16),
            VMEM((2, 2, dim + 16, 2 * new), BF16),
            VMEM((3, dim + 16, 2 * new), BF16),
            VMEM((new, heads * dim), BF16),
            VMEM((peers, new, slice_width), BF16),
            VMEM((peers, new, slice_width), BF16),
            VMEM((hn, new, slice_width), BF16),
            VMEM((2, new, dec_width), BF16),
            VMEM((total, dec_width), BF16),
            VMEM((2, bytes_, dec_width), BF16),
            VMEM((2 * bytes_, dec_width), BF16),
            VMEM((2, 1, bytes_), jnp.int32),
            VMEM((2, 1, bytes_), jnp.int32),
            VMEM((half, bytes_), BF16),
            VMEM((dec_width, bytes_), BF16),
            VMEM((peers, bytes_, out_width), BF16),
            VMEM((peers, bytes_, out_width), BF16),
            pltpu.SemaphoreType.DMA((copies,)),
            pltpu.SemaphoreType.DMA((copies,)),
            pltpu.SemaphoreType.DMA((24,)),
        ],
        compiler_params=pltpu.CompilerParams(
            collective_id=0, has_side_effects=True, vmem_limit_bytes=60 * 2**20
        ),
        name="solve",
    )(
        queries,
        new_keys,
        new_values,
        cache_keys,
        cache_values,
        held,
        patch_hidden,
        flat_weight,
        dec_kv_weight,
        norm_gain.reshape(1, kv_rows),
        key_gain.reshape(1, half),
        query_gain.reshape(1, half),
        dec_query_weight,
        dec_out_weight,
        byte_states,
        byte_patch.reshape(1, bytes_),
        mates,
    )


def solution(mesh):
    placed = (
        P("ctx", "head"),
        P("ctx", "head", None),
        P("ctx", "head", None),
        P("ctx", "head", None),
        P("ctx", "head", None),
        P("ctx", "head", None),
        P("ctx"),
        P(),
        P("head", None, None),
        P(),
        P(None, None, "head"),
        P(None, "head"),
        P(),
        P(),
        P("head", None),
        P("ctx", None),
        P("ctx"),
    )
    return jax.shard_map(
        functools.partial(per_device, mesh.shape["ctx"] // 4, mesh.shape["head"]),
        mesh=mesh,
        in_specs=placed,
        out_specs=(P("ctx", "head"), P("ctx", "head")),
        check_vma=False,
    )
```

```python
import functools

import jax
import jax.numpy as jnp
from jax import lax
from jax.experimental import pallas as pl
from jax.experimental.pallas import tpu as pltpu
from jax.sharding import PartitionSpec as P

MESH = pl.DeviceIdType.MESH
VMEM = pltpu.VMEM
F32 = jnp.float32
BF16 = jnp.bfloat16
HIDE = -1e30
LIFT = 2048.0
LOG2E = 1.4426950408889634


def in_vmem():
    return pl.BlockSpec(memory_space=pltpu.VMEM)


def in_place():
    return pl.BlockSpec(memory_space=pltpu.HBM)


class Place:
    def __init__(self, zn):
        c = lax.axis_index("ctx")
        self.c = c
        self.zn = zn
        self.z = lax.div(c, 4)
        self.yl = lax.rem(lax.div(c, 2), 2)
        self.k = lax.rem(c, 2)
        self.cores = (self.k, 1 - self.k)

    def around(self, step):
        return lax.rem(self.z + (step + 2 * self.zn), self.zn)

    def device(self, step, other_y, other_core):
        y = 1 - self.yl if other_y else self.yl
        return {"ctx": self.around(step) * 4 + y * 2 + self.cores[other_core]}

    def near(self, steps):
        found = [self.device(0, False, True)]
        for core in (False, True):
            found.append(self.device(0, True, core))
            found += [self.device(step, False, core) for step in steps]
        return found


class Copy:
    def __init__(self, dma):
        self.dma, self.got = dma, False

    def start(self):
        self.dma.start()
        return self

    def receive(self):
        if not self.got:
            self.dma.wait_recv()
        self.got = True


class Sends:
    def __init__(self, send_sem, recv_sem):
        self.send_sem, self.recv_sem, self.made = send_sem, recv_sem, []

    def make(self, src, dst, device):
        at = len(self.made)
        copy = Copy(
            pltpu.make_async_remote_copy(
                src_ref=src,
                dst_ref=dst,
                send_sem=self.send_sem.at[at],
                recv_sem=self.recv_sem.at[at],
                device_id=device,
                device_id_type=MESH,
            )
        )
        self.made.append(copy)
        return copy.start()

    def close(self):
        for copy in self.made:
            copy.receive()
        for copy in self.made:
            copy.dma.wait_send()


class Loads:
    def __init__(self, sem):
        self.sem, self.used = sem, 0

    def start(self, src, dst):
        copy = pltpu.make_async_copy(src, dst, self.sem.at[self.used])
        self.used += 1
        copy.start()
        return copy


def greet(devices, meanwhile):
    barrier = pltpu.get_barrier_semaphore()
    for device in devices:
        pl.semaphore_signal(barrier, inc=1, device_id=device, device_id_type=MESH)
    meanwhile()
    pl.semaphore_wait(barrier, len(devices))


def aligned(start, size):
    return pl.ds(pl.multiple_of(start, size), size)


def first_hop(sends, place, source, buffer, step, other_y, cores):
    rows = source.shape[1]
    mine = buffer.at[aligned(place.c * rows, rows), :]
    return [sends.make(source.at[place.cores[core]], mine, place.device(step, other_y, core)) for core in cores]


def ring_gather(sends, place, source, buffer, early, work):
    zn = place.zn
    rows = source.shape[1]
    far, near = zn // 2, zn - 1 - zn // 2
    arrived = {}
    for way, count in ((1, far), (-1, near)):
        if count:
            for core, copy in enumerate(first_hop(sends, place, source, buffer, way, False, (0, 1))):
                arrived[0, core, way, 0] = copy
    from_y = first_hop(sends, place, source, buffer, 0, True, (0, 1))
    from_core = first_hop(sends, place, source, buffer, 0, False, (1,))
    buffer[aligned(place.c * rows, rows), :] = source[place.k]
    early()
    for turn in range(far + 1):
        for stream, step in ((0, turn + 1), (1, turn)):
            y = place.yl if stream == 0 else 1 - place.yl
            counts = (far, near) if stream == 0 else (near, far)
            for core in (0, 1):
                for way, count in zip((1, -1), counts):
                    if step >= count:
                        continue
                    (arrived[stream, core, way, step - 1] if step else from_y[core]).receive()
                    owner = place.around(-way * step) * 4 + y * 2 + place.cores[core]
                    piece = buffer.at[aligned(owner * rows, rows), :]
                    arrived[stream, core, way, step] = sends.make(piece, piece, place.device(way, False, 0))
        if turn == 0:
            for copy in from_y + from_core:
                copy.receive()
        for (_, _, _, step), copy in list(arrived.items()):
            if step == turn - 1:
                copy.receive()
        work(turn)


def direct_steps(zn):
    if zn == 8:
        return (2, -2, 1, -1)
    return tuple(way * n for n in range(1, zn // 2 + 1) for way in (1, -1) if 2 * n < zn or way > 0)


def stride_gather(sends, place, source, buffer, idle):
    zn, rows = place.zn, source.shape[1]
    steps = direct_steps(zn)
    from_y = first_hop(sends, place, source, buffer, 0, True, (0, 1))
    found = {(0, step): first_hop(sends, place, source, buffer, step, False, (0, 1)) for step in steps}
    first_hop(sends, place, source, buffer, 0, False, (1,))
    buffer[aligned(place.c * rows, rows), :] = source[place.k]
    idle()

    def piece(step, y):
        return buffer.at[aligned((place.around(step) * 2 + y) * 2 * rows, 2 * rows), :]

    for copy in from_y:
        copy.receive()
    theirs = piece(0, 1 - place.yl)
    for step in steps:
        found[1, step] = [sends.make(theirs, theirs, place.device(step, False, 0))]
    if zn != 8:
        return
    for stream, y in ((0, place.yl), (1, 1 - place.yl)):
        for way in (1, -1):
            for copy in found[stream, 2 * way]:
                copy.receive()
            passed = piece(-2 * way, y)
            sends.make(passed, passed, place.device(way, False, 0))
            if (way == 1) == (stream == 0):
                sends.make(passed, passed, place.device(2 * way, False, 0))


def pack(ref, out, top, total):
    dim = out.shape[0]
    ref[0:dim, :] = out.astype(BF16)
    coarse = total.astype(BF16).astype(F32)
    row = lax.broadcasted_iota(jnp.int32, (16, out.shape[1]), 0)
    tail = jnp.where(row == 0, top, jnp.where(row == 1, coarse, jnp.where(row == 2, total - coarse, 0.0)))
    ref[dim : dim + 16, :] = tail.astype(BF16)


def unpack(ref):
    value = ref[...]
    dim = value.shape[0] - 16
    tail = value[dim:, :].astype(F32)
    return value[:dim, :].astype(F32), tail[0:1, :], tail[1:2, :] + tail[2:3, :]


def merged(parts):
    top = parts[0][1]
    for part in parts[1:]:
        top = jnp.maximum(top, part[1])
    out, total = 0.0, 0.0
    for o, m, l in parts:
        factor = jnp.exp2(m - top)
        out = out + o * factor
        total = total + l * factor
    return out, top, total


def head_norm(values, gain, half):
    lane = lax.broadcasted_iota(jnp.int32, values.shape, 1)
    first = lane < half
    squares = values * values
    s0 = jnp.sum(jnp.where(first, squares, 0.0), axis=1, keepdims=True)
    s1 = jnp.sum(jnp.where(first, 0.0, squares), axis=1, keepdims=True)
    return values * lax.rsqrt(jnp.where(first, s0, s1) / half + 1e-6) * gain


def solve(
    zn, hn, q_hbm, nk_hbm, nv_hbm, ck_hbm, cv_hbm, cr_hbm,
    hidden_hbm, w_hbm, dkv_hbm, gain_hbm, kgain_hbm, qgain_hbm, dqw_hbm, dow_hbm, states_hbm, bp_hbm, nr_hbm,
    patch_out, byte_out,
    q_in, new_in, old_in, held, q_half, kv_half, qg, kc, vc, key_mark, query_mark, part,
    hidden, w_ref, dkv_in, dkv, gain_ref, kgain, qgain, dqw_ref, dow_ref, states_ref, nr,
    ring_in, ring_out, last, last_in, att, rs_out, rs_in, ag_in, kv_tile, kvg, bq_tile, bq,
    bp_both, span, mix_tile, mix, bs_out, bs_in, send_sem, recv_sem, local_sem,
):
    place = Place(zn)
    sends, loads = Sends(send_sem, recv_sem), Loads(local_sem)
    k, z, yl = place.k, place.z, place.yl
    me = lax.axis_index("head")
    peer = place.device(0, False, True)
    x, yh = lax.div(me, 2), lax.rem(me, 2)
    xn = hn // 2
    ways = [(dx, dy) for dy in (1, 0) for dx in sorted(range(xn), key=lambda n: -min(n, xn - n)) if dx or dy]

    def head_at(dx, dy):
        return lax.rem(x + dx + xn, xn) * 2 + (1 - yh if dy else yh)

    others = [head_at(dx, dy) for dx, dy in ways]
    sources = [me] + [head_at(-dx, dy) for dx, dy in ways]
    q_load = loads.start(q_hbm, q_in)
    kv_loads = [
        (loads.start(ck_hbm, old_in.at[0]), loads.start(nk_hbm, new_in.at[0])),
        (loads.start(cv_hbm, old_in.at[1]), loads.start(nv_hbm, new_in.at[1])),
    ]
    small = [loads.start(cr_hbm, held.at[k]), loads.start(nr_hbm, nr)]
    for_queries = [
        loads.start(a, b)
        for a, b in ((states_hbm, states_ref), (dqw_hbm, dqw_ref), (qgain_hbm, qgain), (bp_hbm, bp_both.at[k]))
    ]
    dkv_load = loads.start(dkv_hbm, dkv_in)
    w_loads = [loads.start(w_hbm, w_ref), loads.start(hidden_hbm, hidden)]
    late = [
        loads.start(a, b)
        for a, b in ((gain_hbm, gain_ref), (kgain_hbm, kgain), (dow_hbm, dow_ref))
    ]
    new, slice_width = hidden.shape
    heads = part.shape[1]
    dim = part.shape[3] - 16
    bytes_, half = states_ref.shape[0], kgain.shape[1]
    cached = ck_hbm.shape[0]
    width = q_half.shape[2]
    chip = z * 2 + yl
    tile = 4 * new
    chip_first = chip * 2 * new
    scale = dim ** (-0.5) * LOG2E

    kept, swaps = [], []

    def flatten():
        q_load.wait()
        flat = (q_in[...].reshape(new, 2 * width).astype(F32) * scale).astype(BF16)
        q_half[0] = flat[:, :width]
        q_half[1] = flat[:, width:]
        for which in (0, 1):
            for copy in kv_loads[which]:
                copy.wait()
            for value, count, at in ((old_in[which], cached, 0), (new_in[which], new, cached)):
                flat = value.reshape(count, 2 * width)
                rows = pl.ds(at, count)
                kv_half[which, 0, rows, :] = flat[:, :width]
                kv_half[which, 1, rows, :] = flat[:, width:]

    greet(place.near(direct_steps(zn)) + [{"head": d} for d in others], flatten)

    def swap(which, out):
        for count, at, to in ((cached, 0, k * cached), (new, cached, 2 * cached + k * new)):
            rows = pl.ds(at, count)
            target = out.at[aligned(to, count), :]
            swaps.append(sends.make(kv_half.at[which, 1 - k, rows, :], target, peer))
            kept.append(loads.start(kv_half.at[which, k, rows, :], target))

    def marks(at, cuts):
        lane = lax.broadcasted_iota(jnp.int32, (1, query_mark.shape[1]), 1)
        low, high = jnp.zeros(lane.shape, F32), jnp.zeros(lane.shape, F32)
        for r in range(8):
            low = jnp.where(lane == r, cuts[r], low)
            high = jnp.where(lane == r, cuts[r + 1], high)
        return jnp.where((at >= low) & (at < high), 1.0, 0.0)

    def positions(count, first):
        return (lax.broadcasted_iota(jnp.int32, (count, query_mark.shape[1]), 0) + first).astype(F32)

    def early():
        for copy in small:
            copy.wait()
        held_swap = sends.make(held.at[k], held.at[k], peer)
        swap(0, kc)
        swap(1, vc)
        cuts = [
            jnp.sum(jnp.where(nr[...] < r, 1.0, 0.0), axis=1, keepdims=True) for r in range(9)
        ]
        query_mark[...] = marks(positions(query_mark.shape[0], 0), cuts).astype(BF16)
        key_mark[2 * cached :, :] = (LIFT * marks(positions(2 * new, chip_first), cuts)).astype(BF16)
        held_swap.receive()
        both = held[...]
        cuts = [
            jnp.sum(jnp.sum(jnp.where(both < r, 1.0, 0.0), axis=0), axis=(0, 1), keepdims=True)
            for r in range(9)
        ]
        key_mark[: 2 * cached, :] = (LIFT * marks(positions(2 * cached, 0), cuts)).astype(BF16)

    def attend(t):
        q0 = pl.multiple_of(t * tile, tile)
        rows = pl.ds(q0, tile)
        columns = [slice(h * dim, (h + 1) * dim) for h in range(heads)]
        scores = []
        for cols in columns:
            found = lax.dot_general(
                jnp.concatenate([kc[:, cols], key_mark[...]], axis=1),
                jnp.concatenate([qg[rows, cols], query_mark[rows, :]], axis=1),
                (((1,), (1,)), ((), ())),
                preferred_element_type=F32,
            )
            late = found[2 * cached :]
            at = lax.broadcasted_iota(jnp.int32, late.shape, 0) + chip_first
            asked = lax.broadcasted_iota(jnp.int32, late.shape, 1) + q0
            late = jnp.where(at <= asked, late, HIDE)
            scores.append(jnp.concatenate([found[: 2 * cached], late], axis=0))
        weights = []
        for found in scores:
            top = jnp.max(found, axis=0, keepdims=True) - LIFT
            top = top.astype(BF16).astype(F32)
            weights.append((top, jnp.exp2(found - (top + LIFT))))
        for h, (top, found) in enumerate(weights):
            total = jnp.sum(found, axis=0, keepdims=True)
            out = lax.dot_general(
                vc[:, columns[h]], found.astype(BF16), (((0,), (0,)), ((), ())), preferred_element_type=F32
            )
            for y in (0, 1):
                cols = slice(y * 2 * new, (y + 1) * 2 * new)
                pack(part.at[t, h, y], out[:, cols], top[:, cols], total[:, cols])

    far, near = zn // 2, zn - 1 - zn // 2
    chains = [(h, y) for h in range(heads) for y in (0, 1)]
    counts = {(h, y): (far, near) if h % 2 == 0 else (near, far) for h, y in chains}
    made = {}

    def reduce_step(step, chosen):
        for chain in chains:
            for way in (0, 1):
                count = counts[chain][way]
                if step >= count or count not in chosen:
                    continue
                sign = 1 - 2 * way
                target = place.around(sign * (count - step))
                if step == 0:
                    src = part.at[target, *chain]
                else:
                    made[chain, way, step - 1].receive()
                    src = ring_out.at[*chain, way, step]
                    pack(src, *merged([unpack(part.at[target, *chain]), unpack(ring_in.at[*chain, way, step - 1])]))
                made[chain, way, step] = sends.make(
                    src, ring_in.at[*chain, way, step], place.device(sign, False, 0)
                )

    def work(turn):
        if turn == 0:
            for copy in kept:
                copy.wait()
            for copy in swaps:
                copy.receive()
        if turn == far:
            reduce_step(0, (near,))

        def one(i, carry):
            attend(lax.rem(z + (1 - 2 * i) * turn + 2 * zn, zn))
            return carry

        lax.fori_loop(0, 1 if turn in (0, far) else 2, one, 0)
        if turn == far:
            reduce_step(0, (far,))

    ring_gather(sends, place, q_half, qg, early, work)

    swapped = []

    def byte_queries():
        for copy in for_queries:
            copy.wait()
        proj = jnp.dot(states_ref[...], dqw_ref[...], preferred_element_type=F32)
        gain = jnp.concatenate([qgain[...], qgain[...]], axis=1)
        normed = head_norm(proj, gain, half)
        lane = lax.broadcasted_iota(jnp.int32, normed.shape, 1)
        bq_tile[0] = jnp.where(lane < half, normed, 0.0).astype(BF16)
        bq_tile[1] = jnp.where(lane < half, pltpu.roll(normed, half, 1), 0.0).astype(BF16)
        rows = aligned(k * bytes_, bytes_)
        swapped.append(sends.make(bp_both.at[k], bp_both.at[k], peer))
        sends.make(bq_tile.at[1 - k], bq.at[rows, :], peer)
        bq[rows, :] = bq_tile[k]

    def flat_weights():
        dkv_load.wait()
        count = dkv.shape[0] // 4
        for i in range(4):
            rows = slice(i * count, (i + 1) * count)
            dkv[rows, :] = dkv_in[rows].reshape(count, dkv.shape[1])

    idle = [byte_queries, flat_weights]
    for step in range(max(far, 1)):
        if step:
            reduce_step(step, (far, near))
        if step < len(idle):
            idle[step]()
    for work_left in idle[max(far, 1) :]:
        work_left()
    summed = {}
    for chain in chains:
        got = [unpack(part.at[z, *chain])]
        for way in (0, 1):
            count = counts[chain][way]
            if count:
                made[chain, way, count - 1].receive()
                got.append(unpack(ring_in.at[*chain, way, count - 1]))
        summed[chain] = merged(got)
    for y in (0, 1):
        for core in (0, 1):
            joined = []
            for a, b in zip(summed[0, y], summed[1, y]):
                lane = lax.broadcasted_iota(jnp.int32, a.shape, 1)
                if core == 0:
                    joined.append(jnp.where(lane < new, a, pltpu.roll(b, new, 1)))
                else:
                    joined.append(jnp.where(lane < new, pltpu.roll(a, new, 1), b))
            pack(last.at[y, core], *joined)
    across = sends.make(last.at[1 - yl, k], last_in.at[0], place.device(0, True, False))
    beside = sends.make(last.at[yl, 1 - k], last_in.at[1], peer)
    diagonal = sends.make(last.at[1 - yl, 1 - k], last_in.at[2], place.device(0, True, True))
    for pair, parts, waits in (
        (k, (last.at[yl, k], last_in.at[0]), (across,)),
        (1 - k, (last_in.at[1], last_in.at[2]), (beside, diagonal)),
    ):
        for copy in waits:
            copy.receive()
        out, _, total = merged([unpack(ref) for ref in parts])
        turned = (out / total).T.astype(BF16)
        both = jnp.concatenate([turned[:new], turned[new:]], axis=1)
        att[:, aligned(pair * 2 * dim, 2 * dim)] = both

    for copy in w_loads:
        copy.wait()
    mine = att[...]

    def columns_for(d):
        return jnp.dot(mine, w_ref[:, aligned(d * slice_width, slice_width)], preferred_element_type=F32)

    rs_sends = []
    for i, d in enumerate(others):
        rs_out[i] = columns_for(d).astype(BF16)
        rs_sends.append(sends.make(rs_out.at[i], rs_in.at[i], {"head": d}))
    own = columns_for(me) + hidden[...].astype(F32)
    for i, copy in enumerate(rs_sends):
        copy.receive()
        own = own + rs_in[i].astype(F32)
    rounded = own.astype(BF16)
    ag_in[0] = rounded
    ag_sends = [sends.make(ag_in.at[0], ag_in.at[1 + i], {"head": d}) for i, d in enumerate(others)]
    patch_out[...] = rounded
    for copy in late:
        copy.wait()
    squares, proj = 0.0, 0.0
    for i, source in enumerate(sources):
        if i:
            ag_sends[i - 1].receive()
        wide = ag_in[i].astype(F32)
        squares = squares + jnp.sum(wide * wide, axis=1, keepdims=True)
        scaled = (wide * gain_ref[:, aligned(source * slice_width, slice_width)]).astype(BF16)
        rows = aligned(source * slice_width, slice_width)
        proj = proj + jnp.dot(scaled, dkv[rows, :], preferred_element_type=F32)
    proj = proj * lax.rsqrt(squares / (hn * slice_width) + 1e-5)
    keys = head_norm(proj[:, : 2 * half], jnp.concatenate([kgain[...], kgain[...]], axis=1), half)
    values = proj[:, 2 * half :]
    lane = lax.broadcasted_iota(jnp.int32, keys.shape, 1)
    kv_tile[0] = jnp.where(lane < half, keys, pltpu.roll(values, half, 1)).astype(BF16)
    kv_tile[1] = jnp.where(lane < half, pltpu.roll(keys, half, 1), values).astype(BF16)

    def byte_spans():
        swapped[0].receive()
        owners = bp_both[...]
        first = jnp.zeros(owners.shape, F32)
        mates = nr[...]
        for r in range(1, 8):
            begins = jnp.sum(jnp.where(mates < r, 1.0, 0.0), axis=1, keepdims=True)[None]
            first = jnp.where(owners.astype(F32) >= begins, begins, first)
        span[...] = first.astype(jnp.int32)

    stride_gather(sends, place, kv_tile, kvg, byte_spans)
    for copy in sends.made:
        copy.receive()
    spans = (span, bp_both)

    block = min(512, kvg.shape[0])
    byte_scale = half ** (-0.5) * LOG2E

    def byte_attention(core):
        queries = bq[aligned(core * bytes_, bytes_), :]
        first, owner = spans[0][core], spans[1][core]
        out, total = 0.0, 0.0
        for b in range(kvg.shape[0] // block):
            kv = kvg[b * block : (b + 1) * block, :]
            scores = lax.dot_general(kv, queries, (((1,), (1,)), ((), ())), preferred_element_type=F32)
            at = lax.broadcasted_iota(jnp.int32, scores.shape, 0) + b * block
            weights = jnp.where((at >= first) & (at <= owner), jnp.exp2(scores * byte_scale), 0.0)
            total = total + jnp.sum(weights, axis=0, keepdims=True)
            out = out + lax.dot_general(
                kv, weights.astype(BF16), (((0,), (0,)), ((), ())), preferred_element_type=F32
            )
        return (out[half:, :] / total).astype(BF16)

    mix_rows = aligned(k * half, half)
    mix_tile[...] = byte_attention(1 - k)
    mix_send = sends.make(mix_tile, mix.at[mix_rows, :], peer)
    mix[mix_rows, :] = byte_attention(k)
    mix_send.receive()
    mixed = mix[...]
    out_width = byte_out.shape[1]

    def byte_columns_for(d):
        cols = aligned(d * out_width, out_width)
        return lax.dot_general(mixed, dow_ref[:, cols], (((0,), (0,)), ((), ())), preferred_element_type=F32)

    bs_sends = []
    for i, d in enumerate(others):
        bs_out[i] = byte_columns_for(d).astype(BF16)
        bs_sends.append(sends.make(bs_out.at[i], bs_in.at[i], {"head": d}))
    own = byte_columns_for(me) + states_ref[:, aligned(me * out_width, out_width)].astype(F32)
    for i, copy in enumerate(bs_sends):
        copy.receive()
        own = own + bs_in[i].astype(F32)
    byte_out[...] = own.astype(BF16)
    sends.close()


def hand_over(a, b, a_out, b_out, sem):
    loads = Loads(sem)
    for copy in (loads.start(a, a_out), loads.start(b, b_out)):
        copy.wait()


def per_device(
    zn,
    hn,
    patch_hidden,
    queries,
    new_keys,
    new_values,
    cache_keys,
    cache_values,
    cache_request,
    new_request,
    out_weight,
    norm_gain,
    dec_kv_weight,
    dec_query_weight,
    query_gain,
    key_gain,
    dec_out_weight,
    byte_states,
    byte_patch,
):
    new, heads, dim = queries.shape
    cached = cache_keys.shape[0]
    total = new_request.shape[0]
    pair = heads // 2 * dim
    all_keys = 2 * (cached + new)
    slice_width = patch_hidden.shape[1]
    held = cache_request.reshape(8, cached // 8)
    mates = new_request.reshape(1, total)
    tile = 4 * new
    kv_rows = dec_kv_weight.shape[0]
    dec_width = dec_kv_weight.shape[2]
    bytes_ = byte_states.shape[0]
    out_width = dec_out_weight.shape[1] // hn
    half = dec_width // 2
    steps = max(zn // 2, 1)
    peers = max(hn - 1, 1)
    copies = 5 + 7 + 4 * zn + 2 + 4 * (zn - 1) + 3 + 3 * (hn - 1) + 3 + 4 * zn + 1
    flat_weight = out_weight.reshape(heads * dim, -1)
    results = pl.pallas_call(
        functools.partial(solve, zn, hn),
        out_shape=(
            jax.ShapeDtypeStruct(patch_hidden.shape, BF16),
            jax.ShapeDtypeStruct((bytes_, out_width), BF16),
        ),
        in_specs=[in_place()] * 17,
        out_specs=(in_vmem(), in_vmem()),
        scratch_shapes=[
            VMEM(queries.shape, BF16),
            VMEM((2, *new_keys.shape), BF16),
            VMEM((2, *cache_keys.shape), BF16),
            VMEM((2, *held.shape), jnp.int32),
            VMEM((2, new, pair), BF16),
            VMEM((2, 2, cached + new, pair), BF16),
            VMEM((total, pair), BF16),
            VMEM((all_keys, pair), BF16),
            VMEM((all_keys, pair), BF16),
            VMEM((all_keys, 128), BF16),
            VMEM((total, 128), BF16),
            VMEM((zn, heads // 2, 2, dim + 16, 2 * new), BF16),
            VMEM(patch_hidden.shape, BF16),
            VMEM(flat_weight.shape, BF16),
            VMEM(dec_kv_weight.shape, BF16),
            VMEM((kv_rows, 2 * dec_width), BF16),
            VMEM((1, kv_rows), F32),
            VMEM((1, half), F32),
            VMEM((1, half), F32),
            VMEM(dec_query_weight.shape, BF16),
            VMEM(dec_out_weight.shape, BF16),
            VMEM(byte_states.shape, BF16),
            VMEM((1, total), jnp.int32),
            VMEM((heads // 2, 2, 2, steps, dim + 16, 2 * new), BF16),
            VMEM((heads // 2, 2, 2, steps, dim + 16, 2 * new), BF16),
            VMEM((2, 2, dim + 16, 2 * new), BF16),
            VMEM((3, dim + 16, 2 * new), BF16),
            VMEM((new, heads * dim), BF16),
            VMEM((peers, new, slice_width), BF16),
            VMEM((peers, new, slice_width), BF16),
            VMEM((hn, new, slice_width), BF16),
            VMEM((2, new, dec_width), BF16),
            VMEM((total, dec_width), BF16),
            VMEM((2, bytes_, dec_width), BF16),
            VMEM((2 * bytes_, dec_width), BF16),
            VMEM((2, 1, bytes_), jnp.int32),
            VMEM((2, 1, bytes_), jnp.int32),
            VMEM((half, bytes_), BF16),
            VMEM((dec_width, bytes_), BF16),
            VMEM((peers, bytes_, out_width), BF16),
            VMEM((peers, bytes_, out_width), BF16),
            pltpu.SemaphoreType.DMA((copies,)),
            pltpu.SemaphoreType.DMA((copies,)),
            pltpu.SemaphoreType.DMA((24,)),
        ],
        compiler_params=pltpu.CompilerParams(
            collective_id=0, has_side_effects=True, vmem_limit_bytes=60 * 2**20
        ),
        name="solve",
    )(
        queries,
        new_keys,
        new_values,
        cache_keys,
        cache_values,
        held,
        patch_hidden,
        flat_weight,
        dec_kv_weight,
        norm_gain.reshape(1, kv_rows),
        key_gain.reshape(1, half),
        query_gain.reshape(1, half),
        dec_query_weight,
        dec_out_weight,
        byte_states,
        byte_patch.reshape(1, bytes_),
        mates,
    )
    return pl.pallas_call(
        hand_over,
        out_shape=tuple(jax.ShapeDtypeStruct(r.shape, r.dtype) for r in results),
        in_specs=[in_place()] * 2,
        out_specs=(in_place(),) * 2,
        scratch_shapes=[pltpu.SemaphoreType.DMA((2,))],
        compiler_params=pltpu.CompilerParams(vmem_limit_bytes=60 * 2**20),
        name="hand_over",
    )(*results)


def solution(mesh):
    placed = (
        P("ctx", "head"),
        P("ctx", "head", None),
        P("ctx", "head", None),
        P("ctx", "head", None),
        P("ctx", "head", None),
        P("ctx", "head", None),
        P("ctx"),
        P(),
        P("head", None, None),
        P(),
        P(None, None, "head"),
        P(None, "head"),
        P(),
        P(),
        P("head", None),
        P("ctx", None),
        P("ctx"),
    )
    return jax.shard_map(
        functools.partial(per_device, mesh.shape["ctx"] // 4, mesh.shape["head"]),
        mesh=mesh,
        in_specs=placed,
        out_specs=(P("ctx", "head"), P("ctx", "head")),
        check_vma=False,
    )
```

```python
import functools

import jax
import jax.numpy as jnp
from jax import lax
from jax.experimental import pallas as pl
from jax.experimental.pallas import tpu as pltpu
from jax.sharding import PartitionSpec as P

MESH = pl.DeviceIdType.MESH
VMEM = pltpu.VMEM
F32 = jnp.float32
BF16 = jnp.bfloat16
HIDE = -1e30
LIFT = 2048.0
LOG2E = 1.4426950408889634


def in_vmem():
    return pl.BlockSpec(memory_space=pltpu.VMEM)


def in_place():
    return pl.BlockSpec(memory_space=pltpu.HBM)


class Place:
    def __init__(self, zn):
        c = lax.axis_index("ctx")
        self.c = c
        self.zn = zn
        self.z = lax.div(c, 4)
        self.yl = lax.rem(lax.div(c, 2), 2)
        self.k = lax.rem(c, 2)
        self.cores = (self.k, 1 - self.k)

    def around(self, step):
        return lax.rem(self.z + (step + 2 * self.zn), self.zn)

    def device(self, step, other_y, other_core):
        y = 1 - self.yl if other_y else self.yl
        return {"ctx": self.around(step) * 4 + y * 2 + self.cores[other_core]}

    def near(self, steps):
        found = [self.device(0, False, True)]
        for core in (False, True):
            found.append(self.device(0, True, core))
            found += [self.device(step, False, core) for step in steps]
        return found


class Copy:
    def __init__(self, dma):
        self.dma, self.got = dma, False

    def start(self):
        self.dma.start()
        return self

    def receive(self):
        if not self.got:
            self.dma.wait_recv()
        self.got = True


class Sends:
    def __init__(self, send_sem, recv_sem):
        self.send_sem, self.recv_sem, self.made = send_sem, recv_sem, []

    def make(self, src, dst, device):
        at = len(self.made)
        copy = Copy(
            pltpu.make_async_remote_copy(
                src_ref=src,
                dst_ref=dst,
                send_sem=self.send_sem.at[at],
                recv_sem=self.recv_sem.at[at],
                device_id=device,
                device_id_type=MESH,
            )
        )
        self.made.append(copy)
        return copy.start()

    def close(self):
        for copy in self.made:
            copy.receive()
        for copy in self.made:
            copy.dma.wait_send()


class Loads:
    def __init__(self, sem):
        self.sem, self.used = sem, 0

    def start(self, src, dst):
        copy = pltpu.make_async_copy(src, dst, self.sem.at[self.used])
        self.used += 1
        copy.start()
        return copy


def greet(devices, meanwhile):
    barrier = pltpu.get_barrier_semaphore()
    for device in devices:
        pl.semaphore_signal(barrier, inc=1, device_id=device, device_id_type=MESH)
    meanwhile()
    pl.semaphore_wait(barrier, len(devices))


def aligned(start, size):
    return pl.ds(pl.multiple_of(start, size), size)


def first_hop(sends, place, source, buffer, step, other_y, cores):
    rows = source.shape[1]
    mine = buffer.at[aligned(place.c * rows, rows), :]
    return [sends.make(source.at[place.cores[core]], mine, place.device(step, other_y, core)) for core in cores]


def direct_steps(zn):
    if zn == 8:
        return (2, -2, 1, -1)
    return tuple(way * n for n in range(1, zn // 2 + 1) for way in (1, -1) if 2 * n < zn or way > 0)


def stride_gather(sends, place, source, buffer, idle, work):
    zn, rows = place.zn, source.shape[1]
    far = zn // 2
    arriving = [[] for _ in range(far + 1)]

    def first(step, other_y, cores):
        return first_hop(sends, place, source, buffer, step, other_y, cores)

    def piece(step, y):
        return buffer.at[aligned((place.around(step) * 2 + y) * 2 * rows, 2 * rows), :]

    steps = direct_steps(zn)
    from_y = first(0, True, (0, 1))
    found = {(0, step): first(step, False, (0, 1)) for step in steps}
    arriving[0] += first(0, False, (1,))
    buffer[aligned(place.c * rows, rows), :] = source[place.k]
    idle()
    for copy in from_y:
        copy.receive()
    theirs = piece(0, 1 - place.yl)
    for step in steps:
        found[1, step] = [sends.make(theirs, theirs, place.device(step, False, 0))]
    for (_, step), copies in found.items():
        arriving[abs(step)] += copies

    def relay(stream):
        for way in (1, -1):
            for copy in found[stream, 2 * way]:
                copy.receive()
            passed = piece(-2 * way, 1 - place.yl if stream else place.yl)
            arriving[3].append(sends.make(passed, passed, place.device(way, False, 0)))
            if (way == 1) == (stream == 0):
                arriving[4].append(sends.make(passed, passed, place.device(2 * way, False, 0)))

    if zn == 8:
        relay(0)
    for n in range(far + 1):
        if n == 1 and zn == 8:
            relay(1)
        for copy in arriving[n]:
            copy.receive()
        work(n)


def pack(ref, out, top, total):
    dim = out.shape[0]
    ref[0:dim, :] = out.astype(BF16)
    coarse = total.astype(BF16).astype(F32)
    row = lax.broadcasted_iota(jnp.int32, (16, out.shape[1]), 0)
    tail = jnp.where(row == 0, top, jnp.where(row == 1, coarse, jnp.where(row == 2, total - coarse, 0.0)))
    ref[dim : dim + 16, :] = tail.astype(BF16)


def unpack(ref):
    value = ref[...]
    dim = value.shape[0] - 16
    tail = value[dim:, :].astype(F32)
    return value[:dim, :].astype(F32), tail[0:1, :], tail[1:2, :] + tail[2:3, :]


def merged(parts):
    top = parts[0][1]
    for part in parts[1:]:
        top = jnp.maximum(top, part[1])
    out, total = 0.0, 0.0
    for o, m, l in parts:
        factor = jnp.exp2(m - top)
        out = out + o * factor
        total = total + l * factor
    return out, top, total


def head_norm(values, gain, half):
    lane = lax.broadcasted_iota(jnp.int32, values.shape, 1)
    first = lane < half
    squares = values * values
    s0 = jnp.sum(jnp.where(first, squares, 0.0), axis=1, keepdims=True)
    s1 = jnp.sum(jnp.where(first, 0.0, squares), axis=1, keepdims=True)
    return values * lax.rsqrt(jnp.where(first, s0, s1) / half + 1e-6) * gain


def solve(
    zn, hn, q_hbm, nk_hbm, nv_hbm, ck_hbm, cv_hbm, cr_hbm,
    hidden_hbm, w_hbm, dkv_hbm, gain_hbm, kgain_hbm, qgain_hbm, dqw_hbm, dow_hbm, states_hbm, bp_hbm, nr_hbm,
    patch_out, byte_out,
    q_in, new_in, old_in, held, q_half, kv_half, qg, kc, vc, key_mark, query_mark, part,
    hidden, w_ref, dkv_in, dkv, gain_ref, kgain, qgain, dqw_ref, dow_ref, states_ref, nr,
    ring_in, ring_out, last, last_in, att, rs_out, rs_in, ag_in, kv_tile, kvg, bq_tile, bq,
    bp_both, span, mix_tile, mix, bs_out, bs_in, send_sem, recv_sem, local_sem,
):
    place = Place(zn)
    sends, loads = Sends(send_sem, recv_sem), Loads(local_sem)
    k, z, yl = place.k, place.z, place.yl
    me = lax.axis_index("head")
    peer = place.device(0, False, True)
    x, yh = lax.div(me, 2), lax.rem(me, 2)
    xn = hn // 2
    ways = [(dx, dy) for dy in (1, 0) for dx in sorted(range(xn), key=lambda n: -min(n, xn - n)) if dx or dy]

    def head_at(dx, dy):
        return lax.rem(x + dx + xn, xn) * 2 + (1 - yh if dy else yh)

    others = [head_at(dx, dy) for dx, dy in ways]
    sources = [me] + [head_at(-dx, dy) for dx, dy in ways]
    q_load = loads.start(q_hbm, q_in)
    kv_loads = [
        (loads.start(ck_hbm, old_in.at[0]), loads.start(nk_hbm, new_in.at[0])),
        (loads.start(cv_hbm, old_in.at[1]), loads.start(nv_hbm, new_in.at[1])),
    ]
    small = [loads.start(cr_hbm, held.at[k]), loads.start(nr_hbm, nr)]
    for_queries = [
        loads.start(a, b)
        for a, b in ((states_hbm, states_ref), (dqw_hbm, dqw_ref), (qgain_hbm, qgain), (bp_hbm, bp_both.at[k]))
    ]
    dkv_load = loads.start(dkv_hbm, dkv_in)
    w_loads = [loads.start(w_hbm, w_ref), loads.start(hidden_hbm, hidden)]
    late = [
        loads.start(a, b)
        for a, b in ((gain_hbm, gain_ref), (kgain_hbm, kgain), (dow_hbm, dow_ref))
    ]
    new, slice_width = hidden.shape
    heads = part.shape[1]
    dim = part.shape[3] - 16
    bytes_, half = states_ref.shape[0], kgain.shape[1]
    cached = ck_hbm.shape[0]
    width = q_half.shape[2]
    chip = z * 2 + yl
    tile = 4 * new
    chip_first = chip * 2 * new
    scale = dim ** (-0.5) * LOG2E

    kept, swaps = [], []

    def flatten():
        q_load.wait()
        flat = (q_in[...].reshape(new, 2 * width).astype(F32) * scale).astype(BF16)
        q_half[0] = flat[:, :width]
        q_half[1] = flat[:, width:]
        for which in (0, 1):
            for copy in kv_loads[which]:
                copy.wait()
            for value, count, at in ((old_in[which], cached, 0), (new_in[which], new, cached)):
                flat = value.reshape(count, 2 * width)
                rows = pl.ds(at, count)
                kv_half[which, 0, rows, :] = flat[:, :width]
                kv_half[which, 1, rows, :] = flat[:, width:]

    greet(place.near(direct_steps(zn)) + [{"head": d} for d in others], flatten)

    def swap(which, out):
        for count, at, to in ((cached, 0, k * cached), (new, cached, 2 * cached + k * new)):
            rows = pl.ds(at, count)
            target = out.at[aligned(to, count), :]
            swaps.append(sends.make(kv_half.at[which, 1 - k, rows, :], target, peer))
            kept.append(loads.start(kv_half.at[which, k, rows, :], target))

    def marks(at, cuts):
        lane = lax.broadcasted_iota(jnp.int32, (1, query_mark.shape[1]), 1)
        low, high = jnp.zeros(lane.shape, F32), jnp.zeros(lane.shape, F32)
        for r in range(8):
            low = jnp.where(lane == r, cuts[r], low)
            high = jnp.where(lane == r, cuts[r + 1], high)
        return jnp.where((at >= low) & (at < high), 1.0, 0.0)

    def positions(count, first):
        return (lax.broadcasted_iota(jnp.int32, (count, query_mark.shape[1]), 0) + first).astype(F32)

    def early():
        for copy in small:
            copy.wait()
        held_swap = sends.make(held.at[k], held.at[k], peer)
        swap(0, kc)
        cuts = [
            jnp.sum(jnp.where(nr[...] < r, 1.0, 0.0), axis=1, keepdims=True) for r in range(9)
        ]
        query_mark[...] = marks(positions(query_mark.shape[0], 0), cuts).astype(BF16)
        key_mark[2 * cached :, :] = (LIFT * marks(positions(2 * new, chip_first), cuts)).astype(BF16)
        swap(1, vc)
        held_swap.receive()
        both = held[...]
        cuts = [
            jnp.sum(jnp.sum(jnp.where(both < r, 1.0, 0.0), axis=0), axis=(0, 1), keepdims=True)
            for r in range(9)
        ]
        key_mark[: 2 * cached, :] = (LIFT * marks(positions(2 * cached, 0), cuts)).astype(BF16)

    def attend(t):
        q0 = pl.multiple_of(t * tile, tile)
        rows = pl.ds(q0, tile)
        columns = [slice(h * dim, (h + 1) * dim) for h in range(heads)]
        scores = []
        for cols in columns:
            found = lax.dot_general(
                jnp.concatenate([kc[:, cols], key_mark[...]], axis=1),
                jnp.concatenate([qg[rows, cols], query_mark[rows, :]], axis=1),
                (((1,), (1,)), ((), ())),
                preferred_element_type=F32,
            )
            late = found[2 * cached :]
            at = lax.broadcasted_iota(jnp.int32, late.shape, 0) + chip_first
            asked = lax.broadcasted_iota(jnp.int32, late.shape, 1) + q0
            late = jnp.where(at <= asked, late, HIDE)
            scores.append(jnp.concatenate([found[: 2 * cached], late], axis=0))
        weights = []
        for found in scores:
            top = jnp.max(found, axis=0, keepdims=True) - LIFT
            top = top.astype(BF16).astype(F32)
            weights.append((top, jnp.exp2(found - (top + LIFT))))
        for h, (top, found) in enumerate(weights):
            total = jnp.sum(found, axis=0, keepdims=True)
            out = lax.dot_general(
                vc[:, columns[h]], found.astype(BF16), (((0,), (0,)), ((), ())), preferred_element_type=F32
            )
            for y in (0, 1):
                cols = slice(y * 2 * new, (y + 1) * 2 * new)
                pack(part.at[t, h, y], out[:, cols], top[:, cols], total[:, cols])

    far, near = zn // 2, zn - 1 - zn // 2
    chains = [(h, y) for h in range(heads) for y in (0, 1)]
    counts = {(h, y): (far, near) if h % 2 == 0 else (near, far) for h, y in chains}
    made = {}

    def reduce_step(step, chosen):
        for chain in chains:
            for way in (0, 1):
                count = counts[chain][way]
                if step >= count or count not in chosen:
                    continue
                sign = 1 - 2 * way
                target = place.around(sign * (count - step))
                if step == 0:
                    src = part.at[target, *chain]
                else:
                    made[chain, way, step - 1].receive()
                    src = ring_out.at[*chain, way, step]
                    pack(src, *merged([unpack(part.at[target, *chain]), unpack(ring_in.at[*chain, way, step - 1])]))
                made[chain, way, step] = sends.make(
                    src, ring_in.at[*chain, way, step], place.device(sign, False, 0)
                )

    def work(turn):
        if turn == 0:
            for copy in kept:
                copy.wait()
            for copy in swaps:
                copy.receive()
        if turn == far:
            reduce_step(0, (near,))

        def one(i, carry):
            attend(lax.rem(z + (1 - 2 * i) * turn + 2 * zn, zn))
            return carry

        lax.fori_loop(0, 1 if turn in (0, far) else 2, one, 0)
        if turn == far:
            reduce_step(0, (far,))

    stride_gather(sends, place, q_half, qg, early, work)

    swapped = []

    def byte_queries():
        for copy in for_queries:
            copy.wait()
        proj = jnp.dot(states_ref[...], dqw_ref[...], preferred_element_type=F32)
        gain = jnp.concatenate([qgain[...], qgain[...]], axis=1)
        normed = head_norm(proj, gain, half)
        lane = lax.broadcasted_iota(jnp.int32, normed.shape, 1)
        bq_tile[0] = jnp.where(lane < half, normed, 0.0).astype(BF16)
        bq_tile[1] = jnp.where(lane < half, pltpu.roll(normed, half, 1), 0.0).astype(BF16)
        rows = aligned(k * bytes_, bytes_)
        swapped.append(sends.make(bp_both.at[k], bp_both.at[k], peer))
        sends.make(bq_tile.at[1 - k], bq.at[rows, :], peer)
        bq[rows, :] = bq_tile[k]

    def flat_weights():
        dkv_load.wait()
        count = dkv.shape[0] // 4
        for i in range(4):
            rows = slice(i * count, (i + 1) * count)
            dkv[rows, :] = dkv_in[rows].reshape(count, dkv.shape[1])

    idle = [byte_queries, flat_weights]
    for step in range(max(far, 1)):
        if step:
            reduce_step(step, (far, near))
        if step < len(idle):
            idle[step]()
    for work_left in idle[max(far, 1) :]:
        work_left()
    summed = {}
    for chain in chains:
        got = [unpack(part.at[z, *chain])]
        for way in (0, 1):
            count = counts[chain][way]
            if count:
                made[chain, way, count - 1].receive()
                got.append(unpack(ring_in.at[*chain, way, count - 1]))
        summed[chain] = merged(got)
    for y in (0, 1):
        for core in (0, 1):
            joined = []
            for a, b in zip(summed[0, y], summed[1, y]):
                lane = lax.broadcasted_iota(jnp.int32, a.shape, 1)
                if core == 0:
                    joined.append(jnp.where(lane < new, a, pltpu.roll(b, new, 1)))
                else:
                    joined.append(jnp.where(lane < new, pltpu.roll(a, new, 1), b))
            pack(last.at[y, core], *joined)
    across = sends.make(last.at[1 - yl, k], last_in.at[0], place.device(0, True, False))
    beside = sends.make(last.at[yl, 1 - k], last_in.at[1], peer)
    diagonal = sends.make(last.at[1 - yl, 1 - k], last_in.at[2], place.device(0, True, True))
    for pair, parts, waits in (
        (k, (last.at[yl, k], last_in.at[0]), (across,)),
        (1 - k, (last_in.at[1], last_in.at[2]), (beside, diagonal)),
    ):
        for copy in waits:
            copy.receive()
        out, _, total = merged([unpack(ref) for ref in parts])
        turned = (out / total).T.astype(BF16)
        both = jnp.concatenate([turned[:new], turned[new:]], axis=1)
        att[:, aligned(pair * 2 * dim, 2 * dim)] = both

    for copy in w_loads:
        copy.wait()
    mine = att[...]

    def columns_for(d):
        return jnp.dot(mine, w_ref[:, aligned(d * slice_width, slice_width)], preferred_element_type=F32)

    rs_sends = []
    for i, d in enumerate(others):
        rs_out[i] = columns_for(d).astype(BF16)
        rs_sends.append(sends.make(rs_out.at[i], rs_in.at[i], {"head": d}))
    own = columns_for(me) + hidden[...].astype(F32)
    for i, copy in enumerate(rs_sends):
        copy.receive()
        own = own + rs_in[i].astype(F32)
    rounded = own.astype(BF16)
    ag_in[0] = rounded
    ag_sends = [sends.make(ag_in.at[0], ag_in.at[1 + i], {"head": d}) for i, d in enumerate(others)]
    patch_out[...] = rounded
    for copy in late:
        copy.wait()
    squares, proj = 0.0, 0.0
    for i, source in enumerate(sources):
        if i:
            ag_sends[i - 1].receive()
        wide = ag_in[i].astype(F32)
        squares = squares + jnp.sum(wide * wide, axis=1, keepdims=True)
        scaled = (wide * gain_ref[:, aligned(source * slice_width, slice_width)]).astype(BF16)
        rows = aligned(source * slice_width, slice_width)
        proj = proj + jnp.dot(scaled, dkv[rows, :], preferred_element_type=F32)
    proj = proj * lax.rsqrt(squares / (hn * slice_width) + 1e-5)
    keys = head_norm(proj[:, : 2 * half], jnp.concatenate([kgain[...], kgain[...]], axis=1), half)
    values = proj[:, 2 * half :]
    lane = lax.broadcasted_iota(jnp.int32, keys.shape, 1)
    kv_tile[0] = jnp.where(lane < half, keys, pltpu.roll(values, half, 1)).astype(BF16)
    kv_tile[1] = jnp.where(lane < half, pltpu.roll(keys, half, 1), values).astype(BF16)

    def byte_spans():
        swapped[0].receive()
        owners = bp_both[...]
        first = jnp.zeros(owners.shape, F32)
        mates = nr[...]
        for r in range(1, 8):
            begins = jnp.sum(jnp.where(mates < r, 1.0, 0.0), axis=1, keepdims=True)[None]
            first = jnp.where(owners.astype(F32) >= begins, begins, first)
        span[...] = first.astype(jnp.int32)

    stride_gather(sends, place, kv_tile, kvg, byte_spans, lambda n: None)
    for copy in sends.made:
        copy.receive()
    spans = (span, bp_both)

    block = min(512, kvg.shape[0])
    byte_scale = half ** (-0.5) * LOG2E

    def byte_attention(core):
        queries = bq[aligned(core * bytes_, bytes_), :]
        first, owner = spans[0][core], spans[1][core]
        out, total = 0.0, 0.0
        for b in range(kvg.shape[0] // block):
            kv = kvg[b * block : (b + 1) * block, :]
            scores = lax.dot_general(kv, queries, (((1,), (1,)), ((), ())), preferred_element_type=F32)
            at = lax.broadcasted_iota(jnp.int32, scores.shape, 0) + b * block
            weights = jnp.where((at >= first) & (at <= owner), jnp.exp2(scores * byte_scale), 0.0)
            total = total + jnp.sum(weights, axis=0, keepdims=True)
            out = out + lax.dot_general(
                kv, weights.astype(BF16), (((0,), (0,)), ((), ())), preferred_element_type=F32
            )
        return (out[half:, :] / total).astype(BF16)

    mix_rows = aligned(k * half, half)
    mix_tile[...] = byte_attention(1 - k)
    mix_send = sends.make(mix_tile, mix.at[mix_rows, :], peer)
    mix[mix_rows, :] = byte_attention(k)
    mix_send.receive()
    mixed = mix[...]
    out_width = byte_out.shape[1]

    def byte_columns_for(d):
        cols = aligned(d * out_width, out_width)
        return lax.dot_general(mixed, dow_ref[:, cols], (((0,), (0,)), ((), ())), preferred_element_type=F32)

    bs_sends = []
    for i, d in enumerate(others):
        bs_out[i] = byte_columns_for(d).astype(BF16)
        bs_sends.append(sends.make(bs_out.at[i], bs_in.at[i], {"head": d}))
    own = byte_columns_for(me) + states_ref[:, aligned(me * out_width, out_width)].astype(F32)
    for i, copy in enumerate(bs_sends):
        copy.receive()
        own = own + bs_in[i].astype(F32)
    byte_out[...] = own.astype(BF16)
    sends.close()


def hand_over(a, b, a_out, b_out, a_held, b_held, sem):
    loads = Loads(sem)
    for copy in (loads.start(a, a_held), loads.start(b, b_held)):
        copy.wait()
    for copy in (loads.start(a_held, a_out), loads.start(b_held, b_out)):
        copy.wait()


def per_device(
    zn,
    hn,
    patch_hidden,
    queries,
    new_keys,
    new_values,
    cache_keys,
    cache_values,
    cache_request,
    new_request,
    out_weight,
    norm_gain,
    dec_kv_weight,
    dec_query_weight,
    query_gain,
    key_gain,
    dec_out_weight,
    byte_states,
    byte_patch,
):
    new, heads, dim = queries.shape
    cached = cache_keys.shape[0]
    total = new_request.shape[0]
    pair = heads // 2 * dim
    all_keys = 2 * (cached + new)
    slice_width = patch_hidden.shape[1]
    held = cache_request.reshape(8, cached // 8)
    mates = new_request.reshape(1, total)
    tile = 4 * new
    kv_rows = dec_kv_weight.shape[0]
    dec_width = dec_kv_weight.shape[2]
    bytes_ = byte_states.shape[0]
    out_width = dec_out_weight.shape[1] // hn
    half = dec_width // 2
    steps = max(zn // 2, 1)
    peers = max(hn - 1, 1)
    copies = 5 + 7 + 4 * zn + 2 + 4 * (zn - 1) + 3 + 3 * (hn - 1) + 3 + 4 * zn + 1
    flat_weight = out_weight.reshape(heads * dim, -1)
    results = pl.pallas_call(
        functools.partial(solve, zn, hn),
        out_shape=(
            jax.ShapeDtypeStruct(patch_hidden.shape, BF16),
            jax.ShapeDtypeStruct((bytes_, out_width), BF16),
        ),
        in_specs=[in_place()] * 17,
        out_specs=(in_vmem(), in_vmem()),
        scratch_shapes=[
            VMEM(queries.shape, BF16),
            VMEM((2, *new_keys.shape), BF16),
            VMEM((2, *cache_keys.shape), BF16),
            VMEM((2, *held.shape), jnp.int32),
            VMEM((2, new, pair), BF16),
            VMEM((2, 2, cached + new, pair), BF16),
            VMEM((total, pair), BF16),
            VMEM((all_keys, pair), BF16),
            VMEM((all_keys, pair), BF16),
            VMEM((all_keys, 128), BF16),
            VMEM((total, 128), BF16),
            VMEM((zn, heads // 2, 2, dim + 16, 2 * new), BF16),
            VMEM(patch_hidden.shape, BF16),
            VMEM(flat_weight.shape, BF16),
            VMEM(dec_kv_weight.shape, BF16),
            VMEM((kv_rows, 2 * dec_width), BF16),
            VMEM((1, kv_rows), F32),
            VMEM((1, half), F32),
            VMEM((1, half), F32),
            VMEM(dec_query_weight.shape, BF16),
            VMEM(dec_out_weight.shape, BF16),
            VMEM(byte_states.shape, BF16),
            VMEM((1, total), jnp.int32),
            VMEM((heads // 2, 2, 2, steps, dim + 16, 2 * new), BF16),
            VMEM((heads // 2, 2, 2, steps, dim + 16, 2 * new), BF16),
            VMEM((2, 2, dim + 16, 2 * new), BF16),
            VMEM((3, dim + 16, 2 * new), BF16),
            VMEM((new, heads * dim), BF16),
            VMEM((peers, new, slice_width), BF16),
            VMEM((peers, new, slice_width), BF16),
            VMEM((hn, new, slice_width), BF16),
            VMEM((2, new, dec_width), BF16),
            VMEM((total, dec_width), BF16),
            VMEM((2, bytes_, dec_width), BF16),
            VMEM((2 * bytes_, dec_width), BF16),
            VMEM((2, 1, bytes_), jnp.int32),
            VMEM((2, 1, bytes_), jnp.int32),
            VMEM((half, bytes_), BF16),
            VMEM((dec_width, bytes_), BF16),
            VMEM((peers, bytes_, out_width), BF16),
            VMEM((peers, bytes_, out_width), BF16),
            pltpu.SemaphoreType.DMA((copies,)),
            pltpu.SemaphoreType.DMA((copies,)),
            pltpu.SemaphoreType.DMA((24,)),
        ],
        compiler_params=pltpu.CompilerParams(
            collective_id=0, has_side_effects=True, vmem_limit_bytes=60 * 2**20
        ),
        name="solve",
    )(
        queries,
        new_keys,
        new_values,
        cache_keys,
        cache_values,
        held,
        patch_hidden,
        flat_weight,
        dec_kv_weight,
        norm_gain.reshape(1, kv_rows),
        key_gain.reshape(1, half),
        query_gain.reshape(1, half),
        dec_query_weight,
        dec_out_weight,
        byte_states,
        byte_patch.reshape(1, bytes_),
        mates,
    )
    return pl.pallas_call(
        hand_over,
        out_shape=tuple(jax.ShapeDtypeStruct(r.shape, r.dtype) for r in results),
        in_specs=[in_place()] * 2,
        out_specs=(in_place(),) * 2,
        scratch_shapes=[VMEM(r.shape, r.dtype) for r in results] + [pltpu.SemaphoreType.DMA((4,))],
        compiler_params=pltpu.CompilerParams(vmem_limit_bytes=60 * 2**20),
        name="hand_over",
    )(*results)


def solution(mesh):
    placed = (
        P("ctx", "head"),
        P("ctx", "head", None),
        P("ctx", "head", None),
        P("ctx", "head", None),
        P("ctx", "head", None),
        P("ctx", "head", None),
        P("ctx"),
        P(),
        P("head", None, None),
        P(),
        P(None, None, "head"),
        P(None, "head"),
        P(),
        P(),
        P("head", None),
        P("ctx", None),
        P("ctx"),
    )
    return jax.shard_map(
        functools.partial(per_device, mesh.shape["ctx"] // 4, mesh.shape["head"]),
        mesh=mesh,
        in_specs=placed,
        out_specs=(P("ctx", "head"), P("ctx", "head")),
        check_vma=False,
    )
```

```python
import functools

import jax
import jax.numpy as jnp
from jax import lax
from jax.experimental import pallas as pl
from jax.experimental.pallas import tpu as pltpu
from jax.sharding import PartitionSpec as P

MESH = pl.DeviceIdType.MESH
VMEM = pltpu.VMEM
F32 = jnp.float32
BF16 = jnp.bfloat16
HIDE = -1e30
LIFT = 2048.0
LOG2E = 1.4426950408889634


def in_vmem():
    return pl.BlockSpec(memory_space=pltpu.VMEM)


def in_place():
    return pl.BlockSpec(memory_space=pltpu.HBM)


class Place:
    def __init__(self, zn):
        c = lax.axis_index("ctx")
        self.c = c
        self.zn = zn
        self.z = lax.div(c, 4)
        self.yl = lax.rem(lax.div(c, 2), 2)
        self.k = lax.rem(c, 2)
        self.cores = (self.k, 1 - self.k)

    def around(self, step):
        return lax.rem(self.z + (step + 2 * self.zn), self.zn)

    def device(self, step, other_y, other_core):
        y = 1 - self.yl if other_y else self.yl
        return {"ctx": self.around(step) * 4 + y * 2 + self.cores[other_core]}

    def near(self, steps):
        found = [self.device(0, False, True)]
        for core in (False, True):
            found += [self.device(step, True, core) for step in (0, 1, -1)]
            found += [self.device(step, False, core) for step in steps]
        return found


class Copy:
    def __init__(self, dma):
        self.dma, self.got = dma, False

    def start(self):
        self.dma.start()
        return self

    def receive(self):
        if not self.got:
            self.dma.wait_recv()
        self.got = True


class Sends:
    def __init__(self, send_sem, recv_sem):
        self.send_sem, self.recv_sem, self.made = send_sem, recv_sem, []

    def make(self, src, dst, device):
        at = len(self.made)
        copy = Copy(
            pltpu.make_async_remote_copy(
                src_ref=src,
                dst_ref=dst,
                send_sem=self.send_sem.at[at],
                recv_sem=self.recv_sem.at[at],
                device_id=device,
                device_id_type=MESH,
            )
        )
        self.made.append(copy)
        return copy.start()

    def close(self):
        for copy in self.made:
            copy.receive()
        for copy in self.made:
            copy.dma.wait_send()


class Loads:
    def __init__(self, sem):
        self.sem, self.used = sem, 0

    def start(self, src, dst):
        copy = pltpu.make_async_copy(src, dst, self.sem.at[self.used])
        self.used += 1
        copy.start()
        return copy


def greet(devices, meanwhile):
    barrier = pltpu.get_barrier_semaphore()
    for device in devices:
        pl.semaphore_signal(barrier, inc=1, device_id=device, device_id_type=MESH)
    meanwhile()
    pl.semaphore_wait(barrier, len(devices))


def aligned(start, size):
    return pl.ds(pl.multiple_of(start, size), size)


def first_hop(sends, place, source, buffer, step, other_y, cores):
    rows = source.shape[1]
    mine = buffer.at[aligned(place.c * rows, rows), :]
    return [sends.make(source.at[place.cores[core]], mine, place.device(step, other_y, core)) for core in cores]


def direct_steps(zn):
    if zn == 8:
        return (2, -2, 1, -1)
    return tuple(way * n for n in range(1, zn // 2 + 1) for way in (1, -1) if 2 * n < zn or way > 0)


def stride_gather(sends, place, source, buffer, idle, work):
    zn, rows = place.zn, source.shape[1]
    far = zn // 2
    arriving = [[] for _ in range(far + 1)]

    def first(step, other_y, cores):
        return first_hop(sends, place, source, buffer, step, other_y, cores)

    def piece(step, y):
        return buffer.at[aligned((place.around(step) * 2 + y) * 2 * rows, 2 * rows), :]

    steps = direct_steps(zn)
    from_y = first(0, True, (0, 1))
    found = {(0, step): first(step, False, (0, 1)) for step in steps}
    arriving[0] += first(0, False, (1,))
    buffer[aligned(place.c * rows, rows), :] = source[place.k]
    idle()
    for copy in from_y:
        copy.receive()
    theirs = piece(0, 1 - place.yl)
    for step in steps:
        found[1, step] = [sends.make(theirs, theirs, place.device(step, False, 0))]
    for (_, step), copies in found.items():
        arriving[abs(step)] += copies

    def relay(stream):
        for way in (1, -1):
            for copy in found[stream, 2 * way]:
                copy.receive()
            passed = piece(-2 * way, 1 - place.yl if stream else place.yl)
            arriving[3].append(sends.make(passed, passed, place.device(way, False, 0)))
            if (way == 1) == (stream == 0):
                arriving[4].append(sends.make(passed, passed, place.device(2 * way, False, 0)))

    if zn == 8:
        relay(0)
    for n in range(far + 1):
        if n == 1 and zn == 8:
            relay(1)
        for copy in arriving[n]:
            copy.receive()
        work(n)


def cross_gather(sends, place, source, buffer, idle, work):
    rows = source.shape[1]
    arriving = [[] for _ in range(5)]

    def first(step, other_y, cores=(0, 1)):
        return first_hop(sends, place, source, buffer, step, other_y, cores)

    def piece(step):
        return buffer.at[aligned((place.around(step) * 2 + place.yl) * 2 * rows, 2 * rows), :]

    def across(step):
        passed = piece(step)
        return sends.make(passed, passed, place.device(0, True, False))

    found = {step: first(step, False) for step in (2, -2)}
    arriving[0] += first(0, True) + first(0, False, (1,))
    for step in (1, -1):
        arriving[1] += first(step, False) + first(step, True)
    buffer[aligned(place.c * rows, rows), :] = source[place.k]
    idle()
    relayed = {}
    for way in (1, -1):
        for copy in found[2 * way]:
            copy.receive()
        passed = piece(-2 * way)
        relayed[way] = sends.make(passed, passed, place.device(way, False, 0))
    side = 1 - 2 * place.k
    passed = piece(-2 * side)
    opposite = sends.make(passed, passed, place.device(2 * side, False, 0))
    arriving[2] += [across(-2), across(2)]
    for n in range(5):
        if n == 2:
            for way in (1, -1):
                relayed[way].receive()
                arriving[3].append(across(-3 * way))
            opposite.receive()
            arriving[4].append(across(4))
        for copy in arriving[n]:
            copy.receive()
        work(n)


def pack(ref, out, top, total):
    dim = out.shape[0]
    ref[0:dim, :] = out.astype(BF16)
    coarse = total.astype(BF16).astype(F32)
    row = lax.broadcasted_iota(jnp.int32, (16, out.shape[1]), 0)
    tail = jnp.where(row == 0, top, jnp.where(row == 1, coarse, jnp.where(row == 2, total - coarse, 0.0)))
    ref[dim : dim + 16, :] = tail.astype(BF16)


def unpack(ref):
    value = ref[...]
    dim = value.shape[0] - 16
    tail = value[dim:, :].astype(F32)
    return value[:dim, :].astype(F32), tail[0:1, :], tail[1:2, :] + tail[2:3, :]


def merged(parts):
    top = parts[0][1]
    for part in parts[1:]:
        top = jnp.maximum(top, part[1])
    out, total = 0.0, 0.0
    for o, m, l in parts:
        factor = jnp.exp2(m - top)
        out = out + o * factor
        total = total + l * factor
    return out, top, total


def head_norm(values, gain, half):
    lane = lax.broadcasted_iota(jnp.int32, values.shape, 1)
    first = lane < half
    squares = values * values
    s0 = jnp.sum(jnp.where(first, squares, 0.0), axis=1, keepdims=True)
    s1 = jnp.sum(jnp.where(first, 0.0, squares), axis=1, keepdims=True)
    return values * lax.rsqrt(jnp.where(first, s0, s1) / half + 1e-6) * gain


def solve(
    zn, hn, q_hbm, nk_hbm, nv_hbm, ck_hbm, cv_hbm, cr_hbm,
    hidden_hbm, w_hbm, dkv_hbm, gain_hbm, kgain_hbm, qgain_hbm, dqw_hbm, dow_hbm, states_hbm, bp_hbm, nr_hbm,
    patch_out, byte_out,
    q_in, new_in, old_in, held, q_half, kv_half, qg, kc, vc, key_mark, query_mark, part,
    hidden, w_ref, dkv_in, dkv, gain_ref, kgain, qgain, dqw_ref, dow_ref, states_ref, nr,
    ring_in, ring_out, last, last_in, att, rs_out, rs_in, ag_in, kv_tile, kvg, bq_tile, bq,
    bp_both, span, mix_tile, mix, bs_out, bs_in, send_sem, recv_sem, local_sem,
):
    place = Place(zn)
    sends, loads = Sends(send_sem, recv_sem), Loads(local_sem)
    k, z, yl = place.k, place.z, place.yl
    me = lax.axis_index("head")
    peer = place.device(0, False, True)
    x, yh = lax.div(me, 2), lax.rem(me, 2)
    xn = hn // 2
    ways = [(dx, dy) for dy in (1, 0) for dx in sorted(range(xn), key=lambda n: -min(n, xn - n)) if dx or dy]

    def head_at(dx, dy):
        return lax.rem(x + dx + xn, xn) * 2 + (1 - yh if dy else yh)

    others = [head_at(dx, dy) for dx, dy in ways]
    sources = [me] + [head_at(-dx, dy) for dx, dy in ways]
    q_load = loads.start(q_hbm, q_in)
    kv_loads = [
        (loads.start(ck_hbm, old_in.at[0]), loads.start(nk_hbm, new_in.at[0])),
        (loads.start(cv_hbm, old_in.at[1]), loads.start(nv_hbm, new_in.at[1])),
    ]
    small = [loads.start(cr_hbm, held.at[k]), loads.start(nr_hbm, nr)]
    for_queries = [
        loads.start(a, b)
        for a, b in ((states_hbm, states_ref), (dqw_hbm, dqw_ref), (qgain_hbm, qgain), (bp_hbm, bp_both.at[k]))
    ]
    dkv_load = loads.start(dkv_hbm, dkv_in)
    w_loads = [loads.start(w_hbm, w_ref), loads.start(hidden_hbm, hidden)]
    late = [
        loads.start(a, b)
        for a, b in ((gain_hbm, gain_ref), (kgain_hbm, kgain), (dow_hbm, dow_ref))
    ]
    new, slice_width = hidden.shape
    heads = part.shape[1]
    dim = part.shape[3] - 16
    bytes_, half = states_ref.shape[0], kgain.shape[1]
    cached = ck_hbm.shape[0]
    width = q_half.shape[2]
    chip = z * 2 + yl
    tile = 4 * new
    chip_first = chip * 2 * new
    scale = dim ** (-0.5) * LOG2E

    kept, swaps = [], []

    def flatten():
        q_load.wait()
        flat = (q_in[...].reshape(new, 2 * width).astype(F32) * scale).astype(BF16)
        q_half[0] = flat[:, :width]
        q_half[1] = flat[:, width:]
        for which in (0, 1):
            for copy in kv_loads[which]:
                copy.wait()
            for value, count, at in ((old_in[which], cached, 0), (new_in[which], new, cached)):
                flat = value.reshape(count, 2 * width)
                rows = pl.ds(at, count)
                kv_half[which, 0, rows, :] = flat[:, :width]
                kv_half[which, 1, rows, :] = flat[:, width:]

    greet(place.near(direct_steps(zn)) + [{"head": d} for d in others], flatten)

    def swap(which, out):
        for count, at, to in ((cached, 0, k * cached), (new, cached, 2 * cached + k * new)):
            rows = pl.ds(at, count)
            target = out.at[aligned(to, count), :]
            swaps.append(sends.make(kv_half.at[which, 1 - k, rows, :], target, peer))
            kept.append(loads.start(kv_half.at[which, k, rows, :], target))

    def marks(at, cuts):
        lane = lax.broadcasted_iota(jnp.int32, (1, query_mark.shape[1]), 1)
        low, high = jnp.zeros(lane.shape, F32), jnp.zeros(lane.shape, F32)
        for r in range(8):
            low = jnp.where(lane == r, cuts[r], low)
            high = jnp.where(lane == r, cuts[r + 1], high)
        return jnp.where((at >= low) & (at < high), 1.0, 0.0)

    def positions(count, first):
        return (lax.broadcasted_iota(jnp.int32, (count, query_mark.shape[1]), 0) + first).astype(F32)

    def early():
        for copy in small:
            copy.wait()
        held_swap = sends.make(held.at[k], held.at[k], peer)
        swap(0, kc)
        cuts = [
            jnp.sum(jnp.where(nr[...] < r, 1.0, 0.0), axis=1, keepdims=True) for r in range(9)
        ]
        query_mark[...] = marks(positions(query_mark.shape[0], 0), cuts).astype(BF16)
        key_mark[2 * cached :, :] = (LIFT * marks(positions(2 * new, chip_first), cuts)).astype(BF16)
        swap(1, vc)
        held_swap.receive()
        both = held[...]
        cuts = [
            jnp.sum(jnp.sum(jnp.where(both < r, 1.0, 0.0), axis=0), axis=(0, 1), keepdims=True)
            for r in range(9)
        ]
        key_mark[: 2 * cached, :] = (LIFT * marks(positions(2 * cached, 0), cuts)).astype(BF16)

    def attend(t):
        q0 = pl.multiple_of(t * tile, tile)
        rows = pl.ds(q0, tile)
        columns = [slice(h * dim, (h + 1) * dim) for h in range(heads)]
        scores = []
        for cols in columns:
            found = lax.dot_general(
                jnp.concatenate([kc[:, cols], key_mark[...]], axis=1),
                jnp.concatenate([qg[rows, cols], query_mark[rows, :]], axis=1),
                (((1,), (1,)), ((), ())),
                preferred_element_type=F32,
            )
            late = found[2 * cached :]
            at = lax.broadcasted_iota(jnp.int32, late.shape, 0) + chip_first
            asked = lax.broadcasted_iota(jnp.int32, late.shape, 1) + q0
            late = jnp.where(at <= asked, late, HIDE)
            scores.append(jnp.concatenate([found[: 2 * cached], late], axis=0))
        weights = []
        for found in scores:
            top = jnp.max(found, axis=0, keepdims=True) - LIFT
            top = top.astype(BF16).astype(F32)
            weights.append((top, jnp.exp2(found - (top + LIFT))))
        for h, (top, found) in enumerate(weights):
            total = jnp.sum(found, axis=0, keepdims=True)
            out = lax.dot_general(
                vc[:, columns[h]], found.astype(BF16), (((0,), (0,)), ((), ())), preferred_element_type=F32
            )
            for y in (0, 1):
                cols = slice(y * 2 * new, (y + 1) * 2 * new)
                pack(part.at[t, h, y], out[:, cols], top[:, cols], total[:, cols])

    far, near = zn // 2, zn - 1 - zn // 2
    chains = [(h, y) for h in range(heads) for y in (0, 1)]
    counts = {(h, y): (far, near) if h % 2 == 0 else (near, far) for h, y in chains}
    made = {}

    def reduce_step(step, chosen):
        for chain in chains:
            for way in (0, 1):
                count = counts[chain][way]
                if step >= count or count not in chosen:
                    continue
                sign = 1 - 2 * way
                target = place.around(sign * (count - step))
                if step == 0:
                    src = part.at[target, *chain]
                else:
                    made[chain, way, step - 1].receive()
                    src = ring_out.at[*chain, way, step]
                    pack(src, *merged([unpack(part.at[target, *chain]), unpack(ring_in.at[*chain, way, step - 1])]))
                made[chain, way, step] = sends.make(
                    src, ring_in.at[*chain, way, step], place.device(sign, False, 0)
                )

    def work(turn):
        if turn == 0:
            for copy in kept:
                copy.wait()
            for copy in swaps:
                copy.receive()
        if turn == far:
            reduce_step(0, (near,))

        def one(i, carry):
            attend(lax.rem(z + (1 - 2 * i) * turn + 2 * zn, zn))
            return carry

        lax.fori_loop(0, 1 if turn in (0, far) else 2, one, 0)
        if turn == far:
            reduce_step(0, (far,))

    gather = cross_gather if zn == 8 else stride_gather
    gather(sends, place, q_half, qg, early, work)

    swapped = []

    def byte_queries():
        for copy in for_queries:
            copy.wait()
        proj = jnp.dot(states_ref[...], dqw_ref[...], preferred_element_type=F32)
        gain = jnp.concatenate([qgain[...], qgain[...]], axis=1)
        normed = head_norm(proj, gain, half)
        lane = lax.broadcasted_iota(jnp.int32, normed.shape, 1)
        bq_tile[0] = jnp.where(lane < half, normed, 0.0).astype(BF16)
        bq_tile[1] = jnp.where(lane < half, pltpu.roll(normed, half, 1), 0.0).astype(BF16)
        rows = aligned(k * bytes_, bytes_)
        swapped.append(sends.make(bp_both.at[k], bp_both.at[k], peer))
        sends.make(bq_tile.at[1 - k], bq.at[rows, :], peer)
        bq[rows, :] = bq_tile[k]

    def flat_weights():
        dkv_load.wait()
        count = dkv.shape[0] // 4
        for i in range(4):
            rows = slice(i * count, (i + 1) * count)
            dkv[rows, :] = dkv_in[rows].reshape(count, dkv.shape[1])

    idle = [byte_queries, flat_weights]
    for step in range(max(far, 1)):
        if step:
            reduce_step(step, (far, near))
        if step < len(idle):
            idle[step]()
    for work_left in idle[max(far, 1) :]:
        work_left()
    summed = {}
    for chain in chains:
        got = [unpack(part.at[z, *chain])]
        for way in (0, 1):
            count = counts[chain][way]
            if count:
                made[chain, way, count - 1].receive()
                got.append(unpack(ring_in.at[*chain, way, count - 1]))
        summed[chain] = merged(got)
    for y in (0, 1):
        for core in (0, 1):
            joined = []
            for a, b in zip(summed[0, y], summed[1, y]):
                lane = lax.broadcasted_iota(jnp.int32, a.shape, 1)
                if core == 0:
                    joined.append(jnp.where(lane < new, a, pltpu.roll(b, new, 1)))
                else:
                    joined.append(jnp.where(lane < new, pltpu.roll(a, new, 1), b))
            pack(last.at[y, core], *joined)
    across = sends.make(last.at[1 - yl, k], last_in.at[0], place.device(0, True, False))
    beside = sends.make(last.at[yl, 1 - k], last_in.at[1], peer)
    diagonal = sends.make(last.at[1 - yl, 1 - k], last_in.at[2], place.device(0, True, True))
    for pair, parts, waits in (
        (k, (last.at[yl, k], last_in.at[0]), (across,)),
        (1 - k, (last_in.at[1], last_in.at[2]), (beside, diagonal)),
    ):
        for copy in waits:
            copy.receive()
        out, _, total = merged([unpack(ref) for ref in parts])
        turned = (out / total).T.astype(BF16)
        both = jnp.concatenate([turned[:new], turned[new:]], axis=1)
        att[:, aligned(pair * 2 * dim, 2 * dim)] = both

    for copy in w_loads:
        copy.wait()
    mine = att[...]

    def columns_for(d):
        return jnp.dot(mine, w_ref[:, aligned(d * slice_width, slice_width)], preferred_element_type=F32)

    rs_sends = []
    for i, d in enumerate(others):
        rs_out[i] = columns_for(d).astype(BF16)
        rs_sends.append(sends.make(rs_out.at[i], rs_in.at[i], {"head": d}))
    own = columns_for(me) + hidden[...].astype(F32)
    for i, copy in enumerate(rs_sends):
        copy.receive()
        own = own + rs_in[i].astype(F32)
    rounded = own.astype(BF16)
    ag_in[0] = rounded
    ag_sends = [sends.make(ag_in.at[0], ag_in.at[1 + i], {"head": d}) for i, d in enumerate(others)]
    patch_out[...] = rounded
    for copy in late:
        copy.wait()
    squares, proj = 0.0, 0.0
    for i, source in enumerate(sources):
        if i:
            ag_sends[i - 1].receive()
        wide = ag_in[i].astype(F32)
        squares = squares + jnp.sum(wide * wide, axis=1, keepdims=True)
        scaled = (wide * gain_ref[:, aligned(source * slice_width, slice_width)]).astype(BF16)
        rows = aligned(source * slice_width, slice_width)
        proj = proj + jnp.dot(scaled, dkv[rows, :], preferred_element_type=F32)
    proj = proj * lax.rsqrt(squares / (hn * slice_width) + 1e-5)
    keys = head_norm(proj[:, : 2 * half], jnp.concatenate([kgain[...], kgain[...]], axis=1), half)
    values = proj[:, 2 * half :]
    lane = lax.broadcasted_iota(jnp.int32, keys.shape, 1)
    kv_tile[0] = jnp.where(lane < half, keys, pltpu.roll(values, half, 1)).astype(BF16)
    kv_tile[1] = jnp.where(lane < half, pltpu.roll(keys, half, 1), values).astype(BF16)

    def byte_spans():
        swapped[0].receive()
        owners = bp_both[...]
        first = jnp.zeros(owners.shape, F32)
        mates = nr[...]
        for r in range(1, 8):
            begins = jnp.sum(jnp.where(mates < r, 1.0, 0.0), axis=1, keepdims=True)[None]
            first = jnp.where(owners.astype(F32) >= begins, begins, first)
        span[...] = first.astype(jnp.int32)

    stride_gather(sends, place, kv_tile, kvg, byte_spans, lambda n: None)
    for copy in sends.made:
        copy.receive()
    spans = (span, bp_both)

    block = min(512, kvg.shape[0])
    byte_scale = half ** (-0.5) * LOG2E

    def byte_attention(core):
        queries = bq[aligned(core * bytes_, bytes_), :]
        first, owner = spans[0][core], spans[1][core]
        out, total = 0.0, 0.0
        for b in range(kvg.shape[0] // block):
            kv = kvg[b * block : (b + 1) * block, :]
            scores = lax.dot_general(kv, queries, (((1,), (1,)), ((), ())), preferred_element_type=F32)
            at = lax.broadcasted_iota(jnp.int32, scores.shape, 0) + b * block
            weights = jnp.where((at >= first) & (at <= owner), jnp.exp2(scores * byte_scale), 0.0)
            total = total + jnp.sum(weights, axis=0, keepdims=True)
            out = out + lax.dot_general(
                kv, weights.astype(BF16), (((0,), (0,)), ((), ())), preferred_element_type=F32
            )
        return (out[half:, :] / total).astype(BF16)

    mix_rows = aligned(k * half, half)
    mix_tile[...] = byte_attention(1 - k)
    mix_send = sends.make(mix_tile, mix.at[mix_rows, :], peer)
    mix[mix_rows, :] = byte_attention(k)
    mix_send.receive()
    mixed = mix[...]
    out_width = byte_out.shape[1]

    def byte_columns_for(d):
        cols = aligned(d * out_width, out_width)
        return lax.dot_general(mixed, dow_ref[:, cols], (((0,), (0,)), ((), ())), preferred_element_type=F32)

    bs_sends = []
    for i, d in enumerate(others):
        bs_out[i] = byte_columns_for(d).astype(BF16)
        bs_sends.append(sends.make(bs_out.at[i], bs_in.at[i], {"head": d}))
    own = byte_columns_for(me) + states_ref[:, aligned(me * out_width, out_width)].astype(F32)
    for i, copy in enumerate(bs_sends):
        copy.receive()
        own = own + bs_in[i].astype(F32)
    byte_out[...] = own.astype(BF16)
    sends.close()


def hand_over(a, b, a_out, b_out, a_held, b_held, sem):
    loads = Loads(sem)
    for copy in (loads.start(a, a_held), loads.start(b, b_held)):
        copy.wait()
    for copy in (loads.start(a_held, a_out), loads.start(b_held, b_out)):
        copy.wait()


def per_device(
    zn,
    hn,
    patch_hidden,
    queries,
    new_keys,
    new_values,
    cache_keys,
    cache_values,
    cache_request,
    new_request,
    out_weight,
    norm_gain,
    dec_kv_weight,
    dec_query_weight,
    query_gain,
    key_gain,
    dec_out_weight,
    byte_states,
    byte_patch,
):
    new, heads, dim = queries.shape
    cached = cache_keys.shape[0]
    total = new_request.shape[0]
    pair = heads // 2 * dim
    all_keys = 2 * (cached + new)
    slice_width = patch_hidden.shape[1]
    held = cache_request.reshape(8, cached // 8)
    mates = new_request.reshape(1, total)
    tile = 4 * new
    kv_rows = dec_kv_weight.shape[0]
    dec_width = dec_kv_weight.shape[2]
    bytes_ = byte_states.shape[0]
    out_width = dec_out_weight.shape[1] // hn
    half = dec_width // 2
    steps = max(zn // 2, 1)
    peers = max(hn - 1, 1)
    copies = 5 + 7 + 4 * zn + 2 + 4 * (zn - 1) + 3 + 3 * (hn - 1) + 3 + 4 * zn + 1
    flat_weight = out_weight.reshape(heads * dim, -1)
    results = pl.pallas_call(
        functools.partial(solve, zn, hn),
        out_shape=(
            jax.ShapeDtypeStruct(patch_hidden.shape, BF16),
            jax.ShapeDtypeStruct((bytes_, out_width), BF16),
        ),
        in_specs=[in_place()] * 17,
        out_specs=(in_vmem(), in_vmem()),
        scratch_shapes=[
            VMEM(queries.shape, BF16),
            VMEM((2, *new_keys.shape), BF16),
            VMEM((2, *cache_keys.shape), BF16),
            VMEM((2, *held.shape), jnp.int32),
            VMEM((2, new, pair), BF16),
            VMEM((2, 2, cached + new, pair), BF16),
            VMEM((total, pair), BF16),
            VMEM((all_keys, pair), BF16),
            VMEM((all_keys, pair), BF16),
            VMEM((all_keys, 128), BF16),
            VMEM((total, 128), BF16),
            VMEM((zn, heads // 2, 2, dim + 16, 2 * new), BF16),
            VMEM(patch_hidden.shape, BF16),
            VMEM(flat_weight.shape, BF16),
            VMEM(dec_kv_weight.shape, BF16),
            VMEM((kv_rows, 2 * dec_width), BF16),
            VMEM((1, kv_rows), F32),
            VMEM((1, half), F32),
            VMEM((1, half), F32),
            VMEM(dec_query_weight.shape, BF16),
            VMEM(dec_out_weight.shape, BF16),
            VMEM(byte_states.shape, BF16),
            VMEM((1, total), jnp.int32),
            VMEM((heads // 2, 2, 2, steps, dim + 16, 2 * new), BF16),
            VMEM((heads // 2, 2, 2, steps, dim + 16, 2 * new), BF16),
            VMEM((2, 2, dim + 16, 2 * new), BF16),
            VMEM((3, dim + 16, 2 * new), BF16),
            VMEM((new, heads * dim), BF16),
            VMEM((peers, new, slice_width), BF16),
            VMEM((peers, new, slice_width), BF16),
            VMEM((hn, new, slice_width), BF16),
            VMEM((2, new, dec_width), BF16),
            VMEM((total, dec_width), BF16),
            VMEM((2, bytes_, dec_width), BF16),
            VMEM((2 * bytes_, dec_width), BF16),
            VMEM((2, 1, bytes_), jnp.int32),
            VMEM((2, 1, bytes_), jnp.int32),
            VMEM((half, bytes_), BF16),
            VMEM((dec_width, bytes_), BF16),
            VMEM((peers, bytes_, out_width), BF16),
            VMEM((peers, bytes_, out_width), BF16),
            pltpu.SemaphoreType.DMA((copies,)),
            pltpu.SemaphoreType.DMA((copies,)),
            pltpu.SemaphoreType.DMA((24,)),
        ],
        compiler_params=pltpu.CompilerParams(
            collective_id=0, has_side_effects=True, vmem_limit_bytes=60 * 2**20
        ),
        name="solve",
    )(
        queries,
        new_keys,
        new_values,
        cache_keys,
        cache_values,
        held,
        patch_hidden,
        flat_weight,
        dec_kv_weight,
        norm_gain.reshape(1, kv_rows),
        key_gain.reshape(1, half),
        query_gain.reshape(1, half),
        dec_query_weight,
        dec_out_weight,
        byte_states,
        byte_patch.reshape(1, bytes_),
        mates,
    )
    return pl.pallas_call(
        hand_over,
        out_shape=tuple(jax.ShapeDtypeStruct(r.shape, r.dtype) for r in results),
        in_specs=[in_place()] * 2,
        out_specs=(in_place(),) * 2,
        scratch_shapes=[VMEM(r.shape, r.dtype) for r in results] + [pltpu.SemaphoreType.DMA((4,))],
        compiler_params=pltpu.CompilerParams(vmem_limit_bytes=60 * 2**20),
        name="hand_over",
    )(*results)


def solution(mesh):
    placed = (
        P("ctx", "head"),
        P("ctx", "head", None),
        P("ctx", "head", None),
        P("ctx", "head", None),
        P("ctx", "head", None),
        P("ctx", "head", None),
        P("ctx"),
        P(),
        P("head", None, None),
        P(),
        P(None, None, "head"),
        P(None, "head"),
        P(),
        P(),
        P("head", None),
        P("ctx", None),
        P("ctx"),
    )
    return jax.shard_map(
        functools.partial(per_device, mesh.shape["ctx"] // 4, mesh.shape["head"]),
        mesh=mesh,
        in_specs=placed,
        out_specs=(P("ctx", "head"), P("ctx", "head")),
        check_vma=False,
    )
```

```python
import functools

import jax
import jax.numpy as jnp
from jax import lax
from jax.experimental import pallas as pl
from jax.experimental.pallas import tpu as pltpu
from jax.sharding import PartitionSpec as P

MESH = pl.DeviceIdType.MESH
VMEM = pltpu.VMEM
F32 = jnp.float32
BF16 = jnp.bfloat16
HIDE = -1e30
LIFT = 2048.0
LOG2E = 1.4426950408889634


def in_vmem():
    return pl.BlockSpec(memory_space=pltpu.VMEM)


def in_place():
    return pl.BlockSpec(memory_space=pltpu.HBM)


class Place:
    def __init__(self, zn):
        c = lax.axis_index("ctx")
        self.c = c
        self.zn = zn
        self.z = lax.div(c, 4)
        self.yl = lax.rem(lax.div(c, 2), 2)
        self.k = lax.rem(c, 2)
        self.cores = (self.k, 1 - self.k)

    def around(self, step):
        return lax.rem(self.z + (step + 2 * self.zn), self.zn)

    def device(self, step, other_y, other_core):
        y = 1 - self.yl if other_y else self.yl
        return {"ctx": self.around(step) * 4 + y * 2 + self.cores[other_core]}

    def near(self, steps):
        found = [self.device(0, False, True)]
        for core in (False, True):
            found += [self.device(step, True, core) for step in (0, 1, -1)]
            found += [self.device(step, False, core) for step in steps]
        return found


class Copy:
    def __init__(self, dma):
        self.dma, self.got = dma, False

    def start(self):
        self.dma.start()
        return self

    def receive(self):
        if not self.got:
            self.dma.wait_recv()
        self.got = True


class Sends:
    def __init__(self, send_sem, recv_sem):
        self.send_sem, self.recv_sem, self.made = send_sem, recv_sem, []

    def make(self, src, dst, device):
        at = len(self.made)
        copy = Copy(
            pltpu.make_async_remote_copy(
                src_ref=src,
                dst_ref=dst,
                send_sem=self.send_sem.at[at],
                recv_sem=self.recv_sem.at[at],
                device_id=device,
                device_id_type=MESH,
            )
        )
        self.made.append(copy)
        return copy.start()

    def close(self):
        for copy in self.made:
            copy.receive()
        for copy in self.made:
            copy.dma.wait_send()


class Loads:
    def __init__(self, sem):
        self.sem, self.used = sem, 0

    def start(self, src, dst):
        copy = pltpu.make_async_copy(src, dst, self.sem.at[self.used])
        self.used += 1
        copy.start()
        return copy


def greet(devices, meanwhile):
    barrier = pltpu.get_barrier_semaphore()
    for device in devices:
        pl.semaphore_signal(barrier, inc=1, device_id=device, device_id_type=MESH)
    meanwhile()
    pl.semaphore_wait(barrier, len(devices))


def aligned(start, size):
    return pl.ds(pl.multiple_of(start, size), size)


def first_hop(sends, place, source, buffer, step, other_y, cores):
    rows = source.shape[1]
    mine = buffer.at[aligned(place.c * rows, rows), :]
    return [sends.make(source.at[place.cores[core]], mine, place.device(step, other_y, core)) for core in cores]


def direct_steps(zn):
    if zn == 8:
        return (2, -2, 1, -1)
    return tuple(way * n for n in range(1, zn // 2 + 1) for way in (1, -1) if 2 * n < zn or way > 0)


def stride_gather(sends, place, source, buffer, idle, work):
    zn, rows = place.zn, source.shape[1]
    far = zn // 2
    arriving = [[] for _ in range(far + 1)]

    def first(step, other_y, cores):
        return first_hop(sends, place, source, buffer, step, other_y, cores)

    def piece(step, y):
        return buffer.at[aligned((place.around(step) * 2 + y) * 2 * rows, 2 * rows), :]

    steps = direct_steps(zn)
    from_y = first(0, True, (0, 1))
    found = {(0, step): first(step, False, (0, 1)) for step in steps}
    arriving[0] += first(0, False, (1,))
    buffer[aligned(place.c * rows, rows), :] = source[place.k]
    idle()
    for copy in from_y:
        copy.receive()
    theirs = piece(0, 1 - place.yl)
    for step in steps:
        found[1, step] = [sends.make(theirs, theirs, place.device(step, False, 0))]
    for (_, step), copies in found.items():
        arriving[abs(step)] += copies

    def relay(stream):
        for way in (1, -1):
            for copy in found[stream, 2 * way]:
                copy.receive()
            passed = piece(-2 * way, 1 - place.yl if stream else place.yl)
            arriving[3].append(sends.make(passed, passed, place.device(way, False, 0)))
            if (way == 1) == (stream == 0):
                arriving[4].append(sends.make(passed, passed, place.device(2 * way, False, 0)))

    if zn == 8:
        relay(0)
    for n in range(far + 1):
        if n == 1 and zn == 8:
            relay(1)
        for copy in arriving[n]:
            copy.receive()
        work(n)


def cross_gather(sends, place, source, buffer, idle, work):
    rows = source.shape[1]
    arriving = [[] for _ in range(5)]

    def first(step, other_y, cores=(0, 1)):
        return first_hop(sends, place, source, buffer, step, other_y, cores)

    def piece(step):
        return buffer.at[aligned((place.around(step) * 2 + place.yl) * 2 * rows, 2 * rows), :]

    def across(step):
        passed = piece(step)
        return sends.make(passed, passed, place.device(0, True, False))

    found = {step: first(step, False) for step in (2, -2)}
    arriving[0] += first(0, True) + first(0, False, (1,))
    for step in (1, -1):
        arriving[1] += first(step, False) + first(step, True)
    buffer[aligned(place.c * rows, rows), :] = source[place.k]
    idle()
    relayed = {}
    for way in (1, -1):
        for copy in found[2 * way]:
            copy.receive()
        passed = piece(-2 * way)
        relayed[way] = sends.make(passed, passed, place.device(way, False, 0))
    side = 1 - 2 * place.k
    passed = piece(-2 * side)
    opposite = sends.make(passed, passed, place.device(2 * side, False, 0))
    arriving[2] += [across(-2), across(2)]
    for n in range(5):
        if n == 2:
            for way in (1, -1):
                relayed[way].receive()
                arriving[3].append(across(-3 * way))
            opposite.receive()
            arriving[4].append(across(4))
        for copy in arriving[n]:
            copy.receive()
        work(n)


def pack(ref, out, top, total):
    dim = out.shape[0]
    ref[0:dim, :] = out.astype(BF16)
    coarse = total.astype(BF16).astype(F32)
    row = lax.broadcasted_iota(jnp.int32, (16, out.shape[1]), 0)
    tail = jnp.where(row == 0, top, jnp.where(row == 1, coarse, jnp.where(row == 2, total - coarse, 0.0)))
    ref[dim : dim + 16, :] = tail.astype(BF16)


def unpack(ref):
    value = ref[...]
    dim = value.shape[0] - 16
    tail = value[dim:, :].astype(F32)
    return value[:dim, :].astype(F32), tail[0:1, :], tail[1:2, :] + tail[2:3, :]


def merged(parts):
    top = parts[0][1]
    for part in parts[1:]:
        top = jnp.maximum(top, part[1])
    out, total = 0.0, 0.0
    for o, m, l in parts:
        factor = jnp.exp2(m - top)
        out = out + o * factor
        total = total + l * factor
    return out, top, total


def head_norm(values, gain, half):
    lane = lax.broadcasted_iota(jnp.int32, values.shape, 1)
    first = lane < half
    squares = values * values
    s0 = jnp.sum(jnp.where(first, squares, 0.0), axis=1, keepdims=True)
    s1 = jnp.sum(jnp.where(first, 0.0, squares), axis=1, keepdims=True)
    return values * lax.rsqrt(jnp.where(first, s0, s1) / half + 1e-6) * gain


def solve(
    zn, hn, q_hbm, nk_hbm, nv_hbm, ck_hbm, cv_hbm, cr_hbm,
    hidden_hbm, w_hbm, dkv_hbm, gain_hbm, kgain_hbm, qgain_hbm, dqw_hbm, dow_hbm, states_hbm, bp_hbm, nr_hbm,
    patch_out, byte_out,
    q_in, new_in, old_in, held, q_half, kv_half, qg, kc, vc, key_mark, query_mark, part,
    hidden, w_ref, dkv_in, dkv, gain_ref, kgain, qgain, dqw_ref, dow_ref, states_ref, nr,
    ring_in, ring_out, last, last_in, att, rs_out, rs_in, ag_in, kv_tile, kvg, bq_tile, bq,
    bp_both, span, mix_tile, mix, bs_out, bs_in, send_sem, recv_sem, local_sem,
):
    place = Place(zn)
    sends, loads = Sends(send_sem, recv_sem), Loads(local_sem)
    k, z, yl = place.k, place.z, place.yl
    me = lax.axis_index("head")
    peer = place.device(0, False, True)
    x, yh = lax.div(me, 2), lax.rem(me, 2)
    xn = hn // 2
    ways = [(dx, dy) for dy in (1, 0) for dx in sorted(range(xn), key=lambda n: -min(n, xn - n)) if dx or dy]

    def head_at(dx, dy):
        return lax.rem(x + dx + xn, xn) * 2 + (1 - yh if dy else yh)

    others = [head_at(dx, dy) for dx, dy in ways]
    sources = [me] + [head_at(-dx, dy) for dx, dy in ways]
    q_load = loads.start(q_hbm, q_in)
    kv_loads = [
        (loads.start(ck_hbm, old_in.at[0]), loads.start(nk_hbm, new_in.at[0])),
        (loads.start(cv_hbm, old_in.at[1]), loads.start(nv_hbm, new_in.at[1])),
    ]
    small = [loads.start(cr_hbm, held.at[k]), loads.start(nr_hbm, nr)]
    for_queries, dkv_loads, w_loads, late = [], [], [], []
    new, slice_width = hidden.shape
    heads = part.shape[1]
    dim = part.shape[3] - 16
    bytes_, half = states_ref.shape[0], kgain.shape[1]
    cached = ck_hbm.shape[0]
    width = q_half.shape[2]
    chip = z * 2 + yl
    tile = 4 * new
    chip_first = chip * 2 * new
    scale = dim ** (-0.5) * LOG2E

    kept, swaps = [], []

    def flatten():
        q_load.wait()
        flat = (q_in[...].reshape(new, 2 * width).astype(F32) * scale).astype(BF16)
        q_half[0] = flat[:, :width]
        q_half[1] = flat[:, width:]
        for which in (0, 1):
            for copy in kv_loads[which]:
                copy.wait()
            for value, count, at in ((old_in[which], cached, 0), (new_in[which], new, cached)):
                flat = value.reshape(count, 2 * width)
                rows = pl.ds(at, count)
                kv_half[which, 0, rows, :] = flat[:, :width]
                kv_half[which, 1, rows, :] = flat[:, width:]

    greet(place.near(direct_steps(zn)) + [{"head": d} for d in others], flatten)

    def swap(which, out):
        for count, at, to in ((cached, 0, k * cached), (new, cached, 2 * cached + k * new)):
            rows = pl.ds(at, count)
            target = out.at[aligned(to, count), :]
            swaps.append(sends.make(kv_half.at[which, 1 - k, rows, :], target, peer))
            kept.append(loads.start(kv_half.at[which, k, rows, :], target))

    def marks(at, cuts):
        lane = lax.broadcasted_iota(jnp.int32, (1, query_mark.shape[1]), 1)
        low, high = jnp.zeros(lane.shape, F32), jnp.zeros(lane.shape, F32)
        for r in range(8):
            low = jnp.where(lane == r, cuts[r], low)
            high = jnp.where(lane == r, cuts[r + 1], high)
        return jnp.where((at >= low) & (at < high), 1.0, 0.0)

    def positions(count, first):
        return (lax.broadcasted_iota(jnp.int32, (count, query_mark.shape[1]), 0) + first).astype(F32)

    def later_loads():
        for group, pairs in (
            (for_queries, ((states_hbm, states_ref), (dqw_hbm, dqw_ref), (qgain_hbm, qgain), (bp_hbm, bp_both.at[k]))),
            (dkv_loads, ((dkv_hbm, dkv_in),)),
            (w_loads, ((w_hbm, w_ref), (hidden_hbm, hidden))),
            (late, ((gain_hbm, gain_ref), (kgain_hbm, kgain), (dow_hbm, dow_ref))),
        ):
            group += [loads.start(a, b) for a, b in pairs]

    def early():
        for copy in small:
            copy.wait()
        held_swap = sends.make(held.at[k], held.at[k], peer)
        swap(0, kc)
        later_loads()
        cuts = [
            jnp.sum(jnp.where(nr[...] < r, 1.0, 0.0), axis=1, keepdims=True) for r in range(9)
        ]
        query_mark[...] = marks(positions(query_mark.shape[0], 0), cuts).astype(BF16)
        key_mark[2 * cached :, :] = (LIFT * marks(positions(2 * new, chip_first), cuts)).astype(BF16)
        swap(1, vc)
        held_swap.receive()
        both = held[...]
        cuts = [
            jnp.sum(jnp.sum(jnp.where(both < r, 1.0, 0.0), axis=0), axis=(0, 1), keepdims=True)
            for r in range(9)
        ]
        key_mark[: 2 * cached, :] = (LIFT * marks(positions(2 * cached, 0), cuts)).astype(BF16)

    def attend(t):
        q0 = pl.multiple_of(t * tile, tile)
        rows = pl.ds(q0, tile)
        columns = [slice(h * dim, (h + 1) * dim) for h in range(heads)]
        scores = []
        for cols in columns:
            found = lax.dot_general(
                jnp.concatenate([kc[:, cols], key_mark[...]], axis=1),
                jnp.concatenate([qg[rows, cols], query_mark[rows, :]], axis=1),
                (((1,), (1,)), ((), ())),
                preferred_element_type=F32,
            )
            late = found[2 * cached :]
            at = lax.broadcasted_iota(jnp.int32, late.shape, 0) + chip_first
            asked = lax.broadcasted_iota(jnp.int32, late.shape, 1) + q0
            late = jnp.where(at <= asked, late, HIDE)
            scores.append(jnp.concatenate([found[: 2 * cached], late], axis=0))
        weights = []
        for found in scores:
            top = jnp.max(found, axis=0, keepdims=True) - LIFT
            top = top.astype(BF16).astype(F32)
            weights.append((top, jnp.exp2(found - (top + LIFT))))
        for h, (top, found) in enumerate(weights):
            total = jnp.sum(found, axis=0, keepdims=True)
            out = lax.dot_general(
                vc[:, columns[h]], found.astype(BF16), (((0,), (0,)), ((), ())), preferred_element_type=F32
            )
            for y in (0, 1):
                cols = slice(y * 2 * new, (y + 1) * 2 * new)
                pack(part.at[t, h, y], out[:, cols], top[:, cols], total[:, cols])

    far, near = zn // 2, zn - 1 - zn // 2
    chains = [(h, y) for h in range(heads) for y in (0, 1)]
    counts = {(h, y): (far, near) if h % 2 == 0 else (near, far) for h, y in chains}
    made = {}

    def reduce_step(step, chosen):
        for chain in chains:
            for way in (0, 1):
                count = counts[chain][way]
                if step >= count or count not in chosen:
                    continue
                sign = 1 - 2 * way
                target = place.around(sign * (count - step))
                if step == 0:
                    src = part.at[target, *chain]
                else:
                    made[chain, way, step - 1].receive()
                    src = ring_out.at[*chain, way, step]
                    pack(src, *merged([unpack(part.at[target, *chain]), unpack(ring_in.at[*chain, way, step - 1])]))
                made[chain, way, step] = sends.make(
                    src, ring_in.at[*chain, way, step], place.device(sign, False, 0)
                )

    def work(turn):
        if turn == 0:
            for copy in kept:
                copy.wait()
            for copy in swaps:
                copy.receive()
        if turn == far:
            reduce_step(0, (near,))

        def one(i, carry):
            attend(lax.rem(z + (1 - 2 * i) * turn + 2 * zn, zn))
            return carry

        lax.fori_loop(0, 1 if turn in (0, far) else 2, one, 0)
        if turn == far:
            reduce_step(0, (far,))

    gather = cross_gather if zn == 8 else stride_gather
    gather(sends, place, q_half, qg, early, work)

    swapped = []

    def byte_queries():
        for copy in for_queries:
            copy.wait()
        proj = jnp.dot(states_ref[...], dqw_ref[...], preferred_element_type=F32)
        gain = jnp.concatenate([qgain[...], qgain[...]], axis=1)
        normed = head_norm(proj, gain, half)
        lane = lax.broadcasted_iota(jnp.int32, normed.shape, 1)
        bq_tile[0] = jnp.where(lane < half, normed, 0.0).astype(BF16)
        bq_tile[1] = jnp.where(lane < half, pltpu.roll(normed, half, 1), 0.0).astype(BF16)
        rows = aligned(k * bytes_, bytes_)
        swapped.append(sends.make(bp_both.at[k], bp_both.at[k], peer))
        sends.make(bq_tile.at[1 - k], bq.at[rows, :], peer)
        bq[rows, :] = bq_tile[k]

    def flat_weights():
        dkv_loads[0].wait()
        count = dkv.shape[0] // 4
        for i in range(4):
            rows = slice(i * count, (i + 1) * count)
            dkv[rows, :] = dkv_in[rows].reshape(count, dkv.shape[1])

    idle = [byte_queries, flat_weights]
    for step in range(max(far, 1)):
        if step:
            reduce_step(step, (far, near))
        if step < len(idle):
            idle[step]()
    for work_left in idle[max(far, 1) :]:
        work_left()
    summed = {}
    for chain in chains:
        got = [unpack(part.at[z, *chain])]
        for way in (0, 1):
            count = counts[chain][way]
            if count:
                made[chain, way, count - 1].receive()
                got.append(unpack(ring_in.at[*chain, way, count - 1]))
        summed[chain] = merged(got)
    for y in (0, 1):
        for core in (0, 1):
            joined = []
            for a, b in zip(summed[0, y], summed[1, y]):
                lane = lax.broadcasted_iota(jnp.int32, a.shape, 1)
                if core == 0:
                    joined.append(jnp.where(lane < new, a, pltpu.roll(b, new, 1)))
                else:
                    joined.append(jnp.where(lane < new, pltpu.roll(a, new, 1), b))
            pack(last.at[y, core], *joined)
    across = sends.make(last.at[1 - yl, k], last_in.at[0], place.device(0, True, False))
    beside = sends.make(last.at[yl, 1 - k], last_in.at[1], peer)
    diagonal = sends.make(last.at[1 - yl, 1 - k], last_in.at[2], place.device(0, True, True))
    for pair, parts, waits in (
        (k, (last.at[yl, k], last_in.at[0]), (across,)),
        (1 - k, (last_in.at[1], last_in.at[2]), (beside, diagonal)),
    ):
        for copy in waits:
            copy.receive()
        out, _, total = merged([unpack(ref) for ref in parts])
        turned = (out / total).T.astype(BF16)
        both = jnp.concatenate([turned[:new], turned[new:]], axis=1)
        att[:, aligned(pair * 2 * dim, 2 * dim)] = both

    for copy in w_loads:
        copy.wait()
    mine = att[...]

    def columns_for(d):
        return jnp.dot(mine, w_ref[:, aligned(d * slice_width, slice_width)], preferred_element_type=F32)

    rs_sends = []
    for i, d in enumerate(others):
        rs_out[i] = columns_for(d).astype(BF16)
        rs_sends.append(sends.make(rs_out.at[i], rs_in.at[i], {"head": d}))
    own = columns_for(me) + hidden[...].astype(F32)
    for i, copy in enumerate(rs_sends):
        copy.receive()
        own = own + rs_in[i].astype(F32)
    rounded = own.astype(BF16)
    ag_in[0] = rounded
    ag_sends = [sends.make(ag_in.at[0], ag_in.at[1 + i], {"head": d}) for i, d in enumerate(others)]
    patch_out[...] = rounded
    for copy in late:
        copy.wait()
    squares, proj = 0.0, 0.0
    for i, source in enumerate(sources):
        if i:
            ag_sends[i - 1].receive()
        wide = ag_in[i].astype(F32)
        squares = squares + jnp.sum(wide * wide, axis=1, keepdims=True)
        scaled = (wide * gain_ref[:, aligned(source * slice_width, slice_width)]).astype(BF16)
        rows = aligned(source * slice_width, slice_width)
        proj = proj + jnp.dot(scaled, dkv[rows, :], preferred_element_type=F32)
    proj = proj * lax.rsqrt(squares / (hn * slice_width) + 1e-5)
    keys = head_norm(proj[:, : 2 * half], jnp.concatenate([kgain[...], kgain[...]], axis=1), half)
    values = proj[:, 2 * half :]
    lane = lax.broadcasted_iota(jnp.int32, keys.shape, 1)
    kv_tile[0] = jnp.where(lane < half, keys, pltpu.roll(values, half, 1)).astype(BF16)
    kv_tile[1] = jnp.where(lane < half, pltpu.roll(keys, half, 1), values).astype(BF16)

    def byte_spans():
        swapped[0].receive()
        owners = bp_both[...]
        first = jnp.zeros(owners.shape, F32)
        mates = nr[...]
        for r in range(1, 8):
            begins = jnp.sum(jnp.where(mates < r, 1.0, 0.0), axis=1, keepdims=True)[None]
            first = jnp.where(owners.astype(F32) >= begins, begins, first)
        span[...] = first.astype(jnp.int32)

    stride_gather(sends, place, kv_tile, kvg, byte_spans, lambda n: None)
    for copy in sends.made:
        copy.receive()
    spans = (span, bp_both)

    block = min(512, kvg.shape[0])
    byte_scale = half ** (-0.5) * LOG2E

    def byte_attention(core):
        queries = bq[aligned(core * bytes_, bytes_), :]
        first, owner = spans[0][core], spans[1][core]
        out, total = 0.0, 0.0
        for b in range(kvg.shape[0] // block):
            kv = kvg[b * block : (b + 1) * block, :]
            scores = lax.dot_general(kv, queries, (((1,), (1,)), ((), ())), preferred_element_type=F32)
            at = lax.broadcasted_iota(jnp.int32, scores.shape, 0) + b * block
            weights = jnp.where((at >= first) & (at <= owner), jnp.exp2(scores * byte_scale), 0.0)
            total = total + jnp.sum(weights, axis=0, keepdims=True)
            out = out + lax.dot_general(
                kv, weights.astype(BF16), (((0,), (0,)), ((), ())), preferred_element_type=F32
            )
        return (out[half:, :] / total).astype(BF16)

    mix_rows = aligned(k * half, half)
    mix_tile[...] = byte_attention(1 - k)
    mix_send = sends.make(mix_tile, mix.at[mix_rows, :], peer)
    mix[mix_rows, :] = byte_attention(k)
    mix_send.receive()
    mixed = mix[...]
    out_width = byte_out.shape[1]

    def byte_columns_for(d):
        cols = aligned(d * out_width, out_width)
        return lax.dot_general(mixed, dow_ref[:, cols], (((0,), (0,)), ((), ())), preferred_element_type=F32)

    bs_sends = []
    for i, d in enumerate(others):
        bs_out[i] = byte_columns_for(d).astype(BF16)
        bs_sends.append(sends.make(bs_out.at[i], bs_in.at[i], {"head": d}))
    own = byte_columns_for(me) + states_ref[:, aligned(me * out_width, out_width)].astype(F32)
    for i, copy in enumerate(bs_sends):
        copy.receive()
        own = own + bs_in[i].astype(F32)
    byte_out[...] = own.astype(BF16)
    sends.close()


def hand_over(a, b, a_out, b_out, a_held, b_held, sem):
    loads = Loads(sem)
    for copy in (loads.start(a, a_held), loads.start(b, b_held)):
        copy.wait()
    for copy in (loads.start(a_held, a_out), loads.start(b_held, b_out)):
        copy.wait()


def per_device(
    zn,
    hn,
    patch_hidden,
    queries,
    new_keys,
    new_values,
    cache_keys,
    cache_values,
    cache_request,
    new_request,
    out_weight,
    norm_gain,
    dec_kv_weight,
    dec_query_weight,
    query_gain,
    key_gain,
    dec_out_weight,
    byte_states,
    byte_patch,
):
    new, heads, dim = queries.shape
    cached = cache_keys.shape[0]
    total = new_request.shape[0]
    pair = heads // 2 * dim
    all_keys = 2 * (cached + new)
    slice_width = patch_hidden.shape[1]
    held = cache_request.reshape(8, cached // 8)
    mates = new_request.reshape(1, total)
    tile = 4 * new
    kv_rows = dec_kv_weight.shape[0]
    dec_width = dec_kv_weight.shape[2]
    bytes_ = byte_states.shape[0]
    out_width = dec_out_weight.shape[1] // hn
    half = dec_width // 2
    steps = max(zn // 2, 1)
    peers = max(hn - 1, 1)
    copies = 5 + 7 + 4 * zn + 2 + 4 * (zn - 1) + 3 + 3 * (hn - 1) + 3 + 4 * zn + 1
    flat_weight = out_weight.reshape(heads * dim, -1)
    results = pl.pallas_call(
        functools.partial(solve, zn, hn),
        out_shape=(
            jax.ShapeDtypeStruct(patch_hidden.shape, BF16),
            jax.ShapeDtypeStruct((bytes_, out_width), BF16),
        ),
        in_specs=[in_place()] * 17,
        out_specs=(in_vmem(), in_vmem()),
        scratch_shapes=[
            VMEM(queries.shape, BF16),
            VMEM((2, *new_keys.shape), BF16),
            VMEM((2, *cache_keys.shape), BF16),
            VMEM((2, *held.shape), jnp.int32),
            VMEM((2, new, pair), BF16),
            VMEM((2, 2, cached + new, pair), BF16),
            VMEM((total, pair), BF16),
            VMEM((all_keys, pair), BF16),
            VMEM((all_keys, pair), BF16),
            VMEM((all_keys, 128), BF16),
            VMEM((total, 128), BF16),
            VMEM((zn, heads // 2, 2, dim + 16, 2 * new), BF16),
            VMEM(patch_hidden.shape, BF16),
            VMEM(flat_weight.shape, BF16),
            VMEM(dec_kv_weight.shape, BF16),
            VMEM((kv_rows, 2 * dec_width), BF16),
            VMEM((1, kv_rows), F32),
            VMEM((1, half), F32),
            VMEM((1, half), F32),
            VMEM(dec_query_weight.shape, BF16),
            VMEM(dec_out_weight.shape, BF16),
            VMEM(byte_states.shape, BF16),
            VMEM((1, total), jnp.int32),
            VMEM((heads // 2, 2, 2, steps, dim + 16, 2 * new), BF16),
            VMEM((heads // 2, 2, 2, steps, dim + 16, 2 * new), BF16),
            VMEM((2, 2, dim + 16, 2 * new), BF16),
            VMEM((3, dim + 16, 2 * new), BF16),
            VMEM((new, heads * dim), BF16),
            VMEM((peers, new, slice_width), BF16),
            VMEM((peers, new, slice_width), BF16),
            VMEM((hn, new, slice_width), BF16),
            VMEM((2, new, dec_width), BF16),
            VMEM((total, dec_width), BF16),
            VMEM((2, bytes_, dec_width), BF16),
            VMEM((2 * bytes_, dec_width), BF16),
            VMEM((2, 1, bytes_), jnp.int32),
            VMEM((2, 1, bytes_), jnp.int32),
            VMEM((half, bytes_), BF16),
            VMEM((dec_width, bytes_), BF16),
            VMEM((peers, bytes_, out_width), BF16),
            VMEM((peers, bytes_, out_width), BF16),
            pltpu.SemaphoreType.DMA((copies,)),
            pltpu.SemaphoreType.DMA((copies,)),
            pltpu.SemaphoreType.DMA((24,)),
        ],
        compiler_params=pltpu.CompilerParams(
            collective_id=0, has_side_effects=True, vmem_limit_bytes=60 * 2**20
        ),
        name="solve",
    )(
        queries,
        new_keys,
        new_values,
        cache_keys,
        cache_values,
        held,
        patch_hidden,
        flat_weight,
        dec_kv_weight,
        norm_gain.reshape(1, kv_rows),
        key_gain.reshape(1, half),
        query_gain.reshape(1, half),
        dec_query_weight,
        dec_out_weight,
        byte_states,
        byte_patch.reshape(1, bytes_),
        mates,
    )
    return pl.pallas_call(
        hand_over,
        out_shape=tuple(jax.ShapeDtypeStruct(r.shape, r.dtype) for r in results),
        in_specs=[in_place()] * 2,
        out_specs=(in_place(),) * 2,
        scratch_shapes=[VMEM(r.shape, r.dtype) for r in results] + [pltpu.SemaphoreType.DMA((4,))],
        compiler_params=pltpu.CompilerParams(vmem_limit_bytes=60 * 2**20),
        name="hand_over",
    )(*results)


def solution(mesh):
    placed = (
        P("ctx", "head"),
        P("ctx", "head", None),
        P("ctx", "head", None),
        P("ctx", "head", None),
        P("ctx", "head", None),
        P("ctx", "head", None),
        P("ctx"),
        P(),
        P("head", None, None),
        P(),
        P(None, None, "head"),
        P(None, "head"),
        P(),
        P(),
        P("head", None),
        P("ctx", None),
        P("ctx"),
    )
    return jax.shard_map(
        functools.partial(per_device, mesh.shape["ctx"] // 4, mesh.shape["head"]),
        mesh=mesh,
        in_specs=placed,
        out_specs=(P("ctx", "head"), P("ctx", "head")),
        check_vma=False,
    )
```
